32 devices in a mesh: groups: 2 (over x), img: 16 (over z, y, core).
Axes of the slice: x: 2, y: 2, z: 4, core: 2. Of those that a mesh axis runs over, the one named last changes fastest.
Arguments:
- descriptors: bfloat16 [32, 256, 1024], P(('groups', 'img')), parts along dimension 0, may hold values from -6 to 6
- attributes: bfloat16 [32, 3, 1024], P(('groups', 'img')), parts along dimension 0, may hold values from -1 to 4, as said below
- counts: int32 [32], P('groups'), parts along dimension 0, may hold values from 256 to 1024
- owner_slot: int32 [32], P('groups'), parts along dimension 0, may hold values from 0 to 15, as said below
- pair_list: int32 [32, 2], P(('groups', 'img')), parts along dimension 0, may hold values from 0 to 15, as said below
Outputs:
- match_xy: float32 [32, 2, 1024], P(('groups', 'img')), parts along dimension 0
- col_lse: float32 [32, 1024], P(('groups', 'img')), parts along dimension 0
- col_xy: float32 [32, 2, 1024], P(('groups', 'img')), parts along dimension 0
The draws below stay inside these ranges and needn't reach their ends.
There are 2 independent parts, one for each index of `groups`. The reference program is written for one: setup_inputs(seed, part) draws one part's arguments, and reference() takes and returns one part's arrays. A program takes and returns all parts, laid end to end along the dimension named above; each array names one. Nothing has to cross between parts.
Inputs may be any that keep to these rules, and one draw needn't show every extreme that they name: owner_slot is a permutation: every slot holds exactly one image id; slot s lies on the device of index s. The query image of row p is stored on the device that holds row p: owner_slot[pair_list[p,0]] == p; the partner differs from the query. `attributes`: scales lie in 0.5 to 4, coordinates in -1 to 1.
All inputs are finite; a program needn't handle non-finite values.
Results may differ from the reference program's by a relative error of at most 0.0003.
Values may be sent and summed in bfloat16 or wider, within the bound.
A program may use at most 64 MiB of HBM per device.

```python
import math
import jax
import jax.numpy as jnp
from jax import lax

D = 256
KP = 1024
IMG_DEV = 1
PAIR_DEV = 1
IMAGES = 16
PAIRS = 16


def slot_table(key):
    return jax.random.permutation(jax.random.fold_in(key, 11), IMAGES).astype(jnp.int32)


def draw_owner_slot(key, part):
    return slot_table(key)


def draw_pair_list(key, part):
    slot_of = slot_table(key)
    stored = jnp.argsort(slot_of).astype(jnp.int32)
    row_ids = jnp.arange(PAIRS, dtype=jnp.int32)
    slot_ids = row_ids // PAIR_DEV * IMG_DEV + row_ids % IMG_DEV
    first_ids = stored[slot_ids]
    hot_ids = jax.random.randint(jax.random.fold_in(key, 12), (4,), 0, IMAGES)
    hot_pick = jax.random.randint(jax.random.fold_in(key, 13), (PAIRS,), 0, 4)
    spread_ids = jax.random.randint(jax.random.fold_in(key, 14), (PAIRS,), 0, IMAGES)
    coin_flip = jax.random.randint(jax.random.fold_in(key, 15), (PAIRS,), 0, 2)
    second_ids = jnp.where(coin_flip == 1, hot_ids[hot_pick], spread_ids)
    second_ids = jnp.where(second_ids == first_ids, (first_ids + 1) % IMAGES, second_ids)
    return jnp.stack([first_ids, second_ids], axis=1).astype(jnp.int32)


def draw_descriptors(key, part):
    normal_part = jax.random.normal(jax.random.fold_in(key, 21), (IMAGES, D, KP), jnp.float32)
    shared = jax.random.normal(jax.random.fold_in(key, 22), (1, D, 1), jnp.float32)
    strength = jax.random.uniform(jax.random.fold_in(key, 23), (IMAGES, 1, 4), jnp.float32, 1.5, 2.2)
    aligned = strength * shared + 0.1 * normal_part[:, :, :4]
    normal_part = jnp.concatenate([aligned, normal_part[:, :, 4:]], axis=2)
    return jnp.clip(normal_part, -6.0, 6.0).astype(jnp.bfloat16)


def draw_attributes(key, part):
    kp_scale = jnp.exp(jax.random.uniform(jax.random.fold_in(key, 31), (IMAGES, 1, KP), jnp.float32, math.log(0.5), math.log(2.0)))
    lifted = jax.random.uniform(jax.random.fold_in(key, 32), (IMAGES, 1, 4), jnp.float32, 3.5, 4.0)
    kp_scale = jnp.concatenate([lifted, kp_scale[:, :, 4:]], axis=2)
    placed = jax.random.uniform(jax.random.fold_in(key, 33), (IMAGES, 2, KP), jnp.float32, -1.0, 1.0)
    return jnp.concatenate([kp_scale, placed], axis=1).astype(jnp.bfloat16)


def place_ends(drawn, rng, smallest, largest):
    longest = drawn.shape.index(max(drawn.shape))
    spots = []
    for shift in (0, 1):
        where = [jax.random.randint(jax.random.fold_in(rng, axis), (), 0, length) for axis, length in enumerate(drawn.shape)]
        where[longest] = (where[longest] + shift) % drawn.shape[longest]
        spots.append(tuple(where))
    return drawn.at[spots[0]].set(smallest).at[spots[1]].set(largest)


def setup_inputs(seed: int = 0, part: int = 0) -> dict:
    key_list = jax.random.split(jax.random.key(seed), 6)
    part_keys = jax.random.split(jax.random.fold_in(key_list[5], part), 6)
    return {
        "descriptors": draw_descriptors(jax.random.fold_in(jax.random.fold_in(key_list[5], part), 71), part),
        "attributes": draw_attributes(jax.random.fold_in(jax.random.fold_in(key_list[5], part), 71), part),
        "counts": place_ends(jax.random.randint(part_keys[2], (IMAGES,), KP // 4, KP + 1), jax.random.fold_in(part_keys[2], 1), KP // 4, KP).astype(jnp.int32),
        "owner_slot": draw_owner_slot(jax.random.fold_in(jax.random.fold_in(key_list[5], part), 71), part),
        "pair_list": draw_pair_list(jax.random.fold_in(jax.random.fold_in(key_list[5], part), 71), part),
    }


far_low = -1e+30

def pair_terms(own_desc, own_attr, own_count, other_desc, other_attr, other_count):
    inv_root = 1.0 / math.sqrt(D)
    raw_scores = lax.dot_general(own_desc, other_desc, (((0,), (0,)), ((), ())), preferred_element_type=jnp.float32)
    own_scale = own_attr[0].astype(jnp.float32) * inv_root
    other_scale = other_attr[0].astype(jnp.float32)
    scores = raw_scores * own_scale[:, None] * other_scale[None, :]
    column_ix = jnp.arange(KP, dtype=jnp.int32)
    row_valid = column_ix < own_count
    col_valid = column_ix < other_count
    row_max = lax.optimization_barrier(jnp.max(jnp.where(col_valid[None, :], scores, far_low), axis=1))
    row_weights = jnp.where(col_valid[None, :], jnp.exp(scores - row_max[:, None]), 0.0)
    row_probs = row_weights / lax.optimization_barrier(jnp.sum(row_weights, axis=1))[:, None]
    matched = jnp.dot(other_attr[1:].astype(jnp.float32), row_probs.T, precision=lax.Precision.HIGHEST)
    matched = jnp.where(row_valid[None, :], matched, 0.0)
    col_top = lax.optimization_barrier(jnp.max(jnp.where(row_valid[:, None], scores, far_low), axis=0))
    col_weights = jnp.where(row_valid[:, None], jnp.exp(scores - col_top[None, :]), 0.0)
    col_total = lax.optimization_barrier(jnp.sum(col_weights, axis=0))
    col_spot = jnp.dot(own_attr[1:].astype(jnp.float32), col_weights, precision=lax.Precision.HIGHEST)
    return (matched, col_top, col_total, col_spot)

def reference(descriptors, attributes, counts, owner_slot, pair_list):
    first_slot = owner_slot[pair_list[:, 0]].astype(jnp.int32)
    second_slot = owner_slot[pair_list[:, 1]].astype(jnp.int32)

    def one_pair(which):
        qa = first_slot[which]
        qb = second_slot[which]
        return pair_terms(descriptors[qa], attributes[qa], counts[pair_list[which, 0]], descriptors[qb], attributes[qb], counts[pair_list[which, 1]])
    matched, col_top, col_total, col_spot = lax.map(one_pair, jnp.arange(PAIRS, dtype=jnp.int32))

    def merge_slot(slot_id):
        hit_mask = second_slot == slot_id
        col_peak = lax.optimization_barrier(jnp.max(jnp.where(hit_mask[:, None], col_top, far_low), axis=0))
        col_peak = jnp.maximum(col_peak, 0.0)
        fade_factor = jnp.where(hit_mask[:, None], jnp.exp(col_top - col_peak[None, :]), 0.0)
        partition = jnp.exp(-col_peak) + lax.optimization_barrier(jnp.sum(fade_factor * col_total, axis=0))
        soft_xy = lax.optimization_barrier(jnp.sum(fade_factor[:, None, :] * col_spot, axis=0)) / partition[None, :]
        return (col_peak + jnp.log(partition), soft_xy)
    log_total, soft_xy = lax.map(merge_slot, jnp.arange(IMAGES, dtype=jnp.int32))
    return (matched, log_total, soft_xy)
```

```python
import functools
import math

import jax
import jax.numpy as jnp
from jax import lax
from jax.experimental import pallas as pl
from jax.experimental.pallas import tpu as pltpu
from jax.sharding import PartitionSpec as P

MESH = pl.DeviceIdType.MESH
LANES = 128
ROWS = 256
ROUNDS = 4
MIN_WIDTH = 16
TILE = 16
far_low = -1e30


def split_dot(left, right, contract):
    high = right.astype(jnp.bfloat16)
    low = (right - high.astype(jnp.float32)).astype(jnp.bfloat16)
    dims = (contract, ((), ()))
    return lax.dot_general(left, high, dims, preferred_element_type=jnp.float32) + lax.dot_general(
        left, low, dims, preferred_element_type=jnp.float32
    )


def with_ones(attr):
    ones = jnp.ones((1, attr.shape[1]), jnp.float32)
    rest = jnp.zeros((4, attr.shape[1]), jnp.float32)
    return jnp.concatenate([attr[0:1], ones, attr[1:3], rest], axis=0)


def kernel(
    n, rounds, desc, attr, counts, owner, pairs, match_o, lse_o, xy_o,
    own, own_t, own_attr, row_scale, own_rows, other_rows, other_scale, want_out, want_all, want_s,
    counts_s, owner_s, pairs_s, attr_in, attr_stage, attr_other,
    stage, partner, scores, row_top, stats_out, stats_in, merged_out, merged_in, direct_in,
    local_sem, want_ss, want_rs, attr_ss1, attr_rs1, attr_ss2, attr_rs2, ss1, rs1, ss2, rs2, ss3, rs3, ss4, rs4, ss5, rs5,
    *pieces,
):
    depth, keypoints = desc.shape[1:]
    chunks = keypoints // LANES
    parts = n // chunks
    blocks = keypoints // ROWS
    me = lax.axis_index("img")
    my_chunk = me // parts
    my_part = lax.rem(me, parts)
    round_chunks = chunks // rounds
    round_parts = n // round_chunks
    width = depth // round_parts
    early = chunks - round_chunks

    def peer(step):
        return lax.rem(me + step, n)

    def remote(src, dst, send, recv, to):
        return pltpu.make_async_remote_copy(
            src_ref=src, dst_ref=dst, send_sem=send, recv_sem=recv, device_id={"img": to}, device_id_type=MESH
        )

    def piece_of(r, k):
        row = pl.multiple_of(lax.rem(k, round_parts) * width, width)
        col = pl.multiple_of((r * round_chunks + k // round_parts) * LANES, LANES)
        return desc.at[0, pl.ds(row, width), pl.ds(col, LANES)]

    def attr_piece(c):
        return attr.at[0, :, pl.ds(pl.multiple_of(c * LANES, LANES), LANES)]

    def copy_want(k, source):
        return remote(want_out, want_all.at[source], want_ss.at[k], want_rs.at[source], k)

    def copy_attr_one(c, source):
        return remote(attr_piece(c), attr_in.at[source], attr_ss1.at[c], attr_rs1.at[source], c * parts)

    def copy_attr_two(k, source):
        return remote(attr_stage.at[k], attr_other.at[source], attr_ss2.at[k], attr_rs2.at[source], k)

    def copy_one(r, k, source):
        return remote(piece_of(r, k), pieces[r].at[source], ss1.at[r, k], rs1.at[r, source], k)

    def copy_two(r, k, source):
        return remote(stage.at[r, k], partner.at[r, source], ss2.at[r, k], rs2.at[r, source], k)

    def copy_stats(k, source):
        return remote(stats_out.at[k // parts], stats_in.at[source], ss3.at[k], rs3.at[source], k)

    def copy_merged(q, k, source_chunk):
        return remote(merged_out.at[q], merged_in.at[source_chunk], ss4.at[q], rs4.at[source_chunk], k)

    def copy_direct(i, k, source):
        return remote(stats_out.at[early + i], direct_in.at[i, source], ss5.at[i, k], rs5.at[i, source], k)

    barrier = pltpu.get_barrier_semaphore()

    @pl.loop(1, n)
    def _(step):
        pl.semaphore_signal(barrier, inc=1, device_id={"img": peer(step)}, device_id_type=MESH)

    local_copies = [
        pltpu.make_async_copy(pairs, pairs_s, local_sem.at[0]),
        pltpu.make_async_copy(owner, owner_s, local_sem.at[1]),
        pltpu.make_async_copy(counts, counts_s, local_sem.at[2]),
        pltpu.make_async_copy(attr, own_attr, local_sem.at[3]),
        pltpu.make_async_copy(desc.at[0], own, local_sem.at[4]),
        *[pltpu.make_async_copy(piece_of(r, me), pieces[r].at[me], local_sem.at[7 + r]) for r in range(rounds)],
    ]
    for copy in local_copies:
        copy.start()
    local_attr = pltpu.make_async_copy(attr_piece(my_chunk), attr_in.at[me], local_sem.at[6])

    @pl.when(my_part == 0)
    def _():
        local_attr.start()

    for copy in local_copies[:3]:
        copy.wait()
    want = owner_s[pairs_s[0, 1]]
    count_a = counts_s[pairs_s[0, 0]]
    count_b = counts_s[pairs_s[0, 1]]
    want_row = jnp.full((1, LANES), want, jnp.int32)
    want_out[...] = want_row
    want_all[me] = want_row
    pl.semaphore_wait(barrier, n - 1)

    @pl.loop(1, n)
    def _(step):
        copy_want(peer(step), me).start()

    @pl.loop(0, chunks)
    def _(step):
        c = lax.rem(my_chunk + step, chunks)

        @pl.when(c * parts != me)
        def _():
            copy_attr_one(c, me).start()

    for r in range(rounds):
        @pl.loop(1, n)
        def _(step):
            copy_one(r, peer(step), me).start()

    for copy in local_copies[3:]:
        copy.wait()
    rows8 = with_ones(own_attr[0].astype(jnp.float32))
    own_rows[...] = rows8.astype(jnp.bfloat16)
    row_scale[...] = jnp.broadcast_to(jnp.transpose(rows8)[:, 0:1] * (1.0 / math.sqrt(depth)), (keypoints, LANES))
    for block in range(blocks):
        rows = slice(block * ROWS, (block + 1) * ROWS)
        own_t[rows, :] = jnp.transpose(own[:, rows])
    row_top[...] = jnp.full((keypoints, LANES), far_low, jnp.float32)

    @pl.loop(1, n)
    def _(step):
        k = peer(step)
        copy_want(k, k).wait_recv()

    to_scalars = pltpu.make_async_copy(want_all, want_s, local_sem.at[5])
    to_scalars.start()
    to_scalars.wait()

    @pl.when(my_part == 0)
    def _():
        local_attr.wait()

        @pl.loop(1, n)
        def _(step):
            k = peer(step)
            copy_attr_one(my_chunk, k).wait_recv()

        @pl.loop(1, n)
        def _(step):
            k = peer(step)
            attr_stage[k] = attr_in[want_s[k, 0, 0]]
            copy_attr_two(k, my_chunk).start()

        attr_other[my_chunk] = attr_in[want]

    for r in range(rounds):
        @pl.loop(1, n)
        def _(step):
            k = peer(step)
            copy_one(r, k, k).wait_recv()

        @pl.loop(1, n)
        def _(step):
            k = peer(step)
            stage[r, k] = pieces[r][want_s[k, 0, 0]]
            copy_two(r, k, me).start()

        partner[r, me] = pieces[r][want]

    for chunk in range(chunks):
        cols = slice(chunk * LANES, (chunk + 1) * LANES)

        @pl.when(chunk * parts != me)
        def _():
            copy_attr_two(chunk * parts, chunk).wait_recv()

        other8 = with_ones(attr_other[chunk].astype(jnp.float32))
        other_rows[:, cols] = other8.astype(jnp.bfloat16)
        other_scale[chunk] = other8[0:1]

    row_ix = lax.broadcasted_iota(jnp.int32, (ROWS, LANES), 0)
    lane_ix = lax.broadcasted_iota(jnp.int32, (1, LANES), 1)
    first_row = lax.broadcasted_iota(jnp.int32, (4, LANES), 0) == 0

    def score_chunk(step):
        r = step // round_chunks
        within = lax.rem(me // round_parts + step, round_chunks)
        c = r * round_chunks + within
        for part in range(round_parts):
            k = within * round_parts + part

            @pl.when(k != me)
            def _():
                copy_two(r, k, k).wait_recv()

        block_b = partner[r, pl.ds(within * round_parts, round_parts)].reshape(depth, LANES)
        scale_b = other_scale[c]
        col_valid = c * LANES + lane_ix < count_b
        col_top = jnp.full((1, LANES), far_low, jnp.float32)
        for block in range(blocks):
            rows = slice(block * ROWS, (block + 1) * ROWS)
            raw = jnp.dot(own_t[rows, :], block_b, preferred_element_type=jnp.float32)
            score = raw * row_scale[rows, :] * scale_b
            scores[c, rows, :] = score
            row_top[rows, :] = jnp.maximum(row_top[rows, :], jnp.where(col_valid, score, far_low))
            masked = jnp.where(block * ROWS + row_ix < count_a, score, far_low)
            col_top = jnp.maximum(col_top, jnp.max(masked, axis=0, keepdims=True))
        sums = jnp.zeros((8, LANES), jnp.float32)
        for block in range(blocks):
            rows = slice(block * ROWS, (block + 1) * ROWS)
            weight = jnp.where(block * ROWS + row_ix < count_a, jnp.exp(scores[c, rows, :] - col_top), 0.0)
            sums = sums + split_dot(own_rows[:, rows], weight, ((1,), (0,)))
        stats = jnp.where(first_row, col_top, sums[0:4])
        stats_out[c] = stats
        return c, within, stats

    def merge(slot, partial):
        hit = want_all[...] == slot
        tops = partial[:, 0:1, :]
        peak = jnp.maximum(jnp.max(jnp.where(hit, tops, far_low), axis=0), 0.0)
        fade = jnp.where(hit, jnp.exp(tops - peak[None]), 0.0)
        total = jnp.sum(fade * partial, axis=0)
        partition = jnp.exp(-peak) + total[1:2]
        return jnp.where(first_row, peak + jnp.log(partition), total / partition)

    @pl.loop(0, early)
    def _(step):
        c, _, stats = score_chunk(step)
        for part in range(parts):
            k = c * parts + part

            @pl.when(k != me)
            def _():
                copy_stats(k, me).start()

            @pl.when(k == me)
            def _():
                stats_in[me] = stats

    @pl.loop(early, chunks)
    def _(step):
        _, i, stats = score_chunk(step)
        direct_in[i, me] = stats

        @pl.loop(1, n)
        def _(hop):
            copy_direct(i, peer(hop), me).start()

    @pl.when(my_chunk < early)
    def _():
        @pl.loop(1, n)
        def _(step):
            k = peer(step)
            copy_stats(k, k).wait_recv()

        @pl.loop(0, chunks)
        def _(q):
            slot = my_part * chunks + q
            merged = merge(slot, stats_in[...])
            merged_out[q] = merged

            @pl.when(slot != me)
            def _():
                copy_merged(q, slot, my_chunk).start()

            @pl.when(slot == me)
            def _():
                merged_in[my_chunk] = merged

    for block in range(blocks):
        rows = slice(block * ROWS, (block + 1) * ROWS)
        top = jnp.max(row_top[rows, :], axis=1, keepdims=True)
        sums = jnp.zeros((8, ROWS), jnp.float32)
        for chunk in range(chunks):
            cols = slice(chunk * LANES, (chunk + 1) * LANES)
            weight = jnp.where(chunk * LANES + lane_ix < count_b, jnp.exp(scores[chunk, rows, :] - top), 0.0)
            sums = sums + split_dot(other_rows[:, cols], weight, ((1,), (1,)))
        row_valid = block * ROWS + lax.broadcasted_iota(jnp.int32, (2, ROWS), 1) < count_a
        match_o[0, :, rows] = jnp.where(row_valid, sums[2:4] / sums[1:2], 0.0)

    def write(chunk, result):
        cols = slice(chunk * LANES, (chunk + 1) * LANES)
        lse_o[:, cols] = result[0:1]
        xy_o[0, :, cols] = result[2:4]

    for i in range(round_chunks):
        @pl.loop(1, n)
        def _(step):
            k = peer(step)
            copy_direct(i, k, k).wait_recv()

        write(early + i, merge(me, direct_in[i]))

    home_part = me // chunks
    for chunk in range(early):
        k = chunk * parts + home_part

        @pl.when(k != me)
        def _():
            copy_merged(chunk, k, chunk).wait_recv()

        write(chunk, merged_in[chunk])

    @pl.loop(1, n)
    def _(step):
        k = peer(step)
        copy_want(k, me).wait_send()
        for r in range(rounds):
            copy_one(r, k, me).wait_send()
            copy_two(r, k, me).wait_send()
        for i in range(round_chunks):
            copy_direct(i, k, me).wait_send()

        @pl.when(k // parts < early)
        def _():
            copy_stats(k, me).wait_send()

    @pl.when(my_chunk < early)
    def _():
        @pl.loop(0, chunks)
        def _(q):
            slot = my_part * chunks + q

            @pl.when(slot != me)
            def _():
                copy_merged(q, slot, my_chunk).wait_send()

    @pl.loop(0, chunks)
    def _(c):
        @pl.when(c * parts != me)
        def _():
            copy_attr_one(c, me).wait_send()

    @pl.when(my_part == 0)
    def _():
        @pl.loop(1, n)
        def _(step):
            copy_attr_two(peer(step), my_chunk).wait_send()


def put_out(match, lse, xy, match_o, lse_o, xy_o, sem):
    copies = [
        pltpu.make_async_copy(match, match_o, sem.at[0]),
        pltpu.make_async_copy(lse, lse_o, sem.at[1]),
        pltpu.make_async_copy(xy, xy_o, sem.at[2]),
    ]
    for copy in copies:
        copy.start()
    for copy in copies:
        copy.wait()


def plan(keypoints):
    half, quarter, eighth = keypoints // 2, keypoints // 4, keypoints // 8
    spans = ((0, half + quarter), (half + quarter, quarter))
    subs = ((0, 0, half), (0, half, quarter), (1, 0, eighth), (1, eighth, eighth))
    return spans, subs


def tile_kernel(
    n, desc, attr, counts, owner, pairs, match_o, lse_o, xy_o,
    own, own_t, own_attr, row_scale, own_rows, other_rows, other_scale, want_out, want_all, want_s,
    counts_s, owner_s, pairs_s, attr_all, attr_stage, attr_other,
    scores, row_top, stats_out, stats_in, merged_out, merged_in, direct_in,
    local_sem, want_ss, want_rs, attr_ss1, attr_rs1, attr_ss2, attr_rs2,
    ss1, rs1, ss2, rs2, ss3, rs3, ss4, rs4, ss5, rs5, *buffers,
):
    depth, keypoints = desc.shape[1:]
    spans, subs = plan(keypoints)
    pieces = buffers[: len(spans)]
    stage = buffers[len(spans) : len(spans) + len(subs)]
    partner = buffers[len(spans) + len(subs) :]
    width = depth // n
    chunks = keypoints // LANES
    parts = n // chunks
    blocks = keypoints // ROWS
    direct = sum(w for r, _, w in subs if r == 1) // LANES
    early = chunks - direct
    team = 4
    me = lax.axis_index("img")
    my_chunk = me // parts
    my_part = lax.rem(me, parts)
    lead = me - lax.rem(me, team)

    def peer(j):
        return lax.rem(me + n // 2 + (j // 2) * (2 * lax.rem(j, 2) - 1), n)

    def remote(src, dst, send, recv, to):
        return pltpu.make_async_remote_copy(
            src_ref=src, dst_ref=dst, send_sem=send, recv_sem=recv, device_id={"img": to}, device_id_type=MESH
        )

    def drain(like, sem):
        pltpu.make_async_copy(like, like, sem).wait()

    def others(buffer):
        return buffer.at[pl.ds(0, n - 1)]

    def piece_of(r, k):
        first, w = spans[r]
        return desc.at[0, pl.ds(pl.multiple_of(k * width, width), width), pl.ds(first, w)]

    def copy_want(k):
        return remote(want_out, want_all.at[me], want_ss, want_rs, k)

    def copy_attr_one(k):
        return remote(attr.at[0], attr_all.at[me], attr_ss1, attr_rs1, k)

    def copy_attr_two(j, k):
        return remote(attr_stage.at[j], attr_other, attr_ss2.at[j], attr_rs2, k)

    def copy_one(r, k):
        return remote(piece_of(r, k), pieces[r].at[me], ss1.at[r], rs1.at[r], k)

    def copy_two(u, k):
        return remote(stage[u].at[k], partner[u].at[me], ss2.at[u], rs2.at[u], k)

    def copy_stats(c, k):
        return remote(stats_out.at[c], stats_in.at[me], ss3.at[k], rs3, k)

    def copy_merged(q, k, source_chunk):
        return remote(merged_out.at[q], merged_in.at[source_chunk], ss4.at[q], rs4.at[source_chunk], k)

    def copy_direct(i, k):
        return remote(stats_out.at[early + i], direct_in.at[i, me], ss5.at[i], rs5.at[i], k)

    barrier = pltpu.get_barrier_semaphore()

    @pl.loop(1, n)
    def _(step):
        pl.semaphore_signal(barrier, inc=1, device_id={"img": peer(step)}, device_id_type=MESH)

    local_copies = [
        pltpu.make_async_copy(pairs, pairs_s, local_sem.at[0]),
        pltpu.make_async_copy(owner, owner_s, local_sem.at[1]),
        pltpu.make_async_copy(counts, counts_s, local_sem.at[2]),
        pltpu.make_async_copy(attr, own_attr, local_sem.at[3]),
        pltpu.make_async_copy(desc.at[0], own, local_sem.at[4]),
        pltpu.make_async_copy(attr.at[0], attr_all.at[me], local_sem.at[6]),
        *[pltpu.make_async_copy(piece_of(r, me), pieces[r].at[me], local_sem.at[7 + r]) for r in range(len(spans))],
    ]
    for copy in local_copies:
        copy.start()
    for copy in local_copies[:3]:
        copy.wait()
    want = owner_s[pairs_s[0, 1]]
    count_a = counts_s[pairs_s[0, 0]]
    count_b = counts_s[pairs_s[0, 1]]
    want_row = jnp.full((1, LANES), want, jnp.int32)
    want_out[...] = want_row
    want_all[me] = want_row
    pl.semaphore_wait(barrier, n - 1)

    @pl.loop(1, n)
    def _(step):
        copy_want(peer(step)).start()

    @pl.loop(1, n)
    def _(step):
        copy_one(0, peer(step)).start()

    @pl.loop(0, n // team)
    def _(t):
        @pl.when(t * team != me)
        def _():
            copy_attr_one(t * team).start()

    @pl.loop(1, n)
    def _(step):
        copy_one(1, peer(step)).start()

    for copy in local_copies[3:]:
        copy.wait()
    rows8 = with_ones(own_attr[0].astype(jnp.float32))
    own_rows[...] = rows8.astype(jnp.bfloat16)
    row_scale[...] = jnp.broadcast_to(jnp.transpose(rows8)[:, 0:1] * (1.0 / math.sqrt(depth)), (keypoints, LANES))
    for block in range(blocks):
        rows = slice(block * ROWS, (block + 1) * ROWS)
        own_t[rows, :] = jnp.transpose(own[:, rows])
    row_top[...] = jnp.full((keypoints, LANES), far_low, jnp.float32)

    drain(others(want_all), want_rs)
    to_scalars = pltpu.make_async_copy(want_all, want_s, local_sem.at[5])
    to_scalars.start()
    to_scalars.wait()

    def forward(u):
        r, first, w = subs[u]

        @pl.loop(1, n)
        def _(step):
            k = peer(step)
            stage[u][k] = pieces[r][want_s[k, 0, 0], :, first : first + w]
            copy_two(u, k).start()

        partner[u][me] = pieces[r][want, :, first : first + w]

    def forward_round(r):
        drain(others(pieces[r]), rs1.at[r])
        for u in range(len(subs)):
            if subs[u][0] == r:
                forward(u)

    forward_round(0)

    @pl.when(me == lead)
    def _():
        drain(others(attr_all), attr_rs1)
        for j in range(1, team):
            attr_stage[j] = attr_all[want_s[me + j, 0, 0]]
            copy_attr_two(j, me + j).start()
        attr_other[...] = attr_all[want]

    forward_round(1)

    @pl.when(me != lead)
    def _():
        drain(attr_other, attr_rs2)

    other8 = with_ones(attr_other[...].astype(jnp.float32))
    other_rows[...] = other8.astype(jnp.bfloat16)
    for chunk in range(chunks):
        other_scale[chunk] = other8[0:1, chunk * LANES : (chunk + 1) * LANES]

    row_ix = lax.broadcasted_iota(jnp.int32, (ROWS, LANES), 0)
    lane_ix = lax.broadcasted_iota(jnp.int32, (1, LANES), 1)
    first_row = lax.broadcasted_iota(jnp.int32, (4, LANES), 0) == 0

    def score_chunk(u, i, c):
        cols = pl.ds(pl.multiple_of(i * LANES, LANES), LANES)
        block_b = partner[u][:, :, cols].reshape(depth, LANES)
        scale_b = other_scale[c]
        col_valid = c * LANES + lane_ix < count_b
        col_top = jnp.full((1, LANES), far_low, jnp.float32)
        for block in range(blocks):
            rows = slice(block * ROWS, (block + 1) * ROWS)
            raw = jnp.dot(own_t[rows, :], block_b, preferred_element_type=jnp.float32)
            score = raw * row_scale[rows, :] * scale_b
            scores[c, rows, :] = score
            row_top[rows, :] = jnp.maximum(row_top[rows, :], jnp.where(col_valid, score, far_low))
            masked = jnp.where(block * ROWS + row_ix < count_a, score, far_low)
            col_top = jnp.maximum(col_top, jnp.max(masked, axis=0, keepdims=True))
        sums = jnp.zeros((8, LANES), jnp.float32)
        for block in range(blocks):
            rows = slice(block * ROWS, (block + 1) * ROWS)
            weight = jnp.where(block * ROWS + row_ix < count_a, jnp.exp(scores[c, rows, :] - col_top), 0.0)
            sums = sums + split_dot(own_rows[:, rows], weight, ((1,), (0,)))
        stats = jnp.where(first_row, col_top, sums[0:4])
        stats_out[c] = stats
        return stats

    def merge(slot, partial):
        hit = want_all[...] == slot
        tops = partial[:, 0:1, :]
        peak = jnp.maximum(jnp.max(jnp.where(hit, tops, far_low), axis=0), 0.0)
        fade = jnp.where(hit, jnp.exp(tops - peak[None]), 0.0)
        total = jnp.sum(fade * partial, axis=0)
        partition = jnp.exp(-peak) + total[1:2]
        return jnp.where(first_row, peak + jnp.log(partition), total / partition)

    for u in range(len(subs)):
        r, first, w = subs[u]
        base = (spans[r][0] + first) // LANES
        drain(others(partner[u]), rs2.at[u])
        if r == 0:
            @pl.loop(0, w // LANES)
            def _(i):
                c = base + i
                stats = score_chunk(u, i, c)
                for part in range(parts):
                    k = c * parts + part

                    @pl.when(k != me)
                    def _():
                        copy_stats(c, k).start()

                    @pl.when(k == me)
                    def _():
                        stats_in[me] = stats
        else:
            for i in range(w // LANES):
                d = base + i - early
                direct_in[d, me] = score_chunk(u, i, base + i)

                @pl.loop(1, n)
                def _(step):
                    copy_direct(d, peer(step)).start()

    @pl.when(my_chunk < early)
    def _():
        drain(others(stats_in), rs3)

        @pl.loop(0, chunks)
        def _(q):
            slot = my_part * chunks + q
            merged = merge(slot, stats_in[...])
            merged_out[q] = merged

            @pl.when(slot != me)
            def _():
                copy_merged(q, slot, my_chunk).start()

            @pl.when(slot == me)
            def _():
                merged_in[my_chunk] = merged

    for block in range(blocks):
        rows = slice(block * ROWS, (block + 1) * ROWS)
        top = jnp.max(row_top[rows, :], axis=1, keepdims=True)
        sums = jnp.zeros((8, ROWS), jnp.float32)
        for chunk in range(chunks):
            cols = slice(chunk * LANES, (chunk + 1) * LANES)
            weight = jnp.where(chunk * LANES + lane_ix < count_b, jnp.exp(scores[chunk, rows, :] - top), 0.0)
            sums = sums + split_dot(other_rows[:, cols], weight, ((1,), (1,)))
        row_valid = block * ROWS + lax.broadcasted_iota(jnp.int32, (2, ROWS), 1) < count_a
        match_o[0, :, rows] = jnp.where(row_valid, sums[2:4] / sums[1:2], 0.0)

    def write(chunk, result):
        cols = slice(chunk * LANES, (chunk + 1) * LANES)
        lse_o[:, cols] = result[0:1]
        xy_o[0, :, cols] = result[2:4]

    drain(others(want_all), want_ss)
    for r in range(len(spans)):
        drain(others(pieces[r]), ss1.at[r])
    for u in range(len(subs)):
        drain(others(partner[u]), ss2.at[u])

    @pl.loop(0, n // team)
    def _(t):
        @pl.when(t * team != me)
        def _():
            drain(attr_other, attr_ss1)

    @pl.when(me == lead)
    def _():
        for j in range(1, team):
            copy_attr_two(j, me + j).wait_send()

    @pl.loop(0, early * parts)
    def _(k):
        @pl.when(k != me)
        def _():
            copy_stats(k // parts, k).wait_send()

    for i in range(direct):
        drain(others(direct_in.at[i]), rs5.at[i])
        write(early + i, merge(me, direct_in[i]))

    home_part = me // chunks
    for chunk in range(early):
        k = chunk * parts + home_part

        @pl.when(k != me)
        def _():
            copy_merged(0, k, chunk).wait_recv()

        write(chunk, merged_in[chunk])

    for i in range(direct):
        drain(others(direct_in.at[i]), ss5.at[i])

    @pl.when(my_chunk < early)
    def _():
        @pl.loop(0, chunks)
        def _(q):
            slot = my_part * chunks + q

            @pl.when(slot != me)
            def _():
                copy_merged(q, slot, my_chunk).wait_send()


def one_tile(n, descriptors, attributes, counts, owner_slot, pair_list):
    _, depth, keypoints = descriptors.shape
    chunks = keypoints // LANES
    spans, subs = plan(keypoints)
    width = depth // n
    direct = sum(w for r, _, w in subs if r == 1) // LANES
    vmem = pl.BlockSpec(memory_space=pltpu.VMEM)
    hbm = pl.BlockSpec(memory_space=pltpu.HBM)
    f32, bf16, i32 = jnp.float32, jnp.bfloat16, jnp.int32
    sems = pltpu.SemaphoreType.DMA
    out_shape = (
        jax.ShapeDtypeStruct((1, 2, keypoints), f32),
        jax.ShapeDtypeStruct((1, keypoints), f32),
        jax.ShapeDtypeStruct((1, 2, keypoints), f32),
    )
    results = pl.pallas_call(
        functools.partial(tile_kernel, n),
        out_shape=out_shape,
        in_specs=[hbm] * 5,
        out_specs=(vmem, vmem, vmem),
        scratch_shapes=[
            pltpu.VMEM((depth, keypoints), bf16),
            pltpu.VMEM((keypoints, depth), bf16),
            pltpu.VMEM((1, 3, keypoints), bf16),
            pltpu.VMEM((keypoints, LANES), f32),
            pltpu.VMEM((8, keypoints), bf16),
            pltpu.VMEM((8, keypoints), bf16),
            pltpu.VMEM((chunks, 1, LANES), f32),
            pltpu.VMEM((1, LANES), i32),
            pltpu.VMEM((n, 1, LANES), i32),
            pltpu.SMEM((n, 1, LANES), i32),
            pltpu.SMEM(counts.shape, i32),
            pltpu.SMEM(owner_slot.shape, i32),
            pltpu.SMEM(pair_list.shape, i32),
            pltpu.VMEM((n, 3, keypoints), bf16),
            pltpu.VMEM((4, 3, keypoints), bf16),
            pltpu.VMEM((3, keypoints), bf16),
            pltpu.VMEM((chunks, keypoints, LANES), f32),
            pltpu.VMEM((keypoints, LANES), f32),
            pltpu.VMEM((chunks, 4, LANES), f32),
            pltpu.VMEM((n, 4, LANES), f32),
            pltpu.VMEM((chunks, 4, LANES), f32),
            pltpu.VMEM((chunks, 4, LANES), f32),
            pltpu.VMEM((direct, n, 4, LANES), f32),
            sems((7 + len(spans),)),
            sems,
            sems,
            sems,
            sems,
            sems((4,)),
            sems,
            *[sems((len(spans),))] * 2,
            *[sems((len(subs),))] * 2,
            sems((n,)),
            sems,
            *[sems((chunks,))] * 2,
            *[sems((direct,))] * 2,
            *[pltpu.VMEM((n, width, w), bf16) for _, w in spans],
            *[pltpu.VMEM((n, width, w), bf16) for _, _, w in subs] * 2,
        ],
        compiler_params=pltpu.CompilerParams(collective_id=0, has_side_effects=True),
    )(descriptors, attributes, counts, owner_slot, pair_list)
    return pl.pallas_call(
        put_out,
        out_shape=out_shape,
        in_specs=[vmem] * 3,
        out_specs=(hbm, hbm, hbm),
        scratch_shapes=[sems((3,))],
    )(*results)


def solution(mesh):
    n = mesh.shape["img"]

    def shards(descriptors, attributes, counts, owner_slot, pair_list):
        _, depth, keypoints = descriptors.shape
        if n * TILE == depth:
            return one_tile(n, descriptors, attributes, counts, owner_slot, pair_list)
        chunks = keypoints // LANES
        parts = n // chunks
        rounds = min(ROUNDS, depth * chunks // (n * MIN_WIDTH))
        width = depth * chunks // (n * rounds)
        vmem = pl.BlockSpec(memory_space=pltpu.VMEM)
        hbm = pl.BlockSpec(memory_space=pltpu.HBM)
        f32, bf16, i32 = jnp.float32, jnp.bfloat16, jnp.int32
        sems = pltpu.SemaphoreType.DMA
        out_shape = (
            jax.ShapeDtypeStruct((1, 2, keypoints), f32),
            jax.ShapeDtypeStruct((1, keypoints), f32),
            jax.ShapeDtypeStruct((1, 2, keypoints), f32),
        )
        results = pl.pallas_call(
            functools.partial(kernel, n, rounds),
            out_shape=out_shape,
            in_specs=[hbm] * 5,
            out_specs=(vmem, vmem, vmem),
            scratch_shapes=[
                pltpu.VMEM((depth, keypoints), bf16),
                pltpu.VMEM((keypoints, depth), bf16),
                pltpu.VMEM((1, 3, keypoints), bf16),
                pltpu.VMEM((keypoints, LANES), f32),
                pltpu.VMEM((8, keypoints), bf16),
                pltpu.VMEM((8, keypoints), bf16),
                pltpu.VMEM((chunks, 1, LANES), f32),
                pltpu.VMEM((1, LANES), i32),
                pltpu.VMEM((n, 1, LANES), i32),
                pltpu.SMEM((n, 1, LANES), i32),
                pltpu.SMEM(counts.shape, i32),
                pltpu.SMEM(owner_slot.shape, i32),
                pltpu.SMEM(pair_list.shape, i32),
                pltpu.VMEM((n, 3, LANES), bf16),
                pltpu.VMEM((n, 3, LANES), bf16),
                pltpu.VMEM((chunks, 3, LANES), bf16),
                *[pltpu.VMEM((rounds, n, width, LANES), bf16)] * 2,
                pltpu.VMEM((chunks, keypoints, LANES), f32),
                pltpu.VMEM((keypoints, LANES), f32),
                pltpu.VMEM((chunks, 4, LANES), f32),
                pltpu.VMEM((n, 4, LANES), f32),
                pltpu.VMEM((chunks, 4, LANES), f32),
                pltpu.VMEM((chunks, 4, LANES), f32),
                pltpu.VMEM((chunks // rounds, n, 4, LANES), f32),
                sems((7 + rounds,)),
                *[sems((n,))] * 2,
                sems((chunks,)),
                *[sems((n,))] * 2,
                sems((chunks,)),
                *[sems((rounds, n))] * 4,
                *[sems((n,))] * 2,
                *[sems((chunks,))] * 2,
                *[sems((chunks // rounds, n))] * 2,
                *[pltpu.VMEM((n, width, LANES), bf16)] * rounds,
            ],
            compiler_params=pltpu.CompilerParams(
                collective_id=0, has_side_effects=True
            ),
        )(descriptors, attributes, counts, owner_slot, pair_list)
        return pl.pallas_call(
            put_out,
            out_shape=out_shape,
            in_specs=[vmem] * 3,
            out_specs=(hbm, hbm, hbm),
            scratch_shapes=[sems((3,))],
        )(*results)

    placed = (
        P(("groups", "img"), None, None),
        P(("groups", "img"), None, None),
        P("groups"),
        P("groups"),
        P(("groups", "img"), None),
    )
    return jax.shard_map(
        shards,
        mesh=mesh,
        in_specs=placed,
        out_specs=(
            P(("groups", "img"), None, None),
            P(("groups", "img"), None),
            P(("groups", "img"), None, None),
        ),
        check_vma=False,
    )
```

```python
import functools
import math

import jax
import jax.numpy as jnp
from jax import lax
from jax.experimental import pallas as pl
from jax.experimental.pallas import tpu as pltpu
from jax.sharding import PartitionSpec as P

MESH = pl.DeviceIdType.MESH
LANES = 128
ROWS = 256
ROUNDS = 4
MIN_WIDTH = 16
TILE = 16
far_low = -1e30


def split_dot(left, right, contract):
    high = right.astype(jnp.bfloat16)
    low = (right - high.astype(jnp.float32)).astype(jnp.bfloat16)
    dims = (contract, ((), ()))
    return lax.dot_general(left, high, dims, preferred_element_type=jnp.float32) + lax.dot_general(
        left, low, dims, preferred_element_type=jnp.float32
    )


def with_ones(attr):
    ones = jnp.ones((1, attr.shape[1]), jnp.float32)
    rest = jnp.zeros((4, attr.shape[1]), jnp.float32)
    return jnp.concatenate([attr[0:1], ones, attr[1:3], rest], axis=0)


def kernel(
    n, rounds, desc, attr, counts, owner, pairs, match_o, lse_o, xy_o,
    own, own_t, own_attr, row_scale, own_rows, other_rows, other_scale, want_out, want_all, want_s,
    counts_s, owner_s, pairs_s, attr_in, attr_stage, attr_other,
    stage, partner, scores, row_top, stats_out, stats_in, merged_out, merged_in, direct_in,
    local_sem, want_ss, want_rs, attr_ss1, attr_rs1, attr_ss2, attr_rs2, ss1, rs1, ss2, rs2, ss3, rs3, ss4, rs4, ss5, rs5,
    *pieces,
):
    depth, keypoints = desc.shape[1:]
    chunks = keypoints // LANES
    parts = n // chunks
    blocks = keypoints // ROWS
    me = lax.axis_index("img")
    my_chunk = me // parts
    my_part = lax.rem(me, parts)
    round_chunks = chunks // rounds
    round_parts = n // round_chunks
    width = depth // round_parts
    early = chunks - round_chunks

    def peer(step):
        return lax.rem(me + step, n)

    def remote(src, dst, send, recv, to):
        return pltpu.make_async_remote_copy(
            src_ref=src, dst_ref=dst, send_sem=send, recv_sem=recv, device_id={"img": to}, device_id_type=MESH
        )

    def piece_of(r, k):
        row = pl.multiple_of(lax.rem(k, round_parts) * width, width)
        col = pl.multiple_of((r * round_chunks + k // round_parts) * LANES, LANES)
        return desc.at[0, pl.ds(row, width), pl.ds(col, LANES)]

    def attr_piece(c):
        return attr.at[0, :, pl.ds(pl.multiple_of(c * LANES, LANES), LANES)]

    def copy_want(k, source):
        return remote(want_out, want_all.at[source], want_ss.at[k], want_rs.at[source], k)

    def copy_attr_one(c, source):
        return remote(attr_piece(c), attr_in.at[source], attr_ss1.at[c], attr_rs1.at[source], c * parts)

    def copy_attr_two(k, source):
        return remote(attr_stage.at[k], attr_other.at[source], attr_ss2.at[k], attr_rs2.at[source], k)

    def copy_one(r, k, source):
        return remote(piece_of(r, k), pieces[r].at[source], ss1.at[r, k], rs1.at[r, source], k)

    def copy_two(r, k, source):
        return remote(stage.at[r, k], partner.at[r, source], ss2.at[r, k], rs2.at[r, source], k)

    def copy_stats(k, source):
        return remote(stats_out.at[k // parts], stats_in.at[source], ss3.at[k], rs3.at[source], k)

    def copy_merged(q, k, source_chunk):
        return remote(merged_out.at[q], merged_in.at[source_chunk], ss4.at[q], rs4.at[source_chunk], k)

    def copy_direct(i, k, source):
        return remote(stats_out.at[early + i], direct_in.at[i, source], ss5.at[i, k], rs5.at[i, source], k)

    barrier = pltpu.get_barrier_semaphore()

    @pl.loop(1, n)
    def _(step):
        pl.semaphore_signal(barrier, inc=1, device_id={"img": peer(step)}, device_id_type=MESH)

    local_copies = [
        pltpu.make_async_copy(pairs, pairs_s, local_sem.at[0]),
        pltpu.make_async_copy(owner, owner_s, local_sem.at[1]),
        pltpu.make_async_copy(counts, counts_s, local_sem.at[2]),
        pltpu.make_async_copy(attr, own_attr, local_sem.at[3]),
        pltpu.make_async_copy(desc.at[0], own, local_sem.at[4]),
        *[pltpu.make_async_copy(piece_of(r, me), pieces[r].at[me], local_sem.at[7 + r]) for r in range(rounds)],
    ]
    for copy in local_copies:
        copy.start()
    local_attr = pltpu.make_async_copy(attr_piece(my_chunk), attr_in.at[me], local_sem.at[6])

    @pl.when(my_part == 0)
    def _():
        local_attr.start()

    for copy in local_copies[:3]:
        copy.wait()
    want = owner_s[pairs_s[0, 1]]
    count_a = counts_s[pairs_s[0, 0]]
    count_b = counts_s[pairs_s[0, 1]]
    want_row = jnp.full((1, LANES), want, jnp.int32)
    want_out[...] = want_row
    want_all[me] = want_row
    pl.semaphore_wait(barrier, n - 1)

    @pl.loop(1, n)
    def _(step):
        copy_want(peer(step), me).start()

    @pl.loop(0, chunks)
    def _(step):
        c = lax.rem(my_chunk + step, chunks)

        @pl.when(c * parts != me)
        def _():
            copy_attr_one(c, me).start()

    for r in range(rounds):
        @pl.loop(1, n)
        def _(step):
            copy_one(r, peer(step), me).start()

    for copy in local_copies[3:]:
        copy.wait()
    rows8 = with_ones(own_attr[0].astype(jnp.float32))
    own_rows[...] = rows8.astype(jnp.bfloat16)
    row_scale[...] = jnp.broadcast_to(jnp.transpose(rows8)[:, 0:1] * (1.0 / math.sqrt(depth)), (keypoints, LANES))
    for block in range(blocks):
        rows = slice(block * ROWS, (block + 1) * ROWS)
        own_t[rows, :] = jnp.transpose(own[:, rows])
    row_top[...] = jnp.full((keypoints, LANES), far_low, jnp.float32)

    @pl.loop(1, n)
    def _(step):
        k = peer(step)
        copy_want(k, k).wait_recv()

    to_scalars = pltpu.make_async_copy(want_all, want_s, local_sem.at[5])
    to_scalars.start()
    to_scalars.wait()

    @pl.when(my_part == 0)
    def _():
        local_attr.wait()

        @pl.loop(1, n)
        def _(step):
            k = peer(step)
            copy_attr_one(my_chunk, k).wait_recv()

        @pl.loop(1, n)
        def _(step):
            k = peer(step)
            attr_stage[k] = attr_in[want_s[k, 0, 0]]
            copy_attr_two(k, my_chunk).start()

        attr_other[my_chunk] = attr_in[want]

    for r in range(rounds):
        @pl.loop(1, n)
        def _(step):
            k = peer(step)
            copy_one(r, k, k).wait_recv()

        @pl.loop(1, n)
        def _(step):
            k = peer(step)
            stage[r, k] = pieces[r][want_s[k, 0, 0]]
            copy_two(r, k, me).start()

        partner[r, me] = pieces[r][want]

    for chunk in range(chunks):
        cols = slice(chunk * LANES, (chunk + 1) * LANES)

        @pl.when(chunk * parts != me)
        def _():
            copy_attr_two(chunk * parts, chunk).wait_recv()

        other8 = with_ones(attr_other[chunk].astype(jnp.float32))
        other_rows[:, cols] = other8.astype(jnp.bfloat16)
        other_scale[chunk] = other8[0:1]

    row_ix = lax.broadcasted_iota(jnp.int32, (ROWS, LANES), 0)
    lane_ix = lax.broadcasted_iota(jnp.int32, (1, LANES), 1)
    first_row = lax.broadcasted_iota(jnp.int32, (4, LANES), 0) == 0

    def score_chunk(step):
        r = step // round_chunks
        within = lax.rem(me // round_parts + step, round_chunks)
        c = r * round_chunks + within
        for part in range(round_parts):
            k = within * round_parts + part

            @pl.when(k != me)
            def _():
                copy_two(r, k, k).wait_recv()

        block_b = partner[r, pl.ds(within * round_parts, round_parts)].reshape(depth, LANES)
        scale_b = other_scale[c]
        col_valid = c * LANES + lane_ix < count_b
        col_top = jnp.full((1, LANES), far_low, jnp.float32)
        for block in range(blocks):
            rows = slice(block * ROWS, (block + 1) * ROWS)
            raw = jnp.dot(own_t[rows, :], block_b, preferred_element_type=jnp.float32)
            score = raw * row_scale[rows, :] * scale_b
            scores[c, rows, :] = score
            row_top[rows, :] = jnp.maximum(row_top[rows, :], jnp.where(col_valid, score, far_low))
            masked = jnp.where(block * ROWS + row_ix < count_a, score, far_low)
            col_top = jnp.maximum(col_top, jnp.max(masked, axis=0, keepdims=True))
        sums = jnp.zeros((8, LANES), jnp.float32)
        for block in range(blocks):
            rows = slice(block * ROWS, (block + 1) * ROWS)
            weight = jnp.where(block * ROWS + row_ix < count_a, jnp.exp(scores[c, rows, :] - col_top), 0.0)
            sums = sums + split_dot(own_rows[:, rows], weight, ((1,), (0,)))
        stats = jnp.where(first_row, col_top, sums[0:4])
        stats_out[c] = stats
        return c, within, stats

    def merge(slot, partial):
        hit = want_all[...] == slot
        tops = partial[:, 0:1, :]
        peak = jnp.maximum(jnp.max(jnp.where(hit, tops, far_low), axis=0), 0.0)
        fade = jnp.where(hit, jnp.exp(tops - peak[None]), 0.0)
        total = jnp.sum(fade * partial, axis=0)
        partition = jnp.exp(-peak) + total[1:2]
        return jnp.where(first_row, peak + jnp.log(partition), total / partition)

    @pl.loop(0, early)
    def _(step):
        c, _, stats = score_chunk(step)
        for part in range(parts):
            k = c * parts + part

            @pl.when(k != me)
            def _():
                copy_stats(k, me).start()

            @pl.when(k == me)
            def _():
                stats_in[me] = stats

    @pl.loop(early, chunks)
    def _(step):
        _, i, stats = score_chunk(step)
        direct_in[i, me] = stats

        @pl.loop(1, n)
        def _(hop):
            copy_direct(i, peer(hop), me).start()

    @pl.when(my_chunk < early)
    def _():
        @pl.loop(1, n)
        def _(step):
            k = peer(step)
            copy_stats(k, k).wait_recv()

        @pl.loop(0, chunks)
        def _(q):
            slot = my_part * chunks + q
            merged = merge(slot, stats_in[...])
            merged_out[q] = merged

            @pl.when(slot != me)
            def _():
                copy_merged(q, slot, my_chunk).start()

            @pl.when(slot == me)
            def _():
                merged_in[my_chunk] = merged

    for block in range(blocks):
        rows = slice(block * ROWS, (block + 1) * ROWS)
        top = jnp.max(row_top[rows, :], axis=1, keepdims=True)
        sums = jnp.zeros((8, ROWS), jnp.float32)
        for chunk in range(chunks):
            cols = slice(chunk * LANES, (chunk + 1) * LANES)
            weight = jnp.where(chunk * LANES + lane_ix < count_b, jnp.exp(scores[chunk, rows, :] - top), 0.0)
            sums = sums + split_dot(other_rows[:, cols], weight, ((1,), (1,)))
        row_valid = block * ROWS + lax.broadcasted_iota(jnp.int32, (2, ROWS), 1) < count_a
        match_o[0, :, rows] = jnp.where(row_valid, sums[2:4] / sums[1:2], 0.0)

    def write(chunk, result):
        cols = slice(chunk * LANES, (chunk + 1) * LANES)
        lse_o[:, cols] = result[0:1]
        xy_o[0, :, cols] = result[2:4]

    for i in range(round_chunks):
        @pl.loop(1, n)
        def _(step):
            k = peer(step)
            copy_direct(i, k, k).wait_recv()

        write(early + i, merge(me, direct_in[i]))

    home_part = me // chunks
    for chunk in range(early):
        k = chunk * parts + home_part

        @pl.when(k != me)
        def _():
            copy_merged(chunk, k, chunk).wait_recv()

        write(chunk, merged_in[chunk])

    @pl.loop(1, n)
    def _(step):
        k = peer(step)
        copy_want(k, me).wait_send()
        for r in range(rounds):
            copy_one(r, k, me).wait_send()
            copy_two(r, k, me).wait_send()
        for i in range(round_chunks):
            copy_direct(i, k, me).wait_send()

        @pl.when(k // parts < early)
        def _():
            copy_stats(k, me).wait_send()

    @pl.when(my_chunk < early)
    def _():
        @pl.loop(0, chunks)
        def _(q):
            slot = my_part * chunks + q

            @pl.when(slot != me)
            def _():
                copy_merged(q, slot, my_chunk).wait_send()

    @pl.loop(0, chunks)
    def _(c):
        @pl.when(c * parts != me)
        def _():
            copy_attr_one(c, me).wait_send()

    @pl.when(my_part == 0)
    def _():
        @pl.loop(1, n)
        def _(step):
            copy_attr_two(peer(step), my_chunk).wait_send()


def put_out(match, lse, xy, match_o, lse_o, xy_o, sem):
    copies = [
        pltpu.make_async_copy(match, match_o, sem.at[0]),
        pltpu.make_async_copy(lse, lse_o, sem.at[1]),
        pltpu.make_async_copy(xy, xy_o, sem.at[2]),
    ]
    for copy in copies:
        copy.start()
    for copy in copies:
        copy.wait()


def plan(keypoints):
    half, quarter, eighth = keypoints // 2, keypoints // 4, keypoints // 8
    spans = ((0, half + quarter), (half + quarter, quarter))
    subs = ((0, 0, half), (0, half, quarter), (1, 0, eighth), (1, eighth, eighth))
    return spans, subs


def tile_kernel(
    n, desc, attr, counts, owner, pairs, match_o, lse_o, xy_o,
    own, own_t, own_attr, row_scale, own_rows, other_rows, other_scale, want_out, want_all, want_s,
    counts_s, owner_s, pairs_s, attr_all, attr_stage, attr_other,
    scores, row_top, stats_out, stats_in, merged_out, merged_in, direct_in,
    local_sem, want_ss, want_rs, attr_ss1, attr_rs1, attr_ss2, attr_rs2,
    ss1, rs1, ss2, rs2, ss3, rs3, ss4, rs4, ss5, rs5, *buffers,
):
    depth, keypoints = desc.shape[1:]
    spans, subs = plan(keypoints)
    pieces = buffers[: len(spans)]
    stage = buffers[len(spans) : len(spans) + len(subs)]
    partner = buffers[len(spans) + len(subs) :]
    width = depth // n
    chunks = keypoints // LANES
    parts = n // chunks
    blocks = keypoints // ROWS
    direct = sum(w for r, _, w in subs if r == 1) // LANES
    early = chunks - direct
    team = 4
    me = lax.axis_index("img")
    my_chunk = me // parts
    my_part = lax.rem(me, parts)
    lead = me - lax.rem(me, team)

    seat = lax.rem(me, team)
    upper = (2 * me) // n

    def each_peer(act):
        @pl.loop(0, n)
        def _(step):
            row = step // team
            far = upper * row + (1 - upper) * (n // team - 1 - row)
            k = far * team + lax.rem(seat + step, team)

            @pl.when(k != me)
            def _():
                act(k)

    def remote(src, dst, send, recv, to):
        return pltpu.make_async_remote_copy(
            src_ref=src, dst_ref=dst, send_sem=send, recv_sem=recv, device_id={"img": to}, device_id_type=MESH
        )

    def drain(like, sem):
        pltpu.make_async_copy(like, like, sem).wait()

    def others(buffer):
        return buffer.at[pl.ds(0, n - 1)]

    def piece_of(r, k):
        first, w = spans[r]
        return desc.at[0, pl.ds(pl.multiple_of(k * width, width), width), pl.ds(first, w)]

    def copy_want(k):
        return remote(want_out, want_all.at[me], want_ss, want_rs, k)

    def copy_attr_one(k):
        return remote(attr.at[0], attr_all.at[me], attr_ss1, attr_rs1, k)

    def copy_attr_two(j, k):
        return remote(attr_stage.at[j], attr_other, attr_ss2.at[j], attr_rs2, k)

    def copy_one(r, k):
        return remote(piece_of(r, k), pieces[r].at[me], ss1.at[r], rs1.at[r], k)

    def copy_two(u, k):
        return remote(stage[u].at[k], partner[u].at[me], ss2.at[u], rs2.at[u], k)

    def copy_stats(c, k):
        return remote(stats_out.at[c], stats_in.at[me], ss3.at[k], rs3, k)

    def copy_merged(q, k, source_chunk):
        return remote(merged_out.at[q], merged_in.at[source_chunk], ss4.at[q], rs4.at[source_chunk], k)

    def copy_direct(i, k):
        return remote(stats_out.at[early + i], direct_in.at[i, me], ss5.at[i], rs5.at[i], k)

    barrier = pltpu.get_barrier_semaphore()

    each_peer(lambda k: pl.semaphore_signal(barrier, inc=1, device_id={"img": k}, device_id_type=MESH))

    local_copies = [
        pltpu.make_async_copy(pairs, pairs_s, local_sem.at[0]),
        pltpu.make_async_copy(owner, owner_s, local_sem.at[1]),
        pltpu.make_async_copy(counts, counts_s, local_sem.at[2]),
        pltpu.make_async_copy(attr, own_attr, local_sem.at[3]),
        pltpu.make_async_copy(desc.at[0], own, local_sem.at[4]),
        pltpu.make_async_copy(attr.at[0], attr_all.at[me], local_sem.at[6]),
        *[pltpu.make_async_copy(piece_of(r, me), pieces[r].at[me], local_sem.at[7 + r]) for r in range(len(spans))],
    ]
    for copy in local_copies:
        copy.start()
    for copy in local_copies[:3]:
        copy.wait()
    want = owner_s[pairs_s[0, 1]]
    count_a = counts_s[pairs_s[0, 0]]
    count_b = counts_s[pairs_s[0, 1]]
    want_row = jnp.full((1, LANES), want, jnp.int32)
    want_out[...] = want_row
    want_all[me] = want_row
    pl.semaphore_wait(barrier, n - 1)

    each_peer(lambda k: copy_want(k).start())
    each_peer(lambda k: copy_one(0, k).start())

    @pl.loop(0, n // team)
    def _(t):
        @pl.when(t * team != me)
        def _():
            copy_attr_one(t * team).start()

    each_peer(lambda k: copy_one(1, k).start())

    for copy in local_copies[3:]:
        copy.wait()
    rows8 = with_ones(own_attr[0].astype(jnp.float32))
    own_rows[...] = rows8.astype(jnp.bfloat16)
    row_scale[...] = jnp.broadcast_to(jnp.transpose(rows8)[:, 0:1] * (1.0 / math.sqrt(depth)), (keypoints, LANES))
    for block in range(blocks):
        rows = slice(block * ROWS, (block + 1) * ROWS)
        own_t[rows, :] = jnp.transpose(own[:, rows])
    row_top[...] = jnp.full((keypoints, LANES), far_low, jnp.float32)

    drain(others(want_all), want_rs)
    to_scalars = pltpu.make_async_copy(want_all, want_s, local_sem.at[5])
    to_scalars.start()
    to_scalars.wait()

    def forward(u):
        r, first, w = subs[u]

        def send(k):
            stage[u][k] = pieces[r][want_s[k, 0, 0], :, first : first + w]
            copy_two(u, k).start()

        each_peer(send)

        partner[u][me] = pieces[r][want, :, first : first + w]

    def forward_round(r):
        drain(others(pieces[r]), rs1.at[r])
        for u in range(len(subs)):
            if subs[u][0] == r:
                forward(u)

    forward_round(0)

    @pl.when(me == lead)
    def _():
        drain(others(attr_all), attr_rs1)
        for j in range(1, team):
            attr_stage[j] = attr_all[want_s[me + j, 0, 0]]
            copy_attr_two(j, me + j).start()
        attr_other[...] = attr_all[want]

    forward_round(1)

    @pl.when(me != lead)
    def _():
        drain(attr_other, attr_rs2)

    other8 = with_ones(attr_other[...].astype(jnp.float32))
    other_rows[...] = other8.astype(jnp.bfloat16)
    for chunk in range(chunks):
        other_scale[chunk] = other8[0:1, chunk * LANES : (chunk + 1) * LANES]

    row_ix = lax.broadcasted_iota(jnp.int32, (ROWS, LANES), 0)
    lane_ix = lax.broadcasted_iota(jnp.int32, (1, LANES), 1)
    first_row = lax.broadcasted_iota(jnp.int32, (4, LANES), 0) == 0

    def score_chunk(u, i, c):
        cols = pl.ds(pl.multiple_of(i * LANES, LANES), LANES)
        block_b = partner[u][:, :, cols].reshape(depth, LANES)
        scale_b = other_scale[c]
        col_valid = c * LANES + lane_ix < count_b
        col_top = jnp.full((1, LANES), far_low, jnp.float32)
        for block in range(blocks):
            rows = slice(block * ROWS, (block + 1) * ROWS)
            raw = jnp.dot(own_t[rows, :], block_b, preferred_element_type=jnp.float32)
            score = raw * row_scale[rows, :] * scale_b
            scores[c, rows, :] = score
            row_top[rows, :] = jnp.maximum(row_top[rows, :], jnp.where(col_valid, score, far_low))
            masked = jnp.where(block * ROWS + row_ix < count_a, score, far_low)
            col_top = jnp.maximum(col_top, jnp.max(masked, axis=0, keepdims=True))
        sums = jnp.zeros((8, LANES), jnp.float32)
        for block in range(blocks):
            rows = slice(block * ROWS, (block + 1) * ROWS)
            weight = jnp.where(block * ROWS + row_ix < count_a, jnp.exp(scores[c, rows, :] - col_top), 0.0)
            sums = sums + split_dot(own_rows[:, rows], weight, ((1,), (0,)))
        stats = jnp.where(first_row, col_top, sums[0:4])
        stats_out[c] = stats
        return stats

    def merge(slot, partial):
        hit = want_all[...] == slot
        tops = partial[:, 0:1, :]
        peak = jnp.maximum(jnp.max(jnp.where(hit, tops, far_low), axis=0), 0.0)
        fade = jnp.where(hit, jnp.exp(tops - peak[None]), 0.0)
        total = jnp.sum(fade * partial, axis=0)
        partition = jnp.exp(-peak) + total[1:2]
        return jnp.where(first_row, peak + jnp.log(partition), total / partition)

    for u in range(len(subs)):
        r, first, w = subs[u]
        base = (spans[r][0] + first) // LANES
        drain(others(partner[u]), rs2.at[u])
        if r == 0:
            @pl.loop(0, w // LANES)
            def _(i):
                c = base + i
                stats = score_chunk(u, i, c)
                for part in range(parts):
                    k = c * parts + part

                    @pl.when(k != me)
                    def _():
                        copy_stats(c, k).start()

                    @pl.when(k == me)
                    def _():
                        stats_in[me] = stats
        else:
            for i in range(w // LANES):
                d = base + i - early
                direct_in[d, me] = score_chunk(u, i, base + i)

                each_peer(lambda k: copy_direct(d, k).start())

    @pl.when(my_chunk < early)
    def _():
        drain(others(stats_in), rs3)

        @pl.loop(0, chunks)
        def _(q):
            slot = my_part * chunks + q
            merged = merge(slot, stats_in[...])
            merged_out[q] = merged

            @pl.when(slot != me)
            def _():
                copy_merged(q, slot, my_chunk).start()

            @pl.when(slot == me)
            def _():
                merged_in[my_chunk] = merged

    for block in range(blocks):
        rows = slice(block * ROWS, (block + 1) * ROWS)
        top = jnp.max(row_top[rows, :], axis=1, keepdims=True)
        sums = jnp.zeros((8, ROWS), jnp.float32)
        for chunk in range(chunks):
            cols = slice(chunk * LANES, (chunk + 1) * LANES)
            weight = jnp.where(chunk * LANES + lane_ix < count_b, jnp.exp(scores[chunk, rows, :] - top), 0.0)
            sums = sums + split_dot(other_rows[:, cols], weight, ((1,), (1,)))
        row_valid = block * ROWS + lax.broadcasted_iota(jnp.int32, (2, ROWS), 1) < count_a
        match_o[0, :, rows] = jnp.where(row_valid, sums[2:4] / sums[1:2], 0.0)

    def write(chunk, result):
        cols = slice(chunk * LANES, (chunk + 1) * LANES)
        lse_o[:, cols] = result[0:1]
        xy_o[0, :, cols] = result[2:4]

    drain(others(want_all), want_ss)
    for r in range(len(spans)):
        drain(others(pieces[r]), ss1.at[r])
    for u in range(len(subs)):
        drain(others(partner[u]), ss2.at[u])

    @pl.loop(0, n // team)
    def _(t):
        @pl.when(t * team != me)
        def _():
            drain(attr_other, attr_ss1)

    @pl.when(me == lead)
    def _():
        for j in range(1, team):
            copy_attr_two(j, me + j).wait_send()

    @pl.loop(0, early * parts)
    def _(k):
        @pl.when(k != me)
        def _():
            copy_stats(k // parts, k).wait_send()

    for i in range(direct):
        drain(others(direct_in.at[i]), rs5.at[i])
        write(early + i, merge(me, direct_in[i]))

    home_part = me // chunks
    for chunk in range(early):
        k = chunk * parts + home_part

        @pl.when(k != me)
        def _():
            copy_merged(0, k, chunk).wait_recv()

        write(chunk, merged_in[chunk])

    for i in range(direct):
        drain(others(direct_in.at[i]), ss5.at[i])

    @pl.when(my_chunk < early)
    def _():
        @pl.loop(0, chunks)
        def _(q):
            slot = my_part * chunks + q

            @pl.when(slot != me)
            def _():
                copy_merged(q, slot, my_chunk).wait_send()


def one_tile(n, descriptors, attributes, counts, owner_slot, pair_list):
    _, depth, keypoints = descriptors.shape
    chunks = keypoints // LANES
    spans, subs = plan(keypoints)
    width = depth // n
    direct = sum(w for r, _, w in subs if r == 1) // LANES
    vmem = pl.BlockSpec(memory_space=pltpu.VMEM)
    hbm = pl.BlockSpec(memory_space=pltpu.HBM)
    f32, bf16, i32 = jnp.float32, jnp.bfloat16, jnp.int32
    sems = pltpu.SemaphoreType.DMA
    shapes = (1, 2, keypoints), (1, keypoints), (1, 2, keypoints)
    out_shape = tuple(jax.ShapeDtypeStruct(shape, f32) for shape in shapes)
    results = pl.pallas_call(
        functools.partial(tile_kernel, n),
        out_shape=tuple(pltpu.VMEM(shape, f32) for shape in shapes),
        in_specs=[hbm] * 5,
        out_specs=(vmem, vmem, vmem),
        scratch_shapes=[
            pltpu.VMEM((depth, keypoints), bf16),
            pltpu.VMEM((keypoints, depth), bf16),
            pltpu.VMEM((1, 3, keypoints), bf16),
            pltpu.VMEM((keypoints, LANES), f32),
            pltpu.VMEM((8, keypoints), bf16),
            pltpu.VMEM((8, keypoints), bf16),
            pltpu.VMEM((chunks, 1, LANES), f32),
            pltpu.VMEM((1, LANES), i32),
            pltpu.VMEM((n, 1, LANES), i32),
            pltpu.SMEM((n, 1, LANES), i32),
            pltpu.SMEM(counts.shape, i32),
            pltpu.SMEM(owner_slot.shape, i32),
            pltpu.SMEM(pair_list.shape, i32),
            pltpu.VMEM((n, 3, keypoints), bf16),
            pltpu.VMEM((4, 3, keypoints), bf16),
            pltpu.VMEM((3, keypoints), bf16),
            pltpu.VMEM((chunks, keypoints, LANES), f32),
            pltpu.VMEM((keypoints, LANES), f32),
            pltpu.VMEM((chunks, 4, LANES), f32),
            pltpu.VMEM((n, 4, LANES), f32),
            pltpu.VMEM((chunks, 4, LANES), f32),
            pltpu.VMEM((chunks, 4, LANES), f32),
            pltpu.VMEM((direct, n, 4, LANES), f32),
            sems((7 + len(spans),)),
            sems,
            sems,
            sems,
            sems,
            sems((4,)),
            sems,
            *[sems((len(spans),))] * 2,
            *[sems((len(subs),))] * 2,
            sems((n,)),
            sems,
            *[sems((chunks,))] * 2,
            *[sems((direct,))] * 2,
            *[pltpu.VMEM((n, width, w), bf16) for _, w in spans],
            *[pltpu.VMEM((n, width, w), bf16) for _, _, w in subs] * 2,
        ],
        compiler_params=pltpu.CompilerParams(collective_id=0, has_side_effects=True),
    )(descriptors, attributes, counts, owner_slot, pair_list)
    return pl.pallas_call(
        put_out,
        out_shape=out_shape,
        in_specs=[vmem] * 3,
        out_specs=(hbm, hbm, hbm),
        scratch_shapes=[sems((3,))],
    )(*[pltpu.with_memory_space_constraint(result, pltpu.VMEM) for result in results])


def solution(mesh):
    n = mesh.shape["img"]

    def shards(descriptors, attributes, counts, owner_slot, pair_list):
        _, depth, keypoints = descriptors.shape
        if n * TILE == depth:
            return one_tile(n, descriptors, attributes, counts, owner_slot, pair_list)
        chunks = keypoints // LANES
        parts = n // chunks
        rounds = min(ROUNDS, depth * chunks // (n * MIN_WIDTH))
        width = depth * chunks // (n * rounds)
        vmem = pl.BlockSpec(memory_space=pltpu.VMEM)
        hbm = pl.BlockSpec(memory_space=pltpu.HBM)
        f32, bf16, i32 = jnp.float32, jnp.bfloat16, jnp.int32
        sems = pltpu.SemaphoreType.DMA
        out_shape = (
            jax.ShapeDtypeStruct((1, 2, keypoints), f32),
            jax.ShapeDtypeStruct((1, keypoints), f32),
            jax.ShapeDtypeStruct((1, 2, keypoints), f32),
        )
        results = pl.pallas_call(
            functools.partial(kernel, n, rounds),
            out_shape=out_shape,
            in_specs=[hbm] * 5,
            out_specs=(vmem, vmem, vmem),
            scratch_shapes=[
                pltpu.VMEM((depth, keypoints), bf16),
                pltpu.VMEM((keypoints, depth), bf16),
                pltpu.VMEM((1, 3, keypoints), bf16),
                pltpu.VMEM((keypoints, LANES), f32),
                pltpu.VMEM((8, keypoints), bf16),
                pltpu.VMEM((8, keypoints), bf16),
                pltpu.VMEM((chunks, 1, LANES), f32),
                pltpu.VMEM((1, LANES), i32),
                pltpu.VMEM((n, 1, LANES), i32),
                pltpu.SMEM((n, 1, LANES), i32),
                pltpu.SMEM(counts.shape, i32),
                pltpu.SMEM(owner_slot.shape, i32),
                pltpu.SMEM(pair_list.shape, i32),
                pltpu.VMEM((n, 3, LANES), bf16),
                pltpu.VMEM((n, 3, LANES), bf16),
                pltpu.VMEM((chunks, 3, LANES), bf16),
                *[pltpu.VMEM((rounds, n, width, LANES), bf16)] * 2,
                pltpu.VMEM((chunks, keypoints, LANES), f32),
                pltpu.VMEM((keypoints, LANES), f32),
                pltpu.VMEM((chunks, 4, LANES), f32),
                pltpu.VMEM((n, 4, LANES), f32),
                pltpu.VMEM((chunks, 4, LANES), f32),
                pltpu.VMEM((chunks, 4, LANES), f32),
                pltpu.VMEM((chunks // rounds, n, 4, LANES), f32),
                sems((7 + rounds,)),
                *[sems((n,))] * 2,
                sems((chunks,)),
                *[sems((n,))] * 2,
                sems((chunks,)),
                *[sems((rounds, n))] * 4,
                *[sems((n,))] * 2,
                *[sems((chunks,))] * 2,
                *[sems((chunks // rounds, n))] * 2,
                *[pltpu.VMEM((n, width, LANES), bf16)] * rounds,
            ],
            compiler_params=pltpu.CompilerParams(
                collective_id=0, has_side_effects=True
            ),
        )(descriptors, attributes, counts, owner_slot, pair_list)
        return pl.pallas_call(
            put_out,
            out_shape=out_shape,
            in_specs=[vmem] * 3,
            out_specs=(hbm, hbm, hbm),
            scratch_shapes=[sems((3,))],
        )(*results)

    placed = (
        P(("groups", "img"), None, None),
        P(("groups", "img"), None, None),
        P("groups"),
        P("groups"),
        P(("groups", "img"), None),
    )
    return jax.shard_map(
        shards,
        mesh=mesh,
        in_specs=placed,
        out_specs=(
            P(("groups", "img"), None, None),
            P(("groups", "img"), None),
            P(("groups", "img"), None, None),
        ),
        check_vma=False,
    )
```

```python
import functools
import math

import jax
import jax.numpy as jnp
from jax import lax
from jax.experimental import pallas as pl
from jax.experimental.pallas import tpu as pltpu
from jax.sharding import PartitionSpec as P

MESH = pl.DeviceIdType.MESH
LANES = 128
ROWS = 256
ROUNDS = 4
MIN_WIDTH = 16
TILE = 16
far_low = -1e30


def split_dot(left, right, contract):
    high = right.astype(jnp.bfloat16)
    low = (right - high.astype(jnp.float32)).astype(jnp.bfloat16)
    dims = (contract, ((), ()))
    return lax.dot_general(left, high, dims, preferred_element_type=jnp.float32) + lax.dot_general(
        left, low, dims, preferred_element_type=jnp.float32
    )


def with_ones(attr):
    ones = jnp.ones((1, attr.shape[1]), jnp.float32)
    rest = jnp.zeros((4, attr.shape[1]), jnp.float32)
    return jnp.concatenate([attr[0:1], ones, attr[1:3], rest], axis=0)


def kernel(
    n, rounds, desc, attr, counts, owner, pairs, match_o, lse_o, xy_o,
    own, own_t, own_attr, row_scale, own_rows, other_rows, other_scale, want_out, want_all, want_s,
    counts_s, owner_s, pairs_s, attr_in, attr_stage, attr_other,
    stage, partner, scores, row_top, stats_out, stats_in, merged_out, merged_in, direct_in,
    local_sem, want_ss, want_rs, attr_ss1, attr_rs1, attr_ss2, attr_rs2, ss1, rs1, ss2, rs2, ss3, rs3, ss4, rs4, ss5, rs5,
    *pieces,
):
    depth, keypoints = desc.shape[1:]
    chunks = keypoints // LANES
    parts = n // chunks
    blocks = keypoints // ROWS
    me = lax.axis_index("img")
    my_chunk = me // parts
    my_part = lax.rem(me, parts)
    round_chunks = chunks // rounds
    round_parts = n // round_chunks
    width = depth // round_parts
    early = chunks - round_chunks

    def peer(step):
        return lax.rem(me + step, n)

    def remote(src, dst, send, recv, to):
        return pltpu.make_async_remote_copy(
            src_ref=src, dst_ref=dst, send_sem=send, recv_sem=recv, device_id={"img": to}, device_id_type=MESH
        )

    def piece_of(r, k):
        row = pl.multiple_of(lax.rem(k, round_parts) * width, width)
        col = pl.multiple_of((r * round_chunks + k // round_parts) * LANES, LANES)
        return desc.at[0, pl.ds(row, width), pl.ds(col, LANES)]

    def attr_piece(c):
        return attr.at[0, :, pl.ds(pl.multiple_of(c * LANES, LANES), LANES)]

    def copy_want(k, source):
        return remote(want_out, want_all.at[source], want_ss.at[k], want_rs.at[source], k)

    def copy_attr_one(c, source):
        return remote(attr_piece(c), attr_in.at[source], attr_ss1.at[c], attr_rs1.at[source], c * parts)

    def copy_attr_two(k, source):
        return remote(attr_stage.at[k], attr_other.at[source], attr_ss2.at[k], attr_rs2.at[source], k)

    def copy_one(r, k, source):
        return remote(piece_of(r, k), pieces[r].at[source], ss1.at[r, k], rs1.at[r, source], k)

    def copy_two(r, k, source):
        return remote(stage.at[r, k], partner.at[r, source], ss2.at[r, k], rs2.at[r, source], k)

    def copy_stats(k, source):
        return remote(stats_out.at[k // parts], stats_in.at[source], ss3.at[k], rs3.at[source], k)

    def copy_merged(q, k, source_chunk):
        return remote(merged_out.at[q], merged_in.at[source_chunk], ss4.at[q], rs4.at[source_chunk], k)

    def copy_direct(i, k, source):
        return remote(stats_out.at[early + i], direct_in.at[i, source], ss5.at[i, k], rs5.at[i, source], k)

    barrier = pltpu.get_barrier_semaphore()

    @pl.loop(1, n)
    def _(step):
        pl.semaphore_signal(barrier, inc=1, device_id={"img": peer(step)}, device_id_type=MESH)

    local_copies = [
        pltpu.make_async_copy(pairs, pairs_s, local_sem.at[0]),
        pltpu.make_async_copy(owner, owner_s, local_sem.at[1]),
        pltpu.make_async_copy(counts, counts_s, local_sem.at[2]),
        pltpu.make_async_copy(attr, own_attr, local_sem.at[3]),
        pltpu.make_async_copy(desc.at[0], own, local_sem.at[4]),
        *[pltpu.make_async_copy(piece_of(r, me), pieces[r].at[me], local_sem.at[7 + r]) for r in range(rounds)],
    ]
    for copy in local_copies:
        copy.start()
    local_attr = pltpu.make_async_copy(attr_piece(my_chunk), attr_in.at[me], local_sem.at[6])

    @pl.when(my_part == 0)
    def _():
        local_attr.start()

    for copy in local_copies[:3]:
        copy.wait()
    want = owner_s[pairs_s[0, 1]]
    count_a = counts_s[pairs_s[0, 0]]
    count_b = counts_s[pairs_s[0, 1]]
    want_row = jnp.full((1, LANES), want, jnp.int32)
    want_out[...] = want_row
    want_all[me] = want_row
    pl.semaphore_wait(barrier, n - 1)

    @pl.loop(1, n)
    def _(step):
        copy_want(peer(step), me).start()

    @pl.loop(0, chunks)
    def _(step):
        c = lax.rem(my_chunk + step, chunks)

        @pl.when(c * parts != me)
        def _():
            copy_attr_one(c, me).start()

    for r in range(rounds):
        @pl.loop(1, n)
        def _(step):
            copy_one(r, peer(step), me).start()

    for copy in local_copies[3:]:
        copy.wait()
    rows8 = with_ones(own_attr[0].astype(jnp.float32))
    own_rows[...] = rows8.astype(jnp.bfloat16)
    row_scale[...] = jnp.broadcast_to(jnp.transpose(rows8)[:, 0:1] * (1.0 / math.sqrt(depth)), (keypoints, LANES))
    for block in range(blocks):
        rows = slice(block * ROWS, (block + 1) * ROWS)
        own_t[rows, :] = jnp.transpose(own[:, rows])
    row_top[...] = jnp.full((keypoints, LANES), far_low, jnp.float32)

    @pl.loop(1, n)
    def _(step):
        k = peer(step)
        copy_want(k, k).wait_recv()

    to_scalars = pltpu.make_async_copy(want_all, want_s, local_sem.at[5])
    to_scalars.start()
    to_scalars.wait()

    @pl.when(my_part == 0)
    def _():
        local_attr.wait()

        @pl.loop(1, n)
        def _(step):
            k = peer(step)
            copy_attr_one(my_chunk, k).wait_recv()

        @pl.loop(1, n)
        def _(step):
            k = peer(step)
            attr_stage[k] = attr_in[want_s[k, 0, 0]]
            copy_attr_two(k, my_chunk).start()

        attr_other[my_chunk] = attr_in[want]

    for r in range(rounds):
        @pl.loop(1, n)
        def _(step):
            k = peer(step)
            copy_one(r, k, k).wait_recv()

        @pl.loop(1, n)
        def _(step):
            k = peer(step)
            stage[r, k] = pieces[r][want_s[k, 0, 0]]
            copy_two(r, k, me).start()

        partner[r, me] = pieces[r][want]

    for chunk in range(chunks):
        cols = slice(chunk * LANES, (chunk + 1) * LANES)

        @pl.when(chunk * parts != me)
        def _():
            copy_attr_two(chunk * parts, chunk).wait_recv()

        other8 = with_ones(attr_other[chunk].astype(jnp.float32))
        other_rows[:, cols] = other8.astype(jnp.bfloat16)
        other_scale[chunk] = other8[0:1]

    row_ix = lax.broadcasted_iota(jnp.int32, (ROWS, LANES), 0)
    lane_ix = lax.broadcasted_iota(jnp.int32, (1, LANES), 1)
    first_row = lax.broadcasted_iota(jnp.int32, (4, LANES), 0) == 0

    def score_chunk(step):
        r = step // round_chunks
        within = lax.rem(me // round_parts + step, round_chunks)
        c = r * round_chunks + within
        for part in range(round_parts):
            k = within * round_parts + part

            @pl.when(k != me)
            def _():
                copy_two(r, k, k).wait_recv()

        block_b = partner[r, pl.ds(within * round_parts, round_parts)].reshape(depth, LANES)
        scale_b = other_scale[c]
        col_valid = c * LANES + lane_ix < count_b
        col_top = jnp.full((1, LANES), far_low, jnp.float32)
        for block in range(blocks):
            rows = slice(block * ROWS, (block + 1) * ROWS)
            raw = jnp.dot(own_t[rows, :], block_b, preferred_element_type=jnp.float32)
            score = raw * row_scale[rows, :] * scale_b
            scores[c, rows, :] = score
            row_top[rows, :] = jnp.maximum(row_top[rows, :], jnp.where(col_valid, score, far_low))
            masked = jnp.where(block * ROWS + row_ix < count_a, score, far_low)
            col_top = jnp.maximum(col_top, jnp.max(masked, axis=0, keepdims=True))
        sums = jnp.zeros((8, LANES), jnp.float32)
        for block in range(blocks):
            rows = slice(block * ROWS, (block + 1) * ROWS)
            weight = jnp.where(block * ROWS + row_ix < count_a, jnp.exp(scores[c, rows, :] - col_top), 0.0)
            sums = sums + split_dot(own_rows[:, rows], weight, ((1,), (0,)))
        stats = jnp.where(first_row, col_top, sums[0:4])
        stats_out[c] = stats
        return c, within, stats

    def merge(slot, partial):
        hit = want_all[...] == slot
        tops = partial[:, 0:1, :]
        peak = jnp.maximum(jnp.max(jnp.where(hit, tops, far_low), axis=0), 0.0)
        fade = jnp.where(hit, jnp.exp(tops - peak[None]), 0.0)
        total = jnp.sum(fade * partial, axis=0)
        partition = jnp.exp(-peak) + total[1:2]
        return jnp.where(first_row, peak + jnp.log(partition), total / partition)

    @pl.loop(0, early)
    def _(step):
        c, _, stats = score_chunk(step)
        for part in range(parts):
            k = c * parts + part

            @pl.when(k != me)
            def _():
                copy_stats(k, me).start()

            @pl.when(k == me)
            def _():
                stats_in[me] = stats

    @pl.loop(early, chunks)
    def _(step):
        _, i, stats = score_chunk(step)
        direct_in[i, me] = stats

        @pl.loop(1, n)
        def _(hop):
            copy_direct(i, peer(hop), me).start()

    @pl.when(my_chunk < early)
    def _():
        @pl.loop(1, n)
        def _(step):
            k = peer(step)
            copy_stats(k, k).wait_recv()

        @pl.loop(0, chunks)
        def _(q):
            slot = my_part * chunks + q
            merged = merge(slot, stats_in[...])
            merged_out[q] = merged

            @pl.when(slot != me)
            def _():
                copy_merged(q, slot, my_chunk).start()

            @pl.when(slot == me)
            def _():
                merged_in[my_chunk] = merged

    for block in range(blocks):
        rows = slice(block * ROWS, (block + 1) * ROWS)
        top = jnp.max(row_top[rows, :], axis=1, keepdims=True)
        sums = jnp.zeros((8, ROWS), jnp.float32)
        for chunk in range(chunks):
            cols = slice(chunk * LANES, (chunk + 1) * LANES)
            weight = jnp.where(chunk * LANES + lane_ix < count_b, jnp.exp(scores[chunk, rows, :] - top), 0.0)
            sums = sums + split_dot(other_rows[:, cols], weight, ((1,), (1,)))
        row_valid = block * ROWS + lax.broadcasted_iota(jnp.int32, (2, ROWS), 1) < count_a
        match_o[0, :, rows] = jnp.where(row_valid, sums[2:4] / sums[1:2], 0.0)

    def write(chunk, result):
        cols = slice(chunk * LANES, (chunk + 1) * LANES)
        lse_o[:, cols] = result[0:1]
        xy_o[0, :, cols] = result[2:4]

    for i in range(round_chunks):
        @pl.loop(1, n)
        def _(step):
            k = peer(step)
            copy_direct(i, k, k).wait_recv()

        write(early + i, merge(me, direct_in[i]))

    home_part = me // chunks
    for chunk in range(early):
        k = chunk * parts + home_part

        @pl.when(k != me)
        def _():
            copy_merged(chunk, k, chunk).wait_recv()

        write(chunk, merged_in[chunk])

    @pl.loop(1, n)
    def _(step):
        k = peer(step)
        copy_want(k, me).wait_send()
        for r in range(rounds):
            copy_one(r, k, me).wait_send()
            copy_two(r, k, me).wait_send()
        for i in range(round_chunks):
            copy_direct(i, k, me).wait_send()

        @pl.when(k // parts < early)
        def _():
            copy_stats(k, me).wait_send()

    @pl.when(my_chunk < early)
    def _():
        @pl.loop(0, chunks)
        def _(q):
            slot = my_part * chunks + q

            @pl.when(slot != me)
            def _():
                copy_merged(q, slot, my_chunk).wait_send()

    @pl.loop(0, chunks)
    def _(c):
        @pl.when(c * parts != me)
        def _():
            copy_attr_one(c, me).wait_send()

    @pl.when(my_part == 0)
    def _():
        @pl.loop(1, n)
        def _(step):
            copy_attr_two(peer(step), my_chunk).wait_send()


def put_out(match, lse, xy, match_o, lse_o, xy_o, sem):
    copies = [
        pltpu.make_async_copy(match, match_o, sem.at[0]),
        pltpu.make_async_copy(lse, lse_o, sem.at[1]),
        pltpu.make_async_copy(xy, xy_o, sem.at[2]),
    ]
    for copy in copies:
        copy.start()
    for copy in copies:
        copy.wait()


def plan(keypoints):
    half, quarter, eighth = keypoints // 2, keypoints // 4, keypoints // 8
    spans = ((0, half + quarter), (half + quarter, quarter))
    subs = ((0, 0, half), (0, half, quarter), (1, 0, eighth), (1, eighth, eighth))
    return spans, subs


def tile_kernel(
    n, desc, attr, counts, owner, pairs, match_o, lse_o, xy_o,
    own, own_t, own_attr, row_scale, own_rows, other_rows, other_scale, want_out, want_all, want_s,
    counts_s, owner_s, pairs_s, attr_all, attr_stage, attr_other,
    scores, stats_out, stats_in, merged_out, merged_in, direct_in,
    local_sem, want_ss, want_rs, attr_ss1, attr_rs1, attr_ss2, attr_rs2,
    ss1, rs1, ss2, rs2, ss3, rs3, ss4, rs4, ss5, rs5, *buffers,
):
    depth, keypoints = desc.shape[1:]
    spans, subs = plan(keypoints)
    pieces = buffers[: len(spans)]
    stage = buffers[len(spans) : len(spans) + len(subs)]
    partner = buffers[len(spans) + len(subs) :]
    width = depth // n
    chunks = keypoints // LANES
    parts = n // chunks
    blocks = keypoints // ROWS
    direct = sum(w for r, _, w in subs if r == 1) // LANES
    early = chunks - direct
    team = n // 4
    me = lax.axis_index("img")
    my_chunk = me // parts
    my_part = lax.rem(me, parts)
    lead = me - lax.rem(me, team)

    seat = lax.rem(me, team)
    my_row = me // team
    upper = my_row // 2
    lower = 1 - upper

    def each_in(rows, first, gap, act):
        @pl.loop(0, rows * team)
        def _(step):
            i = step // team
            row = lower * (rows - 1 - i) + upper * i
            k = (first + gap * row) * team + lax.rem(seat + step, team)

            @pl.when(k != me)
            def _():
                act(k)

    def each_peer(act):
        each_in(4, 0, 1, act)

    def each_inner(act):
        each_in(2, 1, 1, act)

    def each_outer(act):
        each_in(2, 0, 3, act)

    def remote(src, dst, send, recv, to):
        return pltpu.make_async_remote_copy(
            src_ref=src, dst_ref=dst, send_sem=send, recv_sem=recv, device_id={"img": to}, device_id_type=MESH
        )

    def drain(like, sem):
        pltpu.make_async_copy(like, like, sem).wait()

    def others(buffer):
        return buffer.at[pl.ds(0, n - 1)]

    def piece_of(r, k):
        first, w = spans[r]
        return desc.at[0, pl.ds(pl.multiple_of(k * width, width), width), pl.ds(first, w)]

    def copy_want(k):
        return remote(want_out, want_all.at[me], want_ss, want_rs, k)

    def copy_attr_one(k):
        return remote(attr.at[0], attr_all.at[me], attr_ss1, attr_rs1, k)

    def copy_attr_two(j, k):
        return remote(attr_stage.at[j], attr_other, attr_ss2.at[j], attr_rs2, k)

    def copy_one(r, k):
        return remote(piece_of(r, k), pieces[r].at[me], ss1.at[r], rs1.at[r], k)

    def copy_two(u, k):
        return remote(stage[u].at[k], partner[u].at[me], ss2.at[u], rs2.at[u], k)

    def copy_stats(c, k):
        return remote(stats_out.at[c], stats_in.at[me], ss3.at[k], rs3, k)

    def copy_merged(q, k, source_chunk):
        return remote(merged_out.at[q], merged_in.at[source_chunk], ss4.at[q], rs4.at[source_chunk], k)

    def copy_direct(i, k):
        return remote(stats_out.at[early + i], direct_in.at[i, me], ss5.at[i], rs5.at[i], k)

    barrier = pltpu.get_barrier_semaphore()

    inner = jnp.logical_or(my_row == 1, my_row == 2)

    def tell(k):
        pl.semaphore_signal(barrier, inc=1, device_id={"img": k}, device_id_type=MESH)

    @pl.when(inner)
    def _():
        each_inner(tell)

    local_copies = [
        pltpu.make_async_copy(pairs, pairs_s, local_sem.at[0]),
        pltpu.make_async_copy(owner, owner_s, local_sem.at[1]),
        pltpu.make_async_copy(counts, counts_s, local_sem.at[2]),
        pltpu.make_async_copy(attr, own_attr, local_sem.at[3]),
        pltpu.make_async_copy(desc.at[0], own, local_sem.at[4]),
        pltpu.make_async_copy(attr.at[0], attr_all.at[me], local_sem.at[6]),
        *[pltpu.make_async_copy(piece_of(r, me), pieces[r].at[me], local_sem.at[7 + r]) for r in range(len(spans))],
    ]
    for copy in local_copies:
        copy.start()

    for copy in local_copies[:3]:
        copy.wait()
    want = owner_s[pairs_s[0, 1]]
    count_a = counts_s[pairs_s[0, 0]]
    count_b = counts_s[pairs_s[0, 1]]
    want_row = jnp.full((1, LANES), want, jnp.int32)
    want_out[...] = want_row
    want_all[me] = want_row

    @pl.when(inner)
    def _():
        pl.semaphore_wait(barrier, 2 * team - 1)
        each_outer(tell)
        each_inner(lambda k: copy_want(k).start())
        each_inner(lambda k: copy_one(0, k).start())
        pl.semaphore_wait(barrier, 2 * team)
        each_outer(tell)
        each_outer(lambda k: copy_want(k).start())
        each_outer(lambda k: copy_one(0, k).start())

    @pl.when(jnp.logical_not(inner))
    def _():
        pl.semaphore_wait(barrier, 2 * team)
        each_inner(tell)
        each_inner(lambda k: copy_want(k).start())
        each_inner(lambda k: copy_one(0, k).start())
        pl.semaphore_wait(barrier, 2 * team)
        each_outer(lambda k: copy_want(k).start())
        each_outer(lambda k: copy_one(0, k).start())


    @pl.loop(0, n // team)
    def _(t):
        @pl.when(t * team != me)
        def _():
            copy_attr_one(t * team).start()

    each_peer(lambda k: copy_one(1, k).start())

    for copy in local_copies[3:]:
        copy.wait()
    rows8 = with_ones(own_attr[0].astype(jnp.float32))
    own_rows[...] = rows8.astype(jnp.bfloat16)
    row_scale[...] = jnp.broadcast_to(jnp.transpose(rows8)[:, 0:1] * (1.0 / math.sqrt(depth)), (keypoints, LANES))
    for block in range(blocks):
        rows = slice(block * ROWS, (block + 1) * ROWS)
        own_t[rows, :] = jnp.transpose(own[:, rows])

    drain(others(want_all), want_rs)
    to_scalars = pltpu.make_async_copy(want_all, want_s, local_sem.at[5])
    to_scalars.start()
    to_scalars.wait()

    def forward(u):
        r, first, w = subs[u]

        def send(k):
            stage[u][k] = pieces[r][want_s[k, 0, 0], :, first : first + w]
            copy_two(u, k).start()

        each_peer(send)

        partner[u][me] = pieces[r][want, :, first : first + w]

    def forward_round(r):
        drain(others(pieces[r]), rs1.at[r])
        for u in range(len(subs)):
            if subs[u][0] == r:
                forward(u)

    forward_round(0)

    @pl.when(me == lead)
    def _():
        drain(others(attr_all), attr_rs1)
        for j in range(1, team):
            attr_stage[j] = attr_all[want_s[me + j, 0, 0]]
            copy_attr_two(j, me + j).start()
        attr_other[...] = attr_all[want]

    forward_round(1)

    @pl.when(me != lead)
    def _():
        drain(attr_other, attr_rs2)

    other8 = with_ones(attr_other[...].astype(jnp.float32))
    other_rows[...] = other8.astype(jnp.bfloat16)
    for chunk in range(chunks):
        other_scale[chunk] = other8[0:1, chunk * LANES : (chunk + 1) * LANES]

    row_ix = lax.broadcasted_iota(jnp.int32, (ROWS, LANES), 0)
    lane_ix = lax.broadcasted_iota(jnp.int32, (1, LANES), 1)
    first_row = lax.broadcasted_iota(jnp.int32, (4, LANES), 0) == 0

    def score_chunk(u, i, c):
        cols = pl.ds(pl.multiple_of(i * LANES, LANES), LANES)
        block_b = partner[u][:, :, cols].reshape(depth, LANES)
        scale_b = other_scale[c]
        col_top = jnp.full((1, LANES), far_low, jnp.float32)
        for block in range(blocks):
            rows = slice(block * ROWS, (block + 1) * ROWS)
            raw = jnp.dot(own_t[rows, :], block_b, preferred_element_type=jnp.float32)
            score = raw * row_scale[rows, :] * scale_b
            scores[c, rows, :] = score
            masked = jnp.where(block * ROWS + row_ix < count_a, score, far_low)
            col_top = jnp.maximum(col_top, jnp.max(masked, axis=0, keepdims=True))
        sums = jnp.zeros((8, LANES), jnp.float32)
        for block in range(blocks):
            rows = slice(block * ROWS, (block + 1) * ROWS)
            weight = jnp.where(block * ROWS + row_ix < count_a, jnp.exp(scores[c, rows, :] - col_top), 0.0)
            sums = sums + split_dot(own_rows[:, rows], weight, ((1,), (0,)))
        stats = jnp.where(first_row, col_top, sums[0:4])
        stats_out[c] = stats
        return stats

    def merge(slot, partial):
        hit = want_all[...] == slot
        tops = partial[:, 0:1, :]
        peak = jnp.maximum(jnp.max(jnp.where(hit, tops, far_low), axis=0), 0.0)
        fade = jnp.where(hit, jnp.exp(tops - peak[None]), 0.0)
        total = jnp.sum(fade * partial, axis=0)
        partition = jnp.exp(-peak) + total[1:2]
        return jnp.where(first_row, peak + jnp.log(partition), total / partition)

    for u in range(len(subs)):
        r, first, w = subs[u]
        base = (spans[r][0] + first) // LANES
        drain(others(partner[u]), rs2.at[u])
        if r == 0:
            @pl.loop(0, w // LANES)
            def _(i):
                c = base + i
                stats = score_chunk(u, i, c)
                for part in range(parts):
                    k = c * parts + part

                    @pl.when(k != me)
                    def _():
                        copy_stats(c, k).start()

                    @pl.when(k == me)
                    def _():
                        stats_in[me] = stats
        else:
            for i in range(w // LANES):
                d = base + i - early
                direct_in[d, me] = score_chunk(u, i, base + i)

                each_peer(lambda k: copy_direct(d, k).start())

    @pl.when(my_chunk < early)
    def _():
        drain(others(stats_in), rs3)

        @pl.loop(0, chunks)
        def _(q):
            slot = my_part * chunks + q
            merged = merge(slot, stats_in[...])
            merged_out[q] = merged

            @pl.when(slot != me)
            def _():
                copy_merged(q, slot, my_chunk).start()

            @pl.when(slot == me)
            def _():
                merged_in[my_chunk] = merged

    for block in range(blocks):
        rows = slice(block * ROWS, (block + 1) * ROWS)
        top = jnp.full((ROWS, LANES), far_low, jnp.float32)
        for chunk in range(chunks):
            top = jnp.maximum(top, jnp.where(chunk * LANES + lane_ix < count_b, scores[chunk, rows, :], far_low))
        top = jnp.max(top, axis=1, keepdims=True)
        sums = jnp.zeros((8, ROWS), jnp.float32)
        for chunk in range(chunks):
            cols = slice(chunk * LANES, (chunk + 1) * LANES)
            weight = jnp.where(chunk * LANES + lane_ix < count_b, jnp.exp(scores[chunk, rows, :] - top), 0.0)
            sums = sums + split_dot(other_rows[:, cols], weight, ((1,), (1,)))
        row_valid = block * ROWS + lax.broadcasted_iota(jnp.int32, (2, ROWS), 1) < count_a
        match_o[0, :, rows] = jnp.where(row_valid, sums[2:4] / sums[1:2], 0.0)

    def write(chunk, result):
        cols = slice(chunk * LANES, (chunk + 1) * LANES)
        lse_o[:, cols] = result[0:1]
        xy_o[0, :, cols] = result[2:4]

    drain(others(want_all), want_ss)
    for r in range(len(spans)):
        drain(others(pieces[r]), ss1.at[r])
    for u in range(len(subs)):
        drain(others(partner[u]), ss2.at[u])

    @pl.loop(0, n // team)
    def _(t):
        @pl.when(t * team != me)
        def _():
            drain(attr_other, attr_ss1)

    @pl.when(me == lead)
    def _():
        for j in range(1, team):
            copy_attr_two(j, me + j).wait_send()

    @pl.loop(0, early * parts)
    def _(k):
        @pl.when(k != me)
        def _():
            copy_stats(k // parts, k).wait_send()

    for i in range(direct):
        drain(others(direct_in.at[i]), rs5.at[i])
        write(early + i, merge(me, direct_in[i]))

    home_part = me // chunks
    for chunk in range(early):
        k = chunk * parts + home_part

        @pl.when(k != me)
        def _():
            copy_merged(0, k, chunk).wait_recv()

        write(chunk, merged_in[chunk])

    for i in range(direct):
        drain(others(direct_in.at[i]), ss5.at[i])

    @pl.when(my_chunk < early)
    def _():
        @pl.loop(0, chunks)
        def _(q):
            slot = my_part * chunks + q

            @pl.when(slot != me)
            def _():
                copy_merged(q, slot, my_chunk).wait_send()


def one_tile(n, descriptors, attributes, counts, owner_slot, pair_list):
    _, depth, keypoints = descriptors.shape
    chunks = keypoints // LANES
    spans, subs = plan(keypoints)
    width = depth // n
    direct = sum(w for r, _, w in subs if r == 1) // LANES
    vmem = pl.BlockSpec(memory_space=pltpu.VMEM)
    hbm = pl.BlockSpec(memory_space=pltpu.HBM)
    f32, bf16, i32 = jnp.float32, jnp.bfloat16, jnp.int32
    sems = pltpu.SemaphoreType.DMA
    shapes = (1, 2, keypoints), (1, keypoints), (1, 2, keypoints)
    out_shape = tuple(jax.ShapeDtypeStruct(shape, f32) for shape in shapes)
    results = pl.pallas_call(
        functools.partial(tile_kernel, n),
        out_shape=tuple(pltpu.VMEM(shape, f32) for shape in shapes),
        in_specs=[hbm] * 5,
        out_specs=(vmem, vmem, vmem),
        scratch_shapes=[
            pltpu.VMEM((depth, keypoints), bf16),
            pltpu.VMEM((keypoints, depth), bf16),
            pltpu.VMEM((1, 3, keypoints), bf16),
            pltpu.VMEM((keypoints, LANES), f32),
            pltpu.VMEM((8, keypoints), bf16),
            pltpu.VMEM((8, keypoints), bf16),
            pltpu.VMEM((chunks, 1, LANES), f32),
            pltpu.VMEM((1, LANES), i32),
            pltpu.VMEM((n, 1, LANES), i32),
            pltpu.SMEM((n, 1, LANES), i32),
            pltpu.SMEM(counts.shape, i32),
            pltpu.SMEM(owner_slot.shape, i32),
            pltpu.SMEM(pair_list.shape, i32),
            pltpu.VMEM((n, 3, keypoints), bf16),
            pltpu.VMEM((4, 3, keypoints), bf16),
            pltpu.VMEM((3, keypoints), bf16),
            pltpu.VMEM((chunks, keypoints, LANES), f32),
            pltpu.VMEM((chunks, 4, LANES), f32),
            pltpu.VMEM((n, 4, LANES), f32),
            pltpu.VMEM((chunks, 4, LANES), f32),
            pltpu.VMEM((chunks, 4, LANES), f32),
            pltpu.VMEM((direct, n, 4, LANES), f32),
            sems((7 + len(spans),)),
            sems,
            sems,
            sems,
            sems,
            sems((4,)),
            sems,
            *[sems((len(spans),))] * 2,
            *[sems((len(subs),))] * 2,
            sems((n,)),
            sems,
            *[sems((chunks,))] * 2,
            *[sems((direct,))] * 2,
            *[pltpu.VMEM((n, width, w), bf16) for _, w in spans],
            *[pltpu.VMEM((n, width, w), bf16) for _, _, w in subs] * 2,
        ],
        compiler_params=pltpu.CompilerParams(collective_id=0, has_side_effects=True),
    )(descriptors, attributes, counts, owner_slot, pair_list)
    return pl.pallas_call(
        put_out,
        out_shape=out_shape,
        in_specs=[vmem] * 3,
        out_specs=(hbm, hbm, hbm),
        scratch_shapes=[sems((3,))],
    )(*[pltpu.with_memory_space_constraint(result, pltpu.VMEM) for result in results])


def solution(mesh):
    n = mesh.shape["img"]

    def shards(descriptors, attributes, counts, owner_slot, pair_list):
        _, depth, keypoints = descriptors.shape
        if n * TILE == depth and n % 4 == 0:
            return one_tile(n, descriptors, attributes, counts, owner_slot, pair_list)
        chunks = keypoints // LANES
        parts = n // chunks
        rounds = min(ROUNDS, depth * chunks // (n * MIN_WIDTH))
        width = depth * chunks // (n * rounds)
        vmem = pl.BlockSpec(memory_space=pltpu.VMEM)
        hbm = pl.BlockSpec(memory_space=pltpu.HBM)
        f32, bf16, i32 = jnp.float32, jnp.bfloat16, jnp.int32
        sems = pltpu.SemaphoreType.DMA
        out_shape = (
            jax.ShapeDtypeStruct((1, 2, keypoints), f32),
            jax.ShapeDtypeStruct((1, keypoints), f32),
            jax.ShapeDtypeStruct((1, 2, keypoints), f32),
        )
        results = pl.pallas_call(
            functools.partial(kernel, n, rounds),
            out_shape=out_shape,
            in_specs=[hbm] * 5,
            out_specs=(vmem, vmem, vmem),
            scratch_shapes=[
                pltpu.VMEM((depth, keypoints), bf16),
                pltpu.VMEM((keypoints, depth), bf16),
                pltpu.VMEM((1, 3, keypoints), bf16),
                pltpu.VMEM((keypoints, LANES), f32),
                pltpu.VMEM((8, keypoints), bf16),
                pltpu.VMEM((8, keypoints), bf16),
                pltpu.VMEM((chunks, 1, LANES), f32),
                pltpu.VMEM((1, LANES), i32),
                pltpu.VMEM((n, 1, LANES), i32),
                pltpu.SMEM((n, 1, LANES), i32),
                pltpu.SMEM(counts.shape, i32),
                pltpu.SMEM(owner_slot.shape, i32),
                pltpu.SMEM(pair_list.shape, i32),
                pltpu.VMEM((n, 3, LANES), bf16),
                pltpu.VMEM((n, 3, LANES), bf16),
                pltpu.VMEM((chunks, 3, LANES), bf16),
                *[pltpu.VMEM((rounds, n, width, LANES), bf16)] * 2,
                pltpu.VMEM((chunks, keypoints, LANES), f32),
                pltpu.VMEM((keypoints, LANES), f32),
                pltpu.VMEM((chunks, 4, LANES), f32),
                pltpu.VMEM((n, 4, LANES), f32),
                pltpu.VMEM((chunks, 4, LANES), f32),
                pltpu.VMEM((chunks, 4, LANES), f32),
                pltpu.VMEM((chunks // rounds, n, 4, LANES), f32),
                sems((7 + rounds,)),
                *[sems((n,))] * 2,
                sems((chunks,)),
                *[sems((n,))] * 2,
                sems((chunks,)),
                *[sems((rounds, n))] * 4,
                *[sems((n,))] * 2,
                *[sems((chunks,))] * 2,
                *[sems((chunks // rounds, n))] * 2,
                *[pltpu.VMEM((n, width, LANES), bf16)] * rounds,
            ],
            compiler_params=pltpu.CompilerParams(
                collective_id=0, has_side_effects=True
            ),
        )(descriptors, attributes, counts, owner_slot, pair_list)
        return pl.pallas_call(
            put_out,
            out_shape=out_shape,
            in_specs=[vmem] * 3,
            out_specs=(hbm, hbm, hbm),
            scratch_shapes=[sems((3,))],
        )(*results)

    placed = (
        P(("groups", "img"), None, None),
        P(("groups", "img"), None, None),
        P("groups"),
        P("groups"),
        P(("groups", "img"), None),
    )
    return jax.shard_map(
        shards,
        mesh=mesh,
        in_specs=placed,
        out_specs=(
            P(("groups", "img"), None, None),
            P(("groups", "img"), None),
            P(("groups", "img"), None, None),
        ),
        check_vma=False,
    )
```

```python
import functools
import math

import jax
import jax.numpy as jnp
from jax import lax
from jax.experimental import pallas as pl
from jax.experimental.pallas import tpu as pltpu
from jax.sharding import PartitionSpec as P

MESH = pl.DeviceIdType.MESH
LANES = 128
ROWS = 256
ROUNDS = 4
MIN_WIDTH = 16
TILE = 16
far_low = -1e30


def split_dot(left, right, contract):
    high = right.astype(jnp.bfloat16)
    low = (right - high.astype(jnp.float32)).astype(jnp.bfloat16)
    dims = (contract, ((), ()))
    return lax.dot_general(left, high, dims, preferred_element_type=jnp.float32) + lax.dot_general(
        left, low, dims, preferred_element_type=jnp.float32
    )


def with_ones(attr):
    ones = jnp.ones((1, attr.shape[1]), jnp.float32)
    rest = jnp.zeros((4, attr.shape[1]), jnp.float32)
    return jnp.concatenate([attr[0:1], ones, attr[1:3], rest], axis=0)


def kernel(
    n, rounds, desc, attr, counts, owner, pairs, match_o, lse_o, xy_o,
    own, own_t, own_attr, row_scale, own_rows, other_rows, other_scale, want_out, want_all, want_s,
    counts_s, owner_s, pairs_s, attr_in, attr_stage, attr_other,
    stage, partner, scores, row_top, stats_out, stats_in, merged_out, merged_in, direct_in,
    local_sem, want_ss, want_rs, attr_ss1, attr_rs1, attr_ss2, attr_rs2, ss1, rs1, ss2, rs2, ss3, rs3, ss4, rs4, ss5, rs5,
    *pieces,
):
    depth, keypoints = desc.shape[1:]
    chunks = keypoints // LANES
    parts = n // chunks
    blocks = keypoints // ROWS
    me = lax.axis_index("img")
    my_chunk = me // parts
    my_part = lax.rem(me, parts)
    round_chunks = chunks // rounds
    round_parts = n // round_chunks
    width = depth // round_parts
    early = chunks - round_chunks

    def peer(step):
        return lax.rem(me + step, n)

    def remote(src, dst, send, recv, to):
        return pltpu.make_async_remote_copy(
            src_ref=src, dst_ref=dst, send_sem=send, recv_sem=recv, device_id={"img": to}, device_id_type=MESH
        )

    def piece_of(r, k):
        row = pl.multiple_of(lax.rem(k, round_parts) * width, width)
        col = pl.multiple_of((r * round_chunks + k // round_parts) * LANES, LANES)
        return desc.at[0, pl.ds(row, width), pl.ds(col, LANES)]

    def attr_piece(c):
        return attr.at[0, :, pl.ds(pl.multiple_of(c * LANES, LANES), LANES)]

    def copy_want(k, source):
        return remote(want_out, want_all.at[source], want_ss.at[k], want_rs.at[source], k)

    def copy_attr_one(c, source):
        return remote(attr_piece(c), attr_in.at[source], attr_ss1.at[c], attr_rs1.at[source], c * parts)

    def copy_attr_two(k, source):
        return remote(attr_stage.at[k], attr_other.at[source], attr_ss2.at[k], attr_rs2.at[source], k)

    def copy_one(r, k, source):
        return remote(piece_of(r, k), pieces[r].at[source], ss1.at[r, k], rs1.at[r, source], k)

    def copy_two(r, k, source):
        return remote(stage.at[r, k], partner.at[r, source], ss2.at[r, k], rs2.at[r, source], k)

    def copy_stats(k, source):
        return remote(stats_out.at[k // parts], stats_in.at[source], ss3.at[k], rs3.at[source], k)

    def copy_merged(q, k, source_chunk):
        return remote(merged_out.at[q], merged_in.at[source_chunk], ss4.at[q], rs4.at[source_chunk], k)

    def copy_direct(i, k, source):
        return remote(stats_out.at[early + i], direct_in.at[i, source], ss5.at[i, k], rs5.at[i, source], k)

    barrier = pltpu.get_barrier_semaphore()

    @pl.loop(1, n)
    def _(step):
        pl.semaphore_signal(barrier, inc=1, device_id={"img": peer(step)}, device_id_type=MESH)

    local_copies = [
        pltpu.make_async_copy(pairs, pairs_s, local_sem.at[0]),
        pltpu.make_async_copy(owner, owner_s, local_sem.at[1]),
        pltpu.make_async_copy(counts, counts_s, local_sem.at[2]),
        pltpu.make_async_copy(attr, own_attr, local_sem.at[3]),
        pltpu.make_async_copy(desc.at[0], own, local_sem.at[4]),
        *[pltpu.make_async_copy(piece_of(r, me), pieces[r].at[me], local_sem.at[7 + r]) for r in range(rounds)],
    ]
    for copy in local_copies:
        copy.start()
    local_attr = pltpu.make_async_copy(attr_piece(my_chunk), attr_in.at[me], local_sem.at[6])

    @pl.when(my_part == 0)
    def _():
        local_attr.start()

    for copy in local_copies[:3]:
        copy.wait()
    want = owner_s[pairs_s[0, 1]]
    count_a = counts_s[pairs_s[0, 0]]
    count_b = counts_s[pairs_s[0, 1]]
    want_row = jnp.full((1, LANES), want, jnp.int32)
    want_out[...] = want_row
    want_all[me] = want_row
    pl.semaphore_wait(barrier, n - 1)

    @pl.loop(1, n)
    def _(step):
        copy_want(peer(step), me).start()

    @pl.loop(0, chunks)
    def _(step):
        c = lax.rem(my_chunk + step, chunks)

        @pl.when(c * parts != me)
        def _():
            copy_attr_one(c, me).start()

    for r in range(rounds):
        @pl.loop(1, n)
        def _(step):
            copy_one(r, peer(step), me).start()

    for copy in local_copies[3:]:
        copy.wait()
    rows8 = with_ones(own_attr[0].astype(jnp.float32))
    own_rows[...] = rows8.astype(jnp.bfloat16)
    row_scale[...] = jnp.broadcast_to(jnp.transpose(rows8)[:, 0:1] * (1.0 / math.sqrt(depth)), (keypoints, LANES))
    for block in range(blocks):
        rows = slice(block * ROWS, (block + 1) * ROWS)
        own_t[rows, :] = jnp.transpose(own[:, rows])
    row_top[...] = jnp.full((keypoints, LANES), far_low, jnp.float32)

    @pl.loop(1, n)
    def _(step):
        k = peer(step)
        copy_want(k, k).wait_recv()

    to_scalars = pltpu.make_async_copy(want_all, want_s, local_sem.at[5])
    to_scalars.start()
    to_scalars.wait()

    @pl.when(my_part == 0)
    def _():
        local_attr.wait()

        @pl.loop(1, n)
        def _(step):
            k = peer(step)
            copy_attr_one(my_chunk, k).wait_recv()

        @pl.loop(1, n)
        def _(step):
            k = peer(step)
            attr_stage[k] = attr_in[want_s[k, 0, 0]]
            copy_attr_two(k, my_chunk).start()

        attr_other[my_chunk] = attr_in[want]

    for r in range(rounds):
        @pl.loop(1, n)
        def _(step):
            k = peer(step)
            copy_one(r, k, k).wait_recv()

        @pl.loop(1, n)
        def _(step):
            k = peer(step)
            stage[r, k] = pieces[r][want_s[k, 0, 0]]
            copy_two(r, k, me).start()

        partner[r, me] = pieces[r][want]

    for chunk in range(chunks):
        cols = slice(chunk * LANES, (chunk + 1) * LANES)

        @pl.when(chunk * parts != me)
        def _():
            copy_attr_two(chunk * parts, chunk).wait_recv()

        other8 = with_ones(attr_other[chunk].astype(jnp.float32))
        other_rows[:, cols] = other8.astype(jnp.bfloat16)
        other_scale[chunk] = other8[0:1]

    row_ix = lax.broadcasted_iota(jnp.int32, (ROWS, LANES), 0)
    lane_ix = lax.broadcasted_iota(jnp.int32, (1, LANES), 1)
    first_row = lax.broadcasted_iota(jnp.int32, (4, LANES), 0) == 0

    def score_chunk(step):
        r = step // round_chunks
        within = lax.rem(me // round_parts + step, round_chunks)
        c = r * round_chunks + within
        for part in range(round_parts):
            k = within * round_parts + part

            @pl.when(k != me)
            def _():
                copy_two(r, k, k).wait_recv()

        block_b = partner[r, pl.ds(within * round_parts, round_parts)].reshape(depth, LANES)
        scale_b = other_scale[c]
        col_valid = c * LANES + lane_ix < count_b
        col_top = jnp.full((1, LANES), far_low, jnp.float32)
        for block in range(blocks):
            rows = slice(block * ROWS, (block + 1) * ROWS)
            raw = jnp.dot(own_t[rows, :], block_b, preferred_element_type=jnp.float32)
            score = raw * row_scale[rows, :] * scale_b
            scores[c, rows, :] = score
            row_top[rows, :] = jnp.maximum(row_top[rows, :], jnp.where(col_valid, score, far_low))
            masked = jnp.where(block * ROWS + row_ix < count_a, score, far_low)
            col_top = jnp.maximum(col_top, jnp.max(masked, axis=0, keepdims=True))
        sums = jnp.zeros((8, LANES), jnp.float32)
        for block in range(blocks):
            rows = slice(block * ROWS, (block + 1) * ROWS)
            weight = jnp.where(block * ROWS + row_ix < count_a, jnp.exp(scores[c, rows, :] - col_top), 0.0)
            sums = sums + split_dot(own_rows[:, rows], weight, ((1,), (0,)))
        stats = jnp.where(first_row, col_top, sums[0:4])
        stats_out[c] = stats
        return c, within, stats

    def merge(slot, partial):
        hit = want_all[...] == slot
        tops = partial[:, 0:1, :]
        peak = jnp.maximum(jnp.max(jnp.where(hit, tops, far_low), axis=0), 0.0)
        fade = jnp.where(hit, jnp.exp(tops - peak[None]), 0.0)
        total = jnp.sum(fade * partial, axis=0)
        partition = jnp.exp(-peak) + total[1:2]
        return jnp.where(first_row, peak + jnp.log(partition), total / partition)

    @pl.loop(0, early)
    def _(step):
        c, _, stats = score_chunk(step)
        for part in range(parts):
            k = c * parts + part

            @pl.when(k != me)
            def _():
                copy_stats(k, me).start()

            @pl.when(k == me)
            def _():
                stats_in[me] = stats

    @pl.loop(early, chunks)
    def _(step):
        _, i, stats = score_chunk(step)
        direct_in[i, me] = stats

        @pl.loop(1, n)
        def _(hop):
            copy_direct(i, peer(hop), me).start()

    @pl.when(my_chunk < early)
    def _():
        @pl.loop(1, n)
        def _(step):
            k = peer(step)
            copy_stats(k, k).wait_recv()

        @pl.loop(0, chunks)
        def _(q):
            slot = my_part * chunks + q
            merged = merge(slot, stats_in[...])
            merged_out[q] = merged

            @pl.when(slot != me)
            def _():
                copy_merged(q, slot, my_chunk).start()

            @pl.when(slot == me)
            def _():
                merged_in[my_chunk] = merged

    for block in range(blocks):
        rows = slice(block * ROWS, (block + 1) * ROWS)
        top = jnp.max(row_top[rows, :], axis=1, keepdims=True)
        sums = jnp.zeros((8, ROWS), jnp.float32)
        for chunk in range(chunks):
            cols = slice(chunk * LANES, (chunk + 1) * LANES)
            weight = jnp.where(chunk * LANES + lane_ix < count_b, jnp.exp(scores[chunk, rows, :] - top), 0.0)
            sums = sums + split_dot(other_rows[:, cols], weight, ((1,), (1,)))
        row_valid = block * ROWS + lax.broadcasted_iota(jnp.int32, (2, ROWS), 1) < count_a
        match_o[0, :, rows] = jnp.where(row_valid, sums[2:4] / sums[1:2], 0.0)

    def write(chunk, result):
        cols = slice(chunk * LANES, (chunk + 1) * LANES)
        lse_o[:, cols] = result[0:1]
        xy_o[0, :, cols] = result[2:4]

    for i in range(round_chunks):
        @pl.loop(1, n)
        def _(step):
            k = peer(step)
            copy_direct(i, k, k).wait_recv()

        write(early + i, merge(me, direct_in[i]))

    home_part = me // chunks
    for chunk in range(early):
        k = chunk * parts + home_part

        @pl.when(k != me)
        def _():
            copy_merged(chunk, k, chunk).wait_recv()

        write(chunk, merged_in[chunk])

    @pl.loop(1, n)
    def _(step):
        k = peer(step)
        copy_want(k, me).wait_send()
        for r in range(rounds):
            copy_one(r, k, me).wait_send()
            copy_two(r, k, me).wait_send()
        for i in range(round_chunks):
            copy_direct(i, k, me).wait_send()

        @pl.when(k // parts < early)
        def _():
            copy_stats(k, me).wait_send()

    @pl.when(my_chunk < early)
    def _():
        @pl.loop(0, chunks)
        def _(q):
            slot = my_part * chunks + q

            @pl.when(slot != me)
            def _():
                copy_merged(q, slot, my_chunk).wait_send()

    @pl.loop(0, chunks)
    def _(c):
        @pl.when(c * parts != me)
        def _():
            copy_attr_one(c, me).wait_send()

    @pl.when(my_part == 0)
    def _():
        @pl.loop(1, n)
        def _(step):
            copy_attr_two(peer(step), my_chunk).wait_send()


def put_out(match, lse, xy, match_o, lse_o, xy_o, sem):
    copies = [
        pltpu.make_async_copy(match, match_o, sem.at[0]),
        pltpu.make_async_copy(lse, lse_o, sem.at[1]),
        pltpu.make_async_copy(xy, xy_o, sem.at[2]),
    ]
    for copy in copies:
        copy.start()
    for copy in copies:
        copy.wait()


MERGED_SUBS = 1


def plan(keypoints):
    half, quarter, eighth = keypoints // 2, keypoints // 4, keypoints // 8
    spans = ((0, half + quarter), (half + quarter, quarter))
    subs = ((0, 0, half), (0, half, quarter), (1, 0, quarter))
    return spans, subs


def tile_kernel(
    n, desc, attr, counts, owner, pairs, match_o, lse_o, xy_o,
    own, own_t, own_attr, row_scale, own_rows, other_rows, other_scale, want_out, want_all, want_s,
    counts_s, owner_s, pairs_s, attr_all, attr_stage, attr_other,
    scores, stats_out, stats_in, merged_out, merged_in,
    local_sem, want_ss, want_rs, attr_ss1, attr_rs1, attr_ss2, attr_rs2,
    ss1, rs1, ss2, rs2, ss3, rs3, ss4, rs4, ss5, rs5, *buffers,
):
    depth, keypoints = desc.shape[1:]
    spans, subs = plan(keypoints)
    pieces = buffers[: len(spans)]
    stage = buffers[len(spans) : len(spans) + len(subs)]
    partner = buffers[len(spans) + len(subs) : len(spans) + 2 * len(subs)]
    late = MERGED_SUBS
    direct_out = buffers[len(spans) + 2 * len(subs) : len(spans) + 3 * len(subs) - late]
    direct_in = buffers[len(spans) + 3 * len(subs) - late :]
    width = depth // n
    chunks = keypoints // LANES
    parts = n // chunks
    blocks = keypoints // ROWS
    early = sum(w for _, _, w in subs[:MERGED_SUBS]) // LANES
    team = n // 4
    me = lax.axis_index("img")
    my_chunk = lax.rem(me, chunks)
    my_part = me // chunks

    seat = lax.rem(me, team)
    my_row = me // team
    upper = my_row // 2
    lower = 1 - upper
    half = n // 2
    leads = half - team, half
    lead = lower * leads[0] + upper * leads[1]

    def each_in(rows, first, gap, act):
        @pl.loop(0, rows * team)
        def _(step):
            i = step // team
            row = lower * (rows - 1 - i) + upper * i
            k = (first + gap * row) * team + lax.rem(seat + step, team)

            @pl.when(k != me)
            def _():
                act(k)

    def each_peer(act):
        each_in(4, 0, 1, act)

    def each_of(first, last, act):
        @pl.loop(first, last)
        def _(k):
            @pl.when(k != me)
            def _():
                act(k)

    def each_inner(act):
        each_in(2, 1, 1, act)

    def each_outer(act):
        each_in(2, 0, 3, act)

    def remote(src, dst, send, recv, to):
        return pltpu.make_async_remote_copy(
            src_ref=src, dst_ref=dst, send_sem=send, recv_sem=recv, device_id={"img": to}, device_id_type=MESH
        )

    def drain(like, sem):
        pltpu.make_async_copy(like, like, sem).wait()

    def others(buffer):
        return buffer.at[pl.ds(0, n - 1)]

    def piece_of(r, k):
        first, w = spans[r]
        return desc.at[0, pl.ds(pl.multiple_of(k * width, width), width), pl.ds(first, w)]

    def copy_want(k):
        return remote(want_out, want_all.at[me], want_ss, want_rs, k)

    def copy_attr_one(k):
        return remote(attr.at[0], attr_all.at[me], attr_ss1, attr_rs1, k)

    def copy_attr_two(j, k):
        return remote(attr_stage.at[j], attr_other, attr_ss2.at[j], attr_rs2, k)

    def copy_one(r, k):
        return remote(piece_of(r, k), pieces[r].at[me], ss1.at[r], rs1.at[r], k)

    def copy_two(u, k):
        return remote(stage[u].at[k], partner[u].at[me], ss2.at[u], rs2.at[u], k)

    def copy_stats(c, k):
        return remote(stats_out.at[c], stats_in.at[me], ss3.at[k], rs3, k)

    def copy_merged(q, k, source_chunk):
        return remote(merged_out.at[q], merged_in.at[source_chunk], ss4.at[q], rs4.at[source_chunk], k)

    def copy_direct(i, k):
        return remote(direct_out[i], direct_in[i].at[me], ss5.at[i], rs5.at[i], k)

    barrier = pltpu.get_barrier_semaphore()

    inner = jnp.logical_or(my_row == 1, my_row == 2)

    def tell(k):
        pl.semaphore_signal(barrier, inc=1, device_id={"img": k}, device_id_type=MESH)

    @pl.when(inner)
    def _():
        each_inner(tell)

    local_copies = [
        pltpu.make_async_copy(pairs, pairs_s, local_sem.at[0]),
        pltpu.make_async_copy(owner, owner_s, local_sem.at[1]),
        pltpu.make_async_copy(counts, counts_s, local_sem.at[2]),
        pltpu.make_async_copy(attr, own_attr, local_sem.at[3]),
        pltpu.make_async_copy(desc.at[0], own, local_sem.at[4]),
        pltpu.make_async_copy(attr.at[0], attr_all.at[me], local_sem.at[6]),
        *[pltpu.make_async_copy(piece_of(r, me), pieces[r].at[me], local_sem.at[7 + r]) for r in range(len(spans))],
    ]
    for copy in local_copies:
        copy.start()

    for copy in local_copies[:3]:
        copy.wait()
    want = owner_s[pairs_s[0, 1]]
    count_a = counts_s[pairs_s[0, 0]]
    count_b = counts_s[pairs_s[0, 1]]
    want_row = jnp.full((1, LANES), want, jnp.int32)
    want_out[...] = want_row
    want_all[me] = want_row

    def send_attr():
        for k in leads:
            @pl.when(me != k)
            def _():
                copy_attr_one(k).start()

    @pl.when(inner)
    def _():
        pl.semaphore_wait(barrier, 2 * team - 1)
        each_outer(tell)
        each_inner(lambda k: copy_want(k).start())
        each_inner(lambda k: copy_one(0, k).start())
        pl.semaphore_wait(barrier, 2 * team)
        each_outer(tell)
        each_outer(lambda k: copy_want(k).start())
        each_outer(lambda k: copy_one(0, k).start())

    @pl.when(jnp.logical_not(inner))
    def _():
        pl.semaphore_wait(barrier, 2 * team)
        each_inner(tell)
        each_inner(lambda k: copy_want(k).start())
        each_inner(lambda k: copy_one(0, k).start())
        pl.semaphore_wait(barrier, 2 * team)
        each_outer(lambda k: copy_want(k).start())
        each_outer(lambda k: copy_one(0, k).start())


    send_attr()
    each_peer(lambda k: copy_one(1, k).start())

    for copy in local_copies[3:]:
        copy.wait()
    rows8 = with_ones(own_attr[0].astype(jnp.float32))
    own_rows[...] = rows8.astype(jnp.bfloat16)
    row_scale[...] = jnp.broadcast_to(jnp.transpose(rows8)[:, 0:1] * (1.0 / math.sqrt(depth)), (keypoints, LANES))
    for block in range(blocks):
        rows = slice(block * ROWS, (block + 1) * ROWS)
        own_t[rows, :] = jnp.transpose(own[:, rows])

    drain(others(want_all), want_rs)
    to_scalars = pltpu.make_async_copy(want_all, want_s, local_sem.at[5])
    to_scalars.start()
    to_scalars.wait()

    def forward(r, group):
        def send(k):
            pick = want_s[k, 0, 0]
            for u in group:
                _, first, w = subs[u]
                stage[u][k] = pieces[r][pick, :, first : first + w]
                copy_two(u, k).start()

        each_peer(send)
        for u in group:
            _, first, w = subs[u]
            partner[u][me] = pieces[r][want, :, first : first + w]

    def forward_round(r):
        drain(others(pieces[r]), rs1.at[r])
        group = [u for u in range(len(subs)) if subs[u][0] == r]
        if r == 0:
            for u in group:
                forward(r, [u])
        else:
            forward(r, group)

    forward_round(0)
    @pl.when(me == lead)
    def _():
        drain(others(attr_all), attr_rs1)

        @pl.loop(0, half)
        def _(j):
            k = upper * half + j

            @pl.when(k != me)
            def _():
                attr_stage[j] = attr_all[want_s[k, 0, 0]]
                copy_attr_two(j, k).start()

        attr_other[...] = attr_all[want]


    forward_round(1)

    @pl.when(me != lead)
    def _():
        drain(attr_other, attr_rs2)

    other8 = with_ones(attr_other[...].astype(jnp.float32))
    other_rows[...] = other8.astype(jnp.bfloat16)
    for chunk in range(chunks):
        other_scale[chunk] = other8[0:1, chunk * LANES : (chunk + 1) * LANES]

    lane_ix = lax.broadcasted_iota(jnp.int32, (1, LANES), 1)
    first_row = lax.broadcasted_iota(jnp.int32, (4, LANES), 0) == 0

    def score(u, first_chunk):
        w = subs[u][2]
        tall = ROWS // 2 if w > 2 * LANES else ROWS
        row_ix = lax.broadcasted_iota(jnp.int32, (tall, LANES), 0)
        lanes = [slice(i * LANES, (i + 1) * LANES) for i in range(w // LANES)]
        block_b = partner[u][...].reshape(depth, w)
        tops = [jnp.full((8, LANES), far_low, jnp.float32) for _ in lanes]
        for block in range(keypoints // tall):
            rows = slice(block * tall, (block + 1) * tall)
            raw = jnp.dot(own_t[rows, :], block_b, preferred_element_type=jnp.float32)
            valid = block * tall + row_ix < count_a
            for i, cols in enumerate(lanes):
                scaled = raw[:, cols] * row_scale[rows, :] * other_scale[first_chunk + i]
                masked = jnp.where(valid, scaled, far_low)
                scores[first_chunk + i, rows, :] = masked
                tops[i] = jnp.maximum(tops[i], jnp.max(masked.reshape(tall // 8, 8, LANES), axis=0))
        tops = [jnp.max(top, axis=0, keepdims=True) for top in tops]
        sums = [jnp.zeros((8, LANES), jnp.float32) for _ in lanes]
        for block in range(keypoints // tall):
            rows = slice(block * tall, (block + 1) * tall)
            weight = [jnp.exp(scores[first_chunk + i, rows, :] - top) for i, top in enumerate(tops)]
            part = split_dot(own_rows[:, rows], jnp.concatenate(weight, axis=1), ((1,), (0,)))
            sums = [total + part[:, cols] for total, cols in zip(sums, lanes)]
        return [jnp.where(first_row, top, total[0:4]) for top, total in zip(tops, sums)]

    def merge(slot, partial):
        hit = want_all[...] == slot
        tops = partial[:, 0:1, :]
        peak = jnp.maximum(jnp.max(jnp.where(hit, tops, far_low), axis=0), 0.0)
        fade = jnp.where(hit, jnp.exp(tops - peak[None]), 0.0)
        total = jnp.sum(fade * partial, axis=0)
        partition = jnp.exp(-peak) + total[1:2]
        return jnp.where(first_row, peak + jnp.log(partition), total / partition)

    for u in range(len(subs)):
        r, first, w = subs[u]
        base = (spans[r][0] + first) // LANES
        drain(others(partner[u]), rs2.at[u])
        for i, stats in enumerate(score(u, base)):
            c = base + i
            if u < late:
                stats_out[c] = stats
                for part in range(parts):
                    k = part * chunks + c

                    @pl.when(k != me)
                    def _():
                        copy_stats(c, k).start()

                    @pl.when(k == me)
                    def _():
                        stats_in[me] = stats
            else:
                cols = slice(i * LANES, (i + 1) * LANES)
                direct_out[u - late][:, cols] = stats
                direct_in[u - late][me, :, cols] = stats
        if u >= late:
            each_of(0, team, lambda k: copy_direct(u - late, k).start())

    def send_rest(k):
        for i in range(len(subs) - late):
            copy_direct(i, k).start()

    each_of(team, n, send_rest)


    @pl.when(my_chunk < early)
    def _():
        drain(others(stats_in), rs3)

        @pl.loop(0, chunks)
        def _(q):
            slot = my_part * chunks + q
            merged = merge(slot, stats_in[...])
            merged_out[q] = merged

            @pl.when(slot != me)
            def _():
                copy_merged(q, slot, my_chunk).start()

            @pl.when(slot == me)
            def _():
                merged_in[my_chunk] = merged

    for block in range(blocks):
        rows = slice(block * ROWS, (block + 1) * ROWS)
        top = jnp.full((ROWS, LANES), far_low, jnp.float32)
        for chunk in range(chunks):
            top = jnp.maximum(top, jnp.where(chunk * LANES + lane_ix < count_b, scores[chunk, rows, :], far_low))
        top = jnp.max(top, axis=1, keepdims=True)
        sums = jnp.zeros((8, ROWS), jnp.float32)
        for chunk in range(chunks):
            cols = slice(chunk * LANES, (chunk + 1) * LANES)
            weight = jnp.where(chunk * LANES + lane_ix < count_b, jnp.exp(scores[chunk, rows, :] - top), 0.0)
            sums = sums + split_dot(other_rows[:, cols], weight, ((1,), (1,)))
        row_valid = block * ROWS + lax.broadcasted_iota(jnp.int32, (2, ROWS), 1) < count_a
        match_o[0, :, rows] = jnp.where(row_valid, sums[2:4] / sums[1:2], 0.0)

    def write(chunk, result):
        cols = slice(chunk * LANES, (chunk + 1) * LANES)
        lse_o[:, cols] = result[0:1]
        xy_o[0, :, cols] = result[2:4]

    drain(others(want_all), want_ss)
    for r in range(len(spans)):
        drain(others(pieces[r]), ss1.at[r])
    for u in range(len(subs)):
        drain(others(partner[u]), ss2.at[u])

    for k in leads:
        @pl.when(me != k)
        def _():
            drain(attr_other, attr_ss1)

    @pl.when(me == lead)
    def _():
        @pl.loop(0, half)
        def _(j):
            k = upper * half + j

            @pl.when(k != me)
            def _():
                copy_attr_two(j, k).wait_send()

    for part in range(parts):
        @pl.loop(0, early)
        def _(c):
            k = part * chunks + c

            @pl.when(k != me)
            def _():
                copy_stats(c, k).wait_send()

    for i in range(len(subs) - late):
        drain(others(direct_in[i]), ss5.at[i])

    @pl.when(my_chunk < early)
    def _():
        @pl.loop(0, chunks)
        def _(q):
            slot = my_part * chunks + q

            @pl.when(slot != me)
            def _():
                copy_merged(q, slot, my_chunk).wait_send()

    for chunk in range(early):
        k = my_part * chunks + chunk

        @pl.when(k != me)
        def _():
            copy_merged(0, k, chunk).wait_recv()

        write(chunk, merged_in[chunk])

    for u in range(late, len(subs)):
        i = u - late
        drain(others(direct_in[i]), rs5.at[i])
        for j in range(subs[u][2] // LANES):
            part = direct_in[i][:, :, j * LANES : (j + 1) * LANES]
            write((spans[subs[u][0]][0] + subs[u][1]) // LANES + j, merge(me, part))


def one_tile(n, descriptors, attributes, counts, owner_slot, pair_list):
    _, depth, keypoints = descriptors.shape
    chunks = keypoints // LANES
    spans, subs = plan(keypoints)
    width = depth // n
    late = [w for _, _, w in subs[MERGED_SUBS:]]
    vmem = pl.BlockSpec(memory_space=pltpu.VMEM)
    hbm = pl.BlockSpec(memory_space=pltpu.HBM)
    f32, bf16, i32 = jnp.float32, jnp.bfloat16, jnp.int32
    sems = pltpu.SemaphoreType.DMA
    shapes = (1, 2, keypoints), (1, keypoints), (1, 2, keypoints)
    out_shape = tuple(jax.ShapeDtypeStruct(shape, f32) for shape in shapes)
    results = pl.pallas_call(
        functools.partial(tile_kernel, n),
        out_shape=tuple(pltpu.VMEM(shape, f32) for shape in shapes),
        in_specs=[hbm] * 5,
        out_specs=(vmem, vmem, vmem),
        scratch_shapes=[
            pltpu.VMEM((depth, keypoints), bf16),
            pltpu.VMEM((keypoints, depth), bf16),
            pltpu.VMEM((1, 3, keypoints), bf16),
            pltpu.VMEM((keypoints, LANES), f32),
            pltpu.VMEM((8, keypoints), bf16),
            pltpu.VMEM((8, keypoints), bf16),
            pltpu.VMEM((chunks, 1, LANES), f32),
            pltpu.VMEM((1, LANES), i32),
            pltpu.VMEM((n, 1, LANES), i32),
            pltpu.SMEM((n, 1, LANES), i32),
            pltpu.SMEM(counts.shape, i32),
            pltpu.SMEM(owner_slot.shape, i32),
            pltpu.SMEM(pair_list.shape, i32),
            pltpu.VMEM((n, 3, keypoints), bf16),
            pltpu.VMEM((n // 2, 3, keypoints), bf16),
            pltpu.VMEM((3, keypoints), bf16),
            pltpu.VMEM((chunks, keypoints, LANES), f32),
            pltpu.VMEM((chunks, 4, LANES), f32),
            pltpu.VMEM((n, 4, LANES), f32),
            pltpu.VMEM((chunks, 4, LANES), f32),
            pltpu.VMEM((chunks, 4, LANES), f32),
            sems((7 + len(spans),)),
            sems,
            sems,
            sems,
            sems,
            sems((n // 2,)),
            sems,
            *[sems((len(spans),))] * 2,
            *[sems((len(subs),))] * 2,
            sems((n,)),
            sems,
            *[sems((chunks,))] * 2,
            *[sems((len(late),))] * 2,
            *[pltpu.VMEM((n, width, w), bf16) for _, w in spans],
            *[pltpu.VMEM((n, width, w), bf16) for _, _, w in subs] * 2,
            *[pltpu.VMEM((4, w), f32) for w in late],
            *[pltpu.VMEM((n, 4, w), f32) for w in late],
        ],
        compiler_params=pltpu.CompilerParams(collective_id=0, has_side_effects=True),
    )(descriptors, attributes, counts, owner_slot, pair_list)
    return pl.pallas_call(
        put_out,
        out_shape=out_shape,
        in_specs=[vmem] * 3,
        out_specs=(hbm, hbm, hbm),
        scratch_shapes=[sems((3,))],
    )(*[pltpu.with_memory_space_constraint(result, pltpu.VMEM) for result in results])


def solution(mesh):
    n = mesh.shape["img"]

    def shards(descriptors, attributes, counts, owner_slot, pair_list):
        _, depth, keypoints = descriptors.shape
        if n * TILE == depth and n % 4 == 0:
            return one_tile(n, descriptors, attributes, counts, owner_slot, pair_list)
        chunks = keypoints // LANES
        parts = n // chunks
        rounds = min(ROUNDS, depth * chunks // (n * MIN_WIDTH))
        width = depth * chunks // (n * rounds)
        vmem = pl.BlockSpec(memory_space=pltpu.VMEM)
        hbm = pl.BlockSpec(memory_space=pltpu.HBM)
        f32, bf16, i32 = jnp.float32, jnp.bfloat16, jnp.int32
        sems = pltpu.SemaphoreType.DMA
        out_shape = (
            jax.ShapeDtypeStruct((1, 2, keypoints), f32),
            jax.ShapeDtypeStruct((1, keypoints), f32),
            jax.ShapeDtypeStruct((1, 2, keypoints), f32),
        )
        results = pl.pallas_call(
            functools.partial(kernel, n, rounds),
            out_shape=out_shape,
            in_specs=[hbm] * 5,
            out_specs=(vmem, vmem, vmem),
            scratch_shapes=[
                pltpu.VMEM((depth, keypoints), bf16),
                pltpu.VMEM((keypoints, depth), bf16),
                pltpu.VMEM((1, 3, keypoints), bf16),
                pltpu.VMEM((keypoints, LANES), f32),
                pltpu.VMEM((8, keypoints), bf16),
                pltpu.VMEM((8, keypoints), bf16),
                pltpu.VMEM((chunks, 1, LANES), f32),
                pltpu.VMEM((1, LANES), i32),
                pltpu.VMEM((n, 1, LANES), i32),
                pltpu.SMEM((n, 1, LANES), i32),
                pltpu.SMEM(counts.shape, i32),
                pltpu.SMEM(owner_slot.shape, i32),
                pltpu.SMEM(pair_list.shape, i32),
                pltpu.VMEM((n, 3, LANES), bf16),
                pltpu.VMEM((n, 3, LANES), bf16),
                pltpu.VMEM((chunks, 3, LANES), bf16),
                *[pltpu.VMEM((rounds, n, width, LANES), bf16)] * 2,
                pltpu.VMEM((chunks, keypoints, LANES), f32),
                pltpu.VMEM((keypoints, LANES), f32),
                pltpu.VMEM((chunks, 4, LANES), f32),
                pltpu.VMEM((n, 4, LANES), f32),
                pltpu.VMEM((chunks, 4, LANES), f32),
                pltpu.VMEM((chunks, 4, LANES), f32),
                pltpu.VMEM((chunks // rounds, n, 4, LANES), f32),
                sems((7 + rounds,)),
                *[sems((n,))] * 2,
                sems((chunks,)),
                *[sems((n,))] * 2,
                sems((chunks,)),
                *[sems((rounds, n))] * 4,
                *[sems((n,))] * 2,
                *[sems((chunks,))] * 2,
                *[sems((chunks // rounds, n))] * 2,
                *[pltpu.VMEM((n, width, LANES), bf16)] * rounds,
            ],
            compiler_params=pltpu.CompilerParams(
                collective_id=0, has_side_effects=True
            ),
        )(descriptors, attributes, counts, owner_slot, pair_list)
        return pl.pallas_call(
            put_out,
            out_shape=out_shape,
            in_specs=[vmem] * 3,
            out_specs=(hbm, hbm, hbm),
            scratch_shapes=[sems((3,))],
        )(*results)

    placed = (
        P(("groups", "img"), None, None),
        P(("groups", "img"), None, None),
        P("groups"),
        P("groups"),
        P(("groups", "img"), None),
    )
    return jax.shard_map(
        shards,
        mesh=mesh,
        in_specs=placed,
        out_specs=(
            P(("groups", "img"), None, None),
            P(("groups", "img"), None),
            P(("groups", "img"), None, None),
        ),
        check_vma=False,
    )
```

```python
import functools
import math

import jax
import jax.numpy as jnp
from jax import lax
from jax.experimental import pallas as pl
from jax.experimental.pallas import tpu as pltpu
from jax.sharding import PartitionSpec as P

MESH = pl.DeviceIdType.MESH
LANES = 128
ROWS = 256
ROUNDS = 4
MIN_WIDTH = 16
TILE = 16
far_low = -1e30


def split_dot(left, right, contract):
    high = right.astype(jnp.bfloat16)
    low = (right - high.astype(jnp.float32)).astype(jnp.bfloat16)
    dims = (contract, ((), ()))
    return lax.dot_general(left, high, dims, preferred_element_type=jnp.float32) + lax.dot_general(
        left, low, dims, preferred_element_type=jnp.float32
    )


def with_ones(attr):
    ones = jnp.ones((1, attr.shape[1]), jnp.float32)
    rest = jnp.zeros((4, attr.shape[1]), jnp.float32)
    return jnp.concatenate([attr[0:1], ones, attr[1:3], rest], axis=0)


def kernel(
    n, rounds, desc, attr, counts, owner, pairs, match_o, lse_o, xy_o,
    own, own_t, own_attr, row_scale, own_rows, other_rows, other_scale, want_out, want_all, want_s,
    counts_s, owner_s, pairs_s, attr_in, attr_stage, attr_other,
    stage, partner, scores, row_top, stats_out, stats_in, merged_out, merged_in, direct_in,
    local_sem, want_ss, want_rs, attr_ss1, attr_rs1, attr_ss2, attr_rs2, ss1, rs1, ss2, rs2, ss3, rs3, ss4, rs4, ss5, rs5,
    *pieces,
):
    depth, keypoints = desc.shape[1:]
    chunks = keypoints // LANES
    parts = n // chunks
    blocks = keypoints // ROWS
    me = lax.axis_index("img")
    my_chunk = me // parts
    my_part = lax.rem(me, parts)
    round_chunks = chunks // rounds
    round_parts = n // round_chunks
    width = depth // round_parts
    early = chunks - round_chunks

    def peer(step):
        return lax.rem(me + step, n)

    def remote(src, dst, send, recv, to):
        return pltpu.make_async_remote_copy(
            src_ref=src, dst_ref=dst, send_sem=send, recv_sem=recv, device_id={"img": to}, device_id_type=MESH
        )

    def piece_of(r, k):
        row = pl.multiple_of(lax.rem(k, round_parts) * width, width)
        col = pl.multiple_of((r * round_chunks + k // round_parts) * LANES, LANES)
        return desc.at[0, pl.ds(row, width), pl.ds(col, LANES)]

    def attr_piece(c):
        return attr.at[0, :, pl.ds(pl.multiple_of(c * LANES, LANES), LANES)]

    def copy_want(k, source):
        return remote(want_out, want_all.at[source], want_ss.at[k], want_rs.at[source], k)

    def copy_attr_one(c, source):
        return remote(attr_piece(c), attr_in.at[source], attr_ss1.at[c], attr_rs1.at[source], c * parts)

    def copy_attr_two(k, source):
        return remote(attr_stage.at[k], attr_other.at[source], attr_ss2.at[k], attr_rs2.at[source], k)

    def copy_one(r, k, source):
        return remote(piece_of(r, k), pieces[r].at[source], ss1.at[r, k], rs1.at[r, source], k)

    def copy_two(r, k, source):
        return remote(stage.at[r, k], partner.at[r, source], ss2.at[r, k], rs2.at[r, source], k)

    def copy_stats(k, source):
        return remote(stats_out.at[k // parts], stats_in.at[source], ss3.at[k], rs3.at[source], k)

    def copy_merged(q, k, source_chunk):
        return remote(merged_out.at[q], merged_in.at[source_chunk], ss4.at[q], rs4.at[source_chunk], k)

    def copy_direct(i, k, source):
        return remote(stats_out.at[early + i], direct_in.at[i, source], ss5.at[i, k], rs5.at[i, source], k)

    barrier = pltpu.get_barrier_semaphore()

    @pl.loop(1, n)
    def _(step):
        pl.semaphore_signal(barrier, inc=1, device_id={"img": peer(step)}, device_id_type=MESH)

    local_copies = [
        pltpu.make_async_copy(pairs, pairs_s, local_sem.at[0]),
        pltpu.make_async_copy(owner, owner_s, local_sem.at[1]),
        pltpu.make_async_copy(counts, counts_s, local_sem.at[2]),
        pltpu.make_async_copy(attr, own_attr, local_sem.at[3]),
        pltpu.make_async_copy(desc.at[0], own, local_sem.at[4]),
        *[pltpu.make_async_copy(piece_of(r, me), pieces[r].at[me], local_sem.at[7 + r]) for r in range(rounds)],
    ]
    for copy in local_copies:
        copy.start()
    local_attr = pltpu.make_async_copy(attr_piece(my_chunk), attr_in.at[me], local_sem.at[6])

    @pl.when(my_part == 0)
    def _():
        local_attr.start()

    for copy in local_copies[:3]:
        copy.wait()
    want = owner_s[pairs_s[0, 1]]
    count_a = counts_s[pairs_s[0, 0]]
    count_b = counts_s[pairs_s[0, 1]]
    want_row = jnp.full((1, LANES), want, jnp.int32)
    want_out[...] = want_row
    want_all[me] = want_row
    pl.semaphore_wait(barrier, n - 1)

    @pl.loop(1, n)
    def _(step):
        copy_want(peer(step), me).start()

    @pl.loop(0, chunks)
    def _(step):
        c = lax.rem(my_chunk + step, chunks)

        @pl.when(c * parts != me)
        def _():
            copy_attr_one(c, me).start()

    for r in range(rounds):
        @pl.loop(1, n)
        def _(step):
            copy_one(r, peer(step), me).start()

    for copy in local_copies[3:]:
        copy.wait()
    rows8 = with_ones(own_attr[0].astype(jnp.float32))
    own_rows[...] = rows8.astype(jnp.bfloat16)
    row_scale[...] = jnp.broadcast_to(jnp.transpose(rows8)[:, 0:1] * (1.0 / math.sqrt(depth)), (keypoints, LANES))
    for block in range(blocks):
        rows = slice(block * ROWS, (block + 1) * ROWS)
        own_t[rows, :] = jnp.transpose(own[:, rows])
    row_top[...] = jnp.full((keypoints, LANES), far_low, jnp.float32)

    @pl.loop(1, n)
    def _(step):
        k = peer(step)
        copy_want(k, k).wait_recv()

    to_scalars = pltpu.make_async_copy(want_all, want_s, local_sem.at[5])
    to_scalars.start()
    to_scalars.wait()

    @pl.when(my_part == 0)
    def _():
        local_attr.wait()

        @pl.loop(1, n)
        def _(step):
            k = peer(step)
            copy_attr_one(my_chunk, k).wait_recv()

        @pl.loop(1, n)
        def _(step):
            k = peer(step)
            attr_stage[k] = attr_in[want_s[k, 0, 0]]
            copy_attr_two(k, my_chunk).start()

        attr_other[my_chunk] = attr_in[want]

    for r in range(rounds):
        @pl.loop(1, n)
        def _(step):
            k = peer(step)
            copy_one(r, k, k).wait_recv()

        @pl.loop(1, n)
        def _(step):
            k = peer(step)
            stage[r, k] = pieces[r][want_s[k, 0, 0]]
            copy_two(r, k, me).start()

        partner[r, me] = pieces[r][want]

    for chunk in range(chunks):
        cols = slice(chunk * LANES, (chunk + 1) * LANES)

        @pl.when(chunk * parts != me)
        def _():
            copy_attr_two(chunk * parts, chunk).wait_recv()

        other8 = with_ones(attr_other[chunk].astype(jnp.float32))
        other_rows[:, cols] = other8.astype(jnp.bfloat16)
        other_scale[chunk] = other8[0:1]

    row_ix = lax.broadcasted_iota(jnp.int32, (ROWS, LANES), 0)
    lane_ix = lax.broadcasted_iota(jnp.int32, (1, LANES), 1)
    first_row = lax.broadcasted_iota(jnp.int32, (4, LANES), 0) == 0

    def score_chunk(step):
        r = step // round_chunks
        within = lax.rem(me // round_parts + step, round_chunks)
        c = r * round_chunks + within
        for part in range(round_parts):
            k = within * round_parts + part

            @pl.when(k != me)
            def _():
                copy_two(r, k, k).wait_recv()

        block_b = partner[r, pl.ds(within * round_parts, round_parts)].reshape(depth, LANES)
        scale_b = other_scale[c]
        col_valid = c * LANES + lane_ix < count_b
        col_top = jnp.full((1, LANES), far_low, jnp.float32)
        for block in range(blocks):
            rows = slice(block * ROWS, (block + 1) * ROWS)
            raw = jnp.dot(own_t[rows, :], block_b, preferred_element_type=jnp.float32)
            score = raw * row_scale[rows, :] * scale_b
            scores[c, rows, :] = score
            row_top[rows, :] = jnp.maximum(row_top[rows, :], jnp.where(col_valid, score, far_low))
            masked = jnp.where(block * ROWS + row_ix < count_a, score, far_low)
            col_top = jnp.maximum(col_top, jnp.max(masked, axis=0, keepdims=True))
        sums = jnp.zeros((8, LANES), jnp.float32)
        for block in range(blocks):
            rows = slice(block * ROWS, (block + 1) * ROWS)
            weight = jnp.where(block * ROWS + row_ix < count_a, jnp.exp(scores[c, rows, :] - col_top), 0.0)
            sums = sums + split_dot(own_rows[:, rows], weight, ((1,), (0,)))
        stats = jnp.where(first_row, col_top, sums[0:4])
        stats_out[c] = stats
        return c, within, stats

    def merge(slot, partial):
        hit = want_all[...] == slot
        tops = partial[:, 0:1, :]
        peak = jnp.maximum(jnp.max(jnp.where(hit, tops, far_low), axis=0), 0.0)
        fade = jnp.where(hit, jnp.exp(tops - peak[None]), 0.0)
        total = jnp.sum(fade * partial, axis=0)
        partition = jnp.exp(-peak) + total[1:2]
        return jnp.where(first_row, peak + jnp.log(partition), total / partition)

    @pl.loop(0, early)
    def _(step):
        c, _, stats = score_chunk(step)
        for part in range(parts):
            k = c * parts + part

            @pl.when(k != me)
            def _():
                copy_stats(k, me).start()

            @pl.when(k == me)
            def _():
                stats_in[me] = stats

    @pl.loop(early, chunks)
    def _(step):
        _, i, stats = score_chunk(step)
        direct_in[i, me] = stats

        @pl.loop(1, n)
        def _(hop):
            copy_direct(i, peer(hop), me).start()

    @pl.when(my_chunk < early)
    def _():
        @pl.loop(1, n)
        def _(step):
            k = peer(step)
            copy_stats(k, k).wait_recv()

        @pl.loop(0, chunks)
        def _(q):
            slot = my_part * chunks + q
            merged = merge(slot, stats_in[...])
            merged_out[q] = merged

            @pl.when(slot != me)
            def _():
                copy_merged(q, slot, my_chunk).start()

            @pl.when(slot == me)
            def _():
                merged_in[my_chunk] = merged

    for block in range(blocks):
        rows = slice(block * ROWS, (block + 1) * ROWS)
        top = jnp.max(row_top[rows, :], axis=1, keepdims=True)
        sums = jnp.zeros((8, ROWS), jnp.float32)
        for chunk in range(chunks):
            cols = slice(chunk * LANES, (chunk + 1) * LANES)
            weight = jnp.where(chunk * LANES + lane_ix < count_b, jnp.exp(scores[chunk, rows, :] - top), 0.0)
            sums = sums + split_dot(other_rows[:, cols], weight, ((1,), (1,)))
        row_valid = block * ROWS + lax.broadcasted_iota(jnp.int32, (2, ROWS), 1) < count_a
        match_o[0, :, rows] = jnp.where(row_valid, sums[2:4] / sums[1:2], 0.0)

    def write(chunk, result):
        cols = slice(chunk * LANES, (chunk + 1) * LANES)
        lse_o[:, cols] = result[0:1]
        xy_o[0, :, cols] = result[2:4]

    for i in range(round_chunks):
        @pl.loop(1, n)
        def _(step):
            k = peer(step)
            copy_direct(i, k, k).wait_recv()

        write(early + i, merge(me, direct_in[i]))

    home_part = me // chunks
    for chunk in range(early):
        k = chunk * parts + home_part

        @pl.when(k != me)
        def _():
            copy_merged(chunk, k, chunk).wait_recv()

        write(chunk, merged_in[chunk])

    @pl.loop(1, n)
    def _(step):
        k = peer(step)
        copy_want(k, me).wait_send()
        for r in range(rounds):
            copy_one(r, k, me).wait_send()
            copy_two(r, k, me).wait_send()
        for i in range(round_chunks):
            copy_direct(i, k, me).wait_send()

        @pl.when(k // parts < early)
        def _():
            copy_stats(k, me).wait_send()

    @pl.when(my_chunk < early)
    def _():
        @pl.loop(0, chunks)
        def _(q):
            slot = my_part * chunks + q

            @pl.when(slot != me)
            def _():
                copy_merged(q, slot, my_chunk).wait_send()

    @pl.loop(0, chunks)
    def _(c):
        @pl.when(c * parts != me)
        def _():
            copy_attr_one(c, me).wait_send()

    @pl.when(my_part == 0)
    def _():
        @pl.loop(1, n)
        def _(step):
            copy_attr_two(peer(step), my_chunk).wait_send()


def put_out(match, lse, xy, match_o, lse_o, xy_o, sem):
    copies = [
        pltpu.make_async_copy(match, match_o, sem.at[0]),
        pltpu.make_async_copy(lse, lse_o, sem.at[1]),
        pltpu.make_async_copy(xy, xy_o, sem.at[2]),
    ]
    for copy in copies:
        copy.start()
    for copy in copies:
        copy.wait()


SPLIT = 6
MERGED_SUBS = 1


def plan(keypoints):
    eighth = keypoints // 8
    spans = ((0, SPLIT * eighth), (SPLIT * eighth, (8 - SPLIT) * eighth))
    subs = ((0, 4 * eighth), (4 * eighth, 2 * eighth), (6 * eighth, 2 * eighth))
    return spans, subs


def tile_kernel(
    n, desc, attr, counts, owner, pairs, match_o, lse_o, xy_o,
    own, own_t, own_attr, row_scale, own_rows, other_rows, other_scale, want_out, want_all, want_s,
    counts_s, owner_s, pairs_s, attr_all, attr_stage, attr_other,
    scores, stats_out, stats_in, merged_out, merged_in,
    local_sem, want_ss, want_rs, attr_ss1, attr_rs1, attr_ss2, attr_rs2,
    ss1, rs1, ss2, rs2, ss3, rs3, ss4, rs4, ss5, rs5, *buffers,
):
    depth, keypoints = desc.shape[1:]
    spans, subs = plan(keypoints)
    pieces = buffers[: len(spans)]
    stage = buffers[len(spans) : len(spans) + len(subs)]
    partner = buffers[len(spans) + len(subs) : len(spans) + 2 * len(subs)]
    late = MERGED_SUBS
    direct_out = buffers[len(spans) + 2 * len(subs) : len(spans) + 3 * len(subs) - late]
    direct_in = buffers[len(spans) + 3 * len(subs) - late :]
    width = depth // n
    chunks = keypoints // LANES
    parts = n // chunks
    blocks = keypoints // ROWS
    early = sum(w for _, w in subs[:MERGED_SUBS]) // LANES
    team = n // 4
    me = lax.axis_index("img")
    my_chunk = lax.rem(me, chunks)
    my_part = me // chunks

    seat = lax.rem(me, team)
    my_row = me // team
    upper = my_row // 2
    lower = 1 - upper
    half = n // 2
    leads = half - team, half
    lead = lower * leads[0] + upper * leads[1]

    def each_in(rows, first, gap, act):
        @pl.loop(0, rows * team)
        def _(step):
            i = step // team
            row = lower * (rows - 1 - i) + upper * i
            k = (first + gap * row) * team + lax.rem(seat + step, team)

            @pl.when(k != me)
            def _():
                act(k)

    def each_peer(act):
        each_in(4, 0, 1, act)

    def each_of(first, last, act):
        @pl.loop(first, last)
        def _(k):
            @pl.when(k != me)
            def _():
                act(k)

    def each_inner(act):
        each_in(2, 1, 1, act)

    def each_outer(act):
        each_in(2, 0, 3, act)

    def remote(src, dst, send, recv, to):
        return pltpu.make_async_remote_copy(
            src_ref=src, dst_ref=dst, send_sem=send, recv_sem=recv, device_id={"img": to}, device_id_type=MESH
        )

    def drain(like, sem):
        pltpu.make_async_copy(like, like, sem).wait()

    def others(buffer):
        return buffer.at[pl.ds(0, n - 1)]

    def piece_of(r, k):
        first, w = spans[r]
        return desc.at[0, pl.ds(pl.multiple_of(k * width, width), width), pl.ds(first, w)]

    def copy_want(k):
        return remote(want_out, want_all.at[me], want_ss, want_rs, k)

    def copy_attr_one(k):
        return remote(attr.at[0], attr_all.at[me], attr_ss1, attr_rs1, k)

    def copy_attr_two(j, k):
        return remote(attr_stage.at[j], attr_other, attr_ss2.at[j], attr_rs2, k)

    def copy_one(r, k):
        return remote(piece_of(r, k), pieces[r].at[me], ss1.at[r], rs1.at[r], k)

    def copy_two(u, k):
        return remote(stage[u].at[k], partner[u].at[me], ss2.at[u], rs2.at[u], k)

    def copy_stats(c, k):
        return remote(stats_out.at[c], stats_in.at[me], ss3.at[k], rs3, k)

    def copy_merged(q, k, source_chunk):
        return remote(merged_out.at[q], merged_in.at[source_chunk], ss4.at[q], rs4.at[source_chunk], k)

    def copy_direct(i, k):
        return remote(direct_out[i], direct_in[i].at[me], ss5.at[i], rs5.at[i], k)

    barrier = pltpu.get_barrier_semaphore()

    inner = jnp.logical_or(my_row == 1, my_row == 2)

    def tell(k):
        pl.semaphore_signal(barrier, inc=1, device_id={"img": k}, device_id_type=MESH)

    @pl.when(inner)
    def _():
        each_inner(tell)

    local_copies = [
        pltpu.make_async_copy(pairs, pairs_s, local_sem.at[0]),
        pltpu.make_async_copy(owner, owner_s, local_sem.at[1]),
        pltpu.make_async_copy(counts, counts_s, local_sem.at[2]),
        pltpu.make_async_copy(attr, own_attr, local_sem.at[3]),
        pltpu.make_async_copy(desc.at[0], own, local_sem.at[4]),
        pltpu.make_async_copy(attr.at[0], attr_all.at[me], local_sem.at[6]),
        *[pltpu.make_async_copy(piece_of(r, me), pieces[r].at[me], local_sem.at[7 + r]) for r in range(len(spans))],
    ]
    for copy in local_copies:
        copy.start()

    for copy in local_copies[:3]:
        copy.wait()
    want = owner_s[pairs_s[0, 1]]
    count_a = counts_s[pairs_s[0, 0]]
    count_b = counts_s[pairs_s[0, 1]]
    want_row = jnp.full((1, LANES), want, jnp.int32)
    want_out[...] = want_row
    want_all[me] = want_row

    def send_attr():
        for k in leads:
            @pl.when(me != k)
            def _():
                copy_attr_one(k).start()

    @pl.when(inner)
    def _():
        pl.semaphore_wait(barrier, 2 * team - 1)
        each_outer(tell)
        each_inner(lambda k: copy_want(k).start())
        each_inner(lambda k: copy_one(0, k).start())
        pl.semaphore_wait(barrier, 2 * team)
        each_outer(tell)
        each_outer(lambda k: copy_want(k).start())
        each_outer(lambda k: copy_one(0, k).start())

    @pl.when(jnp.logical_not(inner))
    def _():
        pl.semaphore_wait(barrier, 2 * team)
        each_inner(tell)
        each_inner(lambda k: copy_want(k).start())
        each_inner(lambda k: copy_one(0, k).start())
        pl.semaphore_wait(barrier, 2 * team)
        each_outer(lambda k: copy_want(k).start())
        each_outer(lambda k: copy_one(0, k).start())


    send_attr()
    each_peer(lambda k: copy_one(1, k).start())

    for copy in local_copies[3:]:
        copy.wait()
    rows8 = with_ones(own_attr[0].astype(jnp.float32))
    own_rows[...] = rows8.astype(jnp.bfloat16)
    row_scale[...] = jnp.broadcast_to(jnp.transpose(rows8)[:, 0:1] * (1.0 / math.sqrt(depth)), (keypoints, LANES))
    for block in range(blocks):
        rows = slice(block * ROWS, (block + 1) * ROWS)
        own_t[rows, :] = jnp.transpose(own[:, rows])

    drain(others(want_all), want_rs)
    to_scalars = pltpu.make_async_copy(want_all, want_s, local_sem.at[5])
    to_scalars.start()
    to_scalars.wait()

    def pick(u, index, put):
        start, w = subs[u]
        for r, (first, span) in enumerate(spans):
            low, high = max(start, first), min(start + w, first + span)
            if low < high:
                put(slice(low - start, high - start), pieces[r][index, :, low - first : high - first])

    def forward(u):
        def send(k):
            def put(cols, value):
                stage[u][k, :, cols] = value

            pick(u, want_s[k, 0, 0], put)
            copy_two(u, k).start()

        each_peer(send)

        def keep(cols, value):
            partner[u][me, :, cols] = value

        pick(u, want, keep)

    drain(others(pieces[0]), rs1.at[0])
    forward(0)

    @pl.when(jnp.logical_not(inner))
    def _():
        forward(1)

    @pl.when(me == lead)
    def _():
        drain(others(attr_all), attr_rs1)

        @pl.loop(0, half)
        def _(j):
            k = upper * half + j

            @pl.when(k != me)
            def _():
                attr_stage[j] = attr_all[want_s[k, 0, 0]]
                copy_attr_two(j, k).start()

        attr_other[...] = attr_all[want]


    drain(others(pieces[1]), rs1.at[1])

    @pl.when(inner)
    def _():
        forward(1)

    forward(2)

    @pl.when(me != lead)
    def _():
        drain(attr_other, attr_rs2)

    other8 = with_ones(attr_other[...].astype(jnp.float32))
    other_rows[...] = other8.astype(jnp.bfloat16)
    for chunk in range(chunks):
        other_scale[chunk] = other8[0:1, chunk * LANES : (chunk + 1) * LANES]

    lane_ix = lax.broadcasted_iota(jnp.int32, (1, LANES), 1)
    first_row = lax.broadcasted_iota(jnp.int32, (4, LANES), 0) == 0

    def score(u, first_chunk):
        w = subs[u][1]
        narrow = w == 2 * LANES
        tall = ROWS if w == LANES else ROWS // 2
        spot = range(keypoints // tall)
        row_ix = lax.broadcasted_iota(jnp.int32, (tall, LANES), 0)
        lanes = [slice(i * LANES, (i + 1) * LANES) for i in range(w // LANES)]
        block_b = partner[u][...].reshape(depth, w)
        block_tops, block_sums = [], []
        for block in spot:
            rows = slice(block * tall, (block + 1) * tall)
            raw = jnp.dot(own_t[rows, :], block_b, preferred_element_type=jnp.float32)
            valid = block * tall + row_ix < count_a
            tops, weight = [], []
            for i, cols in enumerate(lanes):
                scaled = raw[:, cols] * row_scale[rows, :] * other_scale[first_chunk + i]
                masked = jnp.where(valid, scaled, far_low)
                scores[first_chunk + i, rows, :] = masked
                if narrow:
                    tops.append(jnp.max(masked, axis=0, keepdims=True))
                    weight.append(jnp.exp(masked - tops[i]))
                else:
                    tops.append(jnp.max(masked.reshape(tall // 8, 8, LANES), axis=0))
            block_tops.append(tops)
            if narrow:
                block_sums.append(split_dot(own_rows[:, rows], jnp.concatenate(weight, axis=1), ((1,), (0,))))
        tops = [functools.reduce(jnp.maximum, [found[i] for found in block_tops]) for i in range(len(lanes))]
        if narrow:
            sums = [
                sum(block_sums[block][:, cols] * jnp.exp(block_tops[block][i] - tops[i]) for block in spot)
                for i, cols in enumerate(lanes)
            ]
            return [jnp.where(first_row, top, total[0:4]) for top, total in zip(tops, sums)]
        tops = [jnp.max(top, axis=0, keepdims=True) for top in tops]
        sums = [jnp.zeros((8, LANES), jnp.float32) for _ in lanes]
        for block in spot:
            rows = slice(block * tall, (block + 1) * tall)
            weight = [jnp.exp(scores[first_chunk + i, rows, :] - top) for i, top in enumerate(tops)]
            part = split_dot(own_rows[:, rows], jnp.concatenate(weight, axis=1), ((1,), (0,)))
            sums = [total + part[:, cols] for total, cols in zip(sums, lanes)]
        return [jnp.where(first_row, top, total[0:4]) for top, total in zip(tops, sums)]

    def merge(slot, partial):
        hit = want_all[...] == slot
        tops = partial[:, 0:1, :]
        peak = jnp.maximum(jnp.max(jnp.where(hit, tops, far_low), axis=0), 0.0)
        fade = jnp.where(hit, jnp.exp(tops - peak[None]), 0.0)
        total = jnp.sum(fade * partial, axis=0)
        partition = jnp.exp(-peak) + total[1:2]
        return jnp.where(first_row, peak + jnp.log(partition), total / partition)

    for u in range(len(subs)):
        base = subs[u][0] // LANES
        drain(others(partner[u]), rs2.at[u])
        for i, stats in enumerate(score(u, base)):
            c = base + i
            if u < late:
                stats_out[c] = stats
                for part in range(parts):
                    k = part * chunks + c

                    @pl.when(k != me)
                    def _():
                        copy_stats(c, k).start()

                    @pl.when(k == me)
                    def _():
                        stats_in[me] = stats
            else:
                cols = slice(i * LANES, (i + 1) * LANES)
                direct_out[u - late][:, cols] = stats
                direct_in[u - late][me, :, cols] = stats
        if u >= late:
            each_of(0, team, lambda k: copy_direct(u - late, k).start())

    def send_rest(k):
        for i in range(len(subs) - late):
            copy_direct(i, k).start()

    each_of(team, n, send_rest)


    def row_block(block):
        rows = slice(block * ROWS, (block + 1) * ROWS)
        top = jnp.full((ROWS, LANES), far_low, jnp.float32)
        for chunk in range(chunks):
            top = jnp.maximum(top, jnp.where(chunk * LANES + lane_ix < count_b, scores[chunk, rows, :], far_low))
        top = jnp.max(top, axis=1, keepdims=True)
        sums = jnp.zeros((8, ROWS), jnp.float32)
        for chunk in range(chunks):
            cols = slice(chunk * LANES, (chunk + 1) * LANES)
            weight = jnp.where(chunk * LANES + lane_ix < count_b, jnp.exp(scores[chunk, rows, :] - top), 0.0)
            sums = sums + split_dot(other_rows[:, cols], weight, ((1,), (1,)))
        row_valid = block * ROWS + lax.broadcasted_iota(jnp.int32, (2, ROWS), 1) < count_a
        match_o[0, :, rows] = jnp.where(row_valid, sums[2:4] / sums[1:2], 0.0)

    row_block(0)
    row_block(1)

    @pl.when(my_chunk < early)
    def _():
        drain(others(stats_in), rs3)

        @pl.loop(0, chunks)
        def _(q):
            slot = my_part * chunks + q
            merged = merge(slot, stats_in[...])
            merged_out[q] = merged

            @pl.when(slot != me)
            def _():
                copy_merged(q, slot, my_chunk).start()

            @pl.when(slot == me)
            def _():
                merged_in[my_chunk] = merged

    for block in range(2, blocks):
        row_block(block)

    def write(chunk, result):
        cols = slice(chunk * LANES, (chunk + 1) * LANES)
        lse_o[:, cols] = result[0:1]
        xy_o[0, :, cols] = result[2:4]

    drain(others(want_all), want_ss)
    for r in range(len(spans)):
        drain(others(pieces[r]), ss1.at[r])
    for u in range(len(subs)):
        drain(others(partner[u]), ss2.at[u])

    for k in leads:
        @pl.when(me != k)
        def _():
            drain(attr_other, attr_ss1)

    @pl.when(me == lead)
    def _():
        @pl.loop(0, half)
        def _(j):
            k = upper * half + j

            @pl.when(k != me)
            def _():
                copy_attr_two(j, k).wait_send()

    for part in range(parts):
        @pl.loop(0, early)
        def _(c):
            k = part * chunks + c

            @pl.when(k != me)
            def _():
                copy_stats(c, k).wait_send()

    for i in range(len(subs) - late):
        drain(others(direct_in[i]), ss5.at[i])

    @pl.when(my_chunk < early)
    def _():
        @pl.loop(0, chunks)
        def _(q):
            slot = my_part * chunks + q

            @pl.when(slot != me)
            def _():
                copy_merged(q, slot, my_chunk).wait_send()

    for chunk in range(early):
        k = my_part * chunks + chunk

        @pl.when(k != me)
        def _():
            copy_merged(0, k, chunk).wait_recv()

        write(chunk, merged_in[chunk])

    for u in range(late, len(subs)):
        i = u - late
        drain(others(direct_in[i]), rs5.at[i])
        for j in range(subs[u][1] // LANES):
            part = direct_in[i][:, :, j * LANES : (j + 1) * LANES]
            write(subs[u][0] // LANES + j, merge(me, part))


def one_tile(n, descriptors, attributes, counts, owner_slot, pair_list):
    _, depth, keypoints = descriptors.shape
    chunks = keypoints // LANES
    spans, subs = plan(keypoints)
    width = depth // n
    late = [w for _, w in subs[MERGED_SUBS:]]
    vmem = pl.BlockSpec(memory_space=pltpu.VMEM)
    hbm = pl.BlockSpec(memory_space=pltpu.HBM)
    f32, bf16, i32 = jnp.float32, jnp.bfloat16, jnp.int32
    sems = pltpu.SemaphoreType.DMA
    shapes = (1, 2, keypoints), (1, keypoints), (1, 2, keypoints)
    out_shape = tuple(jax.ShapeDtypeStruct(shape, f32) for shape in shapes)
    results = pl.pallas_call(
        functools.partial(tile_kernel, n),
        out_shape=tuple(pltpu.VMEM(shape, f32) for shape in shapes),
        in_specs=[hbm] * 5,
        out_specs=(vmem, vmem, vmem),
        scratch_shapes=[
            pltpu.VMEM((depth, keypoints), bf16),
            pltpu.VMEM((keypoints, depth), bf16),
            pltpu.VMEM((1, 3, keypoints), bf16),
            pltpu.VMEM((keypoints, LANES), f32),
            pltpu.VMEM((8, keypoints), bf16),
            pltpu.VMEM((8, keypoints), bf16),
            pltpu.VMEM((chunks, 1, LANES), f32),
            pltpu.VMEM((1, LANES), i32),
            pltpu.VMEM((n, 1, LANES), i32),
            pltpu.SMEM((n, 1, LANES), i32),
            pltpu.SMEM(counts.shape, i32),
            pltpu.SMEM(owner_slot.shape, i32),
            pltpu.SMEM(pair_list.shape, i32),
            pltpu.VMEM((n, 3, keypoints), bf16),
            pltpu.VMEM((n // 2, 3, keypoints), bf16),
            pltpu.VMEM((3, keypoints), bf16),
            pltpu.VMEM((chunks, keypoints, LANES), f32),
            pltpu.VMEM((chunks, 4, LANES), f32),
            pltpu.VMEM((n, 4, LANES), f32),
            pltpu.VMEM((chunks, 4, LANES), f32),
            pltpu.VMEM((chunks, 4, LANES), f32),
            sems((7 + len(spans),)),
            sems,
            sems,
            sems,
            sems,
            sems((n // 2,)),
            sems,
            *[sems((len(spans),))] * 2,
            *[sems((len(subs),))] * 2,
            sems((n,)),
            sems,
            *[sems((chunks,))] * 2,
            *[sems((len(late),))] * 2,
            *[pltpu.VMEM((n, width, w), bf16) for _, w in spans],
            *[pltpu.VMEM((n, width, w), bf16) for _, w in subs] * 2,
            *[pltpu.VMEM((4, w), f32) for w in late],
            *[pltpu.VMEM((n, 4, w), f32) for w in late],
        ],
        compiler_params=pltpu.CompilerParams(collective_id=0, has_side_effects=True),
    )(descriptors, attributes, counts, owner_slot, pair_list)
    return pl.pallas_call(
        put_out,
        out_shape=out_shape,
        in_specs=[vmem] * 3,
        out_specs=(hbm, hbm, hbm),
        scratch_shapes=[sems((3,))],
    )(*[pltpu.with_memory_space_constraint(result, pltpu.VMEM) for result in results])


def solution(mesh):
    n = mesh.shape["img"]

    def shards(descriptors, attributes, counts, owner_slot, pair_list):
        _, depth, keypoints = descriptors.shape
        if n * TILE == depth and n % 4 == 0:
            return one_tile(n, descriptors, attributes, counts, owner_slot, pair_list)
        chunks = keypoints // LANES
        parts = n // chunks
        rounds = min(ROUNDS, depth * chunks // (n * MIN_WIDTH))
        width = depth * chunks // (n * rounds)
        vmem = pl.BlockSpec(memory_space=pltpu.VMEM)
        hbm = pl.BlockSpec(memory_space=pltpu.HBM)
        f32, bf16, i32 = jnp.float32, jnp.bfloat16, jnp.int32
        sems = pltpu.SemaphoreType.DMA
        out_shape = (
            jax.ShapeDtypeStruct((1, 2, keypoints), f32),
            jax.ShapeDtypeStruct((1, keypoints), f32),
            jax.ShapeDtypeStruct((1, 2, keypoints), f32),
        )
        results = pl.pallas_call(
            functools.partial(kernel, n, rounds),
            out_shape=out_shape,
            in_specs=[hbm] * 5,
            out_specs=(vmem, vmem, vmem),
            scratch_shapes=[
                pltpu.VMEM((depth, keypoints), bf16),
                pltpu.VMEM((keypoints, depth), bf16),
                pltpu.VMEM((1, 3, keypoints), bf16),
                pltpu.VMEM((keypoints, LANES), f32),
                pltpu.VMEM((8, keypoints), bf16),
                pltpu.VMEM((8, keypoints), bf16),
                pltpu.VMEM((chunks, 1, LANES), f32),
                pltpu.VMEM((1, LANES), i32),
                pltpu.VMEM((n, 1, LANES), i32),
                pltpu.SMEM((n, 1, LANES), i32),
                pltpu.SMEM(counts.shape, i32),
                pltpu.SMEM(owner_slot.shape, i32),
                pltpu.SMEM(pair_list.shape, i32),
                pltpu.VMEM((n, 3, LANES), bf16),
                pltpu.VMEM((n, 3, LANES), bf16),
                pltpu.VMEM((chunks, 3, LANES), bf16),
                *[pltpu.VMEM((rounds, n, width, LANES), bf16)] * 2,
                pltpu.VMEM((chunks, keypoints, LANES), f32),
                pltpu.VMEM((keypoints, LANES), f32),
                pltpu.VMEM((chunks, 4, LANES), f32),
                pltpu.VMEM((n, 4, LANES), f32),
                pltpu.VMEM((chunks, 4, LANES), f32),
                pltpu.VMEM((chunks, 4, LANES), f32),
                pltpu.VMEM((chunks // rounds, n, 4, LANES), f32),
                sems((7 + rounds,)),
                *[sems((n,))] * 2,
                sems((chunks,)),
                *[sems((n,))] * 2,
                sems((chunks,)),
                *[sems((rounds, n))] * 4,
                *[sems((n,))] * 2,
                *[sems((chunks,))] * 2,
                *[sems((chunks // rounds, n))] * 2,
                *[pltpu.VMEM((n, width, LANES), bf16)] * rounds,
            ],
            compiler_params=pltpu.CompilerParams(
                collective_id=0, has_side_effects=True
            ),
        )(descriptors, attributes, counts, owner_slot, pair_list)
        return pl.pallas_call(
            put_out,
            out_shape=out_shape,
            in_specs=[vmem] * 3,
            out_specs=(hbm, hbm, hbm),
            scratch_shapes=[sems((3,))],
        )(*results)

    placed = (
        P(("groups", "img"), None, None),
        P(("groups", "img"), None, None),
        P("groups"),
        P("groups"),
        P(("groups", "img"), None),
    )
    return jax.shard_map(
        shards,
        mesh=mesh,
        in_specs=placed,
        out_specs=(
            P(("groups", "img"), None, None),
            P(("groups", "img"), None),
            P(("groups", "img"), None, None),
        ),
        check_vma=False,
    )
```

```python
import functools
import math

import jax
import jax.numpy as jnp
from jax import lax
from jax.experimental import pallas as pl
from jax.experimental.pallas import tpu as pltpu
from jax.sharding import PartitionSpec as P

MESH = pl.DeviceIdType.MESH
LANES = 128
ROWS = 256
ROUNDS = 4
MIN_WIDTH = 16
TILE = 16
far_low = -1e30


def split_dot(left, right, contract):
    high = right.astype(jnp.bfloat16)
    low = (right - high.astype(jnp.float32)).astype(jnp.bfloat16)
    dims = (contract, ((), ()))
    return lax.dot_general(left, high, dims, preferred_element_type=jnp.float32) + lax.dot_general(
        left, low, dims, preferred_element_type=jnp.float32
    )


def with_ones(attr):
    ones = jnp.ones((1, attr.shape[1]), jnp.float32)
    rest = jnp.zeros((4, attr.shape[1]), jnp.float32)
    return jnp.concatenate([attr[0:1], ones, attr[1:3], rest], axis=0)


def kernel(
    n, rounds, desc, attr, counts, owner, pairs, match_o, lse_o, xy_o,
    own, own_t, own_attr, row_scale, own_rows, other_rows, other_scale, want_out, want_all, want_s,
    counts_s, owner_s, pairs_s, attr_in, attr_stage, attr_other,
    stage, partner, scores, row_top, stats_out, stats_in, merged_out, merged_in, direct_in,
    local_sem, want_ss, want_rs, attr_ss1, attr_rs1, attr_ss2, attr_rs2, ss1, rs1, ss2, rs2, ss3, rs3, ss4, rs4, ss5, rs5,
    *pieces,
):
    depth, keypoints = desc.shape[1:]
    chunks = keypoints // LANES
    parts = n // chunks
    blocks = keypoints // ROWS
    me = lax.axis_index("img")
    my_chunk = me // parts
    my_part = lax.rem(me, parts)
    round_chunks = chunks // rounds
    round_parts = n // round_chunks
    width = depth // round_parts
    early = chunks - round_chunks

    def peer(step):
        return lax.rem(me + step, n)

    def remote(src, dst, send, recv, to):
        return pltpu.make_async_remote_copy(
            src_ref=src, dst_ref=dst, send_sem=send, recv_sem=recv, device_id={"img": to}, device_id_type=MESH
        )

    def piece_of(r, k):
        row = pl.multiple_of(lax.rem(k, round_parts) * width, width)
        col = pl.multiple_of((r * round_chunks + k // round_parts) * LANES, LANES)
        return desc.at[0, pl.ds(row, width), pl.ds(col, LANES)]

    def attr_piece(c):
        return attr.at[0, :, pl.ds(pl.multiple_of(c * LANES, LANES), LANES)]

    def copy_want(k, source):
        return remote(want_out, want_all.at[source], want_ss.at[k], want_rs.at[source], k)

    def copy_attr_one(c, source):
        return remote(attr_piece(c), attr_in.at[source], attr_ss1.at[c], attr_rs1.at[source], c * parts)

    def copy_attr_two(k, source):
        return remote(attr_stage.at[k], attr_other.at[source], attr_ss2.at[k], attr_rs2.at[source], k)

    def copy_one(r, k, source):
        return remote(piece_of(r, k), pieces[r].at[source], ss1.at[r, k], rs1.at[r, source], k)

    def copy_two(r, k, source):
        return remote(stage.at[r, k], partner.at[r, source], ss2.at[r, k], rs2.at[r, source], k)

    def copy_stats(k, source):
        return remote(stats_out.at[k // parts], stats_in.at[source], ss3.at[k], rs3.at[source], k)

    def copy_merged(q, k, source_chunk):
        return remote(merged_out.at[q], merged_in.at[source_chunk], ss4.at[q], rs4.at[source_chunk], k)

    def copy_direct(i, k, source):
        return remote(stats_out.at[early + i], direct_in.at[i, source], ss5.at[i, k], rs5.at[i, source], k)

    barrier = pltpu.get_barrier_semaphore()

    @pl.loop(1, n)
    def _(step):
        pl.semaphore_signal(barrier, inc=1, device_id={"img": peer(step)}, device_id_type=MESH)

    local_copies = [
        pltpu.make_async_copy(pairs, pairs_s, local_sem.at[0]),
        pltpu.make_async_copy(owner, owner_s, local_sem.at[1]),
        pltpu.make_async_copy(counts, counts_s, local_sem.at[2]),
        pltpu.make_async_copy(attr, own_attr, local_sem.at[3]),
        pltpu.make_async_copy(desc.at[0], own, local_sem.at[4]),
        *[pltpu.make_async_copy(piece_of(r, me), pieces[r].at[me], local_sem.at[7 + r]) for r in range(rounds)],
    ]
    for copy in local_copies:
        copy.start()
    local_attr = pltpu.make_async_copy(attr_piece(my_chunk), attr_in.at[me], local_sem.at[6])

    @pl.when(my_part == 0)
    def _():
        local_attr.start()

    for copy in local_copies[:3]:
        copy.wait()
    want = owner_s[pairs_s[0, 1]]
    count_a = counts_s[pairs_s[0, 0]]
    count_b = counts_s[pairs_s[0, 1]]
    want_row = jnp.full((1, LANES), want, jnp.int32)
    want_out[...] = want_row
    want_all[me] = want_row
    pl.semaphore_wait(barrier, n - 1)

    @pl.loop(1, n)
    def _(step):
        copy_want(peer(step), me).start()

    @pl.loop(0, chunks)
    def _(step):
        c = lax.rem(my_chunk + step, chunks)

        @pl.when(c * parts != me)
        def _():
            copy_attr_one(c, me).start()

    for r in range(rounds):
        @pl.loop(1, n)
        def _(step):
            copy_one(r, peer(step), me).start()

    for copy in local_copies[3:]:
        copy.wait()
    rows8 = with_ones(own_attr[0].astype(jnp.float32))
    own_rows[...] = rows8.astype(jnp.bfloat16)
    row_scale[...] = jnp.broadcast_to(jnp.transpose(rows8)[:, 0:1] * (1.0 / math.sqrt(depth)), (keypoints, LANES))
    for block in range(blocks):
        rows = slice(block * ROWS, (block + 1) * ROWS)
        own_t[rows, :] = jnp.transpose(own[:, rows])
    row_top[...] = jnp.full((keypoints, LANES), far_low, jnp.float32)

    @pl.loop(1, n)
    def _(step):
        k = peer(step)
        copy_want(k, k).wait_recv()

    to_scalars = pltpu.make_async_copy(want_all, want_s, local_sem.at[5])
    to_scalars.start()
    to_scalars.wait()

    @pl.when(my_part == 0)
    def _():
        local_attr.wait()

        @pl.loop(1, n)
        def _(step):
            k = peer(step)
            copy_attr_one(my_chunk, k).wait_recv()

        @pl.loop(1, n)
        def _(step):
            k = peer(step)
            attr_stage[k] = attr_in[want_s[k, 0, 0]]
            copy_attr_two(k, my_chunk).start()

        attr_other[my_chunk] = attr_in[want]

    for r in range(rounds):
        @pl.loop(1, n)
        def _(step):
            k = peer(step)
            copy_one(r, k, k).wait_recv()

        @pl.loop(1, n)
        def _(step):
            k = peer(step)
            stage[r, k] = pieces[r][want_s[k, 0, 0]]
            copy_two(r, k, me).start()

        partner[r, me] = pieces[r][want]

    for chunk in range(chunks):
        cols = slice(chunk * LANES, (chunk + 1) * LANES)

        @pl.when(chunk * parts != me)
        def _():
            copy_attr_two(chunk * parts, chunk).wait_recv()

        other8 = with_ones(attr_other[chunk].astype(jnp.float32))
        other_rows[:, cols] = other8.astype(jnp.bfloat16)
        other_scale[chunk] = other8[0:1]

    row_ix = lax.broadcasted_iota(jnp.int32, (ROWS, LANES), 0)
    lane_ix = lax.broadcasted_iota(jnp.int32, (1, LANES), 1)
    first_row = lax.broadcasted_iota(jnp.int32, (4, LANES), 0) == 0

    def score_chunk(step):
        r = step // round_chunks
        within = lax.rem(me // round_parts + step, round_chunks)
        c = r * round_chunks + within
        for part in range(round_parts):
            k = within * round_parts + part

            @pl.when(k != me)
            def _():
                copy_two(r, k, k).wait_recv()

        block_b = partner[r, pl.ds(within * round_parts, round_parts)].reshape(depth, LANES)
        scale_b = other_scale[c]
        col_valid = c * LANES + lane_ix < count_b
        col_top = jnp.full((1, LANES), far_low, jnp.float32)
        for block in range(blocks):
            rows = slice(block * ROWS, (block + 1) * ROWS)
            raw = jnp.dot(own_t[rows, :], block_b, preferred_element_type=jnp.float32)
            score = raw * row_scale[rows, :] * scale_b
            scores[c, rows, :] = score
            row_top[rows, :] = jnp.maximum(row_top[rows, :], jnp.where(col_valid, score, far_low))
            masked = jnp.where(block * ROWS + row_ix < count_a, score, far_low)
            col_top = jnp.maximum(col_top, jnp.max(masked, axis=0, keepdims=True))
        sums = jnp.zeros((8, LANES), jnp.float32)
        for block in range(blocks):
            rows = slice(block * ROWS, (block + 1) * ROWS)
            weight = jnp.where(block * ROWS + row_ix < count_a, jnp.exp(scores[c, rows, :] - col_top), 0.0)
            sums = sums + split_dot(own_rows[:, rows], weight, ((1,), (0,)))
        stats = jnp.where(first_row, col_top, sums[0:4])
        stats_out[c] = stats
        return c, within, stats

    def merge(slot, partial):
        hit = want_all[...] == slot
        tops = partial[:, 0:1, :]
        peak = jnp.maximum(jnp.max(jnp.where(hit, tops, far_low), axis=0), 0.0)
        fade = jnp.where(hit, jnp.exp(tops - peak[None]), 0.0)
        total = jnp.sum(fade * partial, axis=0)
        partition = jnp.exp(-peak) + total[1:2]
        return jnp.where(first_row, peak + jnp.log(partition), total / partition)

    @pl.loop(0, early)
    def _(step):
        c, _, stats = score_chunk(step)
        for part in range(parts):
            k = c * parts + part

            @pl.when(k != me)
            def _():
                copy_stats(k, me).start()

            @pl.when(k == me)
            def _():
                stats_in[me] = stats

    @pl.loop(early, chunks)
    def _(step):
        _, i, stats = score_chunk(step)
        direct_in[i, me] = stats

        @pl.loop(1, n)
        def _(hop):
            copy_direct(i, peer(hop), me).start()

    @pl.when(my_chunk < early)
    def _():
        @pl.loop(1, n)
        def _(step):
            k = peer(step)
            copy_stats(k, k).wait_recv()

        @pl.loop(0, chunks)
        def _(q):
            slot = my_part * chunks + q
            merged = merge(slot, stats_in[...])
            merged_out[q] = merged

            @pl.when(slot != me)
            def _():
                copy_merged(q, slot, my_chunk).start()

            @pl.when(slot == me)
            def _():
                merged_in[my_chunk] = merged

    for block in range(blocks):
        rows = slice(block * ROWS, (block + 1) * ROWS)
        top = jnp.max(row_top[rows, :], axis=1, keepdims=True)
        sums = jnp.zeros((8, ROWS), jnp.float32)
        for chunk in range(chunks):
            cols = slice(chunk * LANES, (chunk + 1) * LANES)
            weight = jnp.where(chunk * LANES + lane_ix < count_b, jnp.exp(scores[chunk, rows, :] - top), 0.0)
            sums = sums + split_dot(other_rows[:, cols], weight, ((1,), (1,)))
        row_valid = block * ROWS + lax.broadcasted_iota(jnp.int32, (2, ROWS), 1) < count_a
        match_o[0, :, rows] = jnp.where(row_valid, sums[2:4] / sums[1:2], 0.0)

    def write(chunk, result):
        cols = slice(chunk * LANES, (chunk + 1) * LANES)
        lse_o[:, cols] = result[0:1]
        xy_o[0, :, cols] = result[2:4]

    for i in range(round_chunks):
        @pl.loop(1, n)
        def _(step):
            k = peer(step)
            copy_direct(i, k, k).wait_recv()

        write(early + i, merge(me, direct_in[i]))

    home_part = me // chunks
    for chunk in range(early):
        k = chunk * parts + home_part

        @pl.when(k != me)
        def _():
            copy_merged(chunk, k, chunk).wait_recv()

        write(chunk, merged_in[chunk])

    @pl.loop(1, n)
    def _(step):
        k = peer(step)
        copy_want(k, me).wait_send()
        for r in range(rounds):
            copy_one(r, k, me).wait_send()
            copy_two(r, k, me).wait_send()
        for i in range(round_chunks):
            copy_direct(i, k, me).wait_send()

        @pl.when(k // parts < early)
        def _():
            copy_stats(k, me).wait_send()

    @pl.when(my_chunk < early)
    def _():
        @pl.loop(0, chunks)
        def _(q):
            slot = my_part * chunks + q

            @pl.when(slot != me)
            def _():
                copy_merged(q, slot, my_chunk).wait_send()

    @pl.loop(0, chunks)
    def _(c):
        @pl.when(c * parts != me)
        def _():
            copy_attr_one(c, me).wait_send()

    @pl.when(my_part == 0)
    def _():
        @pl.loop(1, n)
        def _(step):
            copy_attr_two(peer(step), my_chunk).wait_send()


def put_out(match, lse, xy, match_o, lse_o, xy_o, sem):
    copies = [
        pltpu.make_async_copy(match, match_o, sem.at[0]),
        pltpu.make_async_copy(lse, lse_o, sem.at[1]),
        pltpu.make_async_copy(xy, xy_o, sem.at[2]),
    ]
    for copy in copies:
        copy.start()
    for copy in copies:
        copy.wait()


SPLIT = 6
MERGED_SUBS = 1


def plan(keypoints):
    eighth = keypoints // 8
    spans = ((0, SPLIT * eighth), (SPLIT * eighth, (8 - SPLIT) * eighth))
    subs = ((0, 4 * eighth), (4 * eighth, 2 * eighth), (6 * eighth, 2 * eighth))
    return spans, subs


def tile_kernel(
    n, desc, attr, counts, owner, pairs, match_o, lse_o, xy_o,
    own, own_t, own_attr, row_scale, own_rows, other_rows, other_scale, want_out, want_all, want_s,
    counts_s, owner_s, pairs_s, attr_all, attr_stage, attr_other,
    scores, stats_out, stats_in, merged_out, merged_in,
    local_sem, want_ss, want_rs, attr_ss1, attr_rs1, attr_ss2, attr_rs2,
    ss1, rs1, ss2, rs2, ss3, rs3, ss4, rs4, ss5, rs5, *buffers,
):
    depth, keypoints = desc.shape[1:]
    spans, subs = plan(keypoints)
    pieces = buffers[: len(spans)]
    stage = buffers[len(spans) : len(spans) + len(subs)]
    partner = buffers[len(spans) + len(subs) : len(spans) + 2 * len(subs)]
    late = MERGED_SUBS
    direct_out = buffers[len(spans) + 2 * len(subs) : len(spans) + 3 * len(subs) - late]
    direct_in = buffers[len(spans) + 3 * len(subs) - late :]
    width = depth // n
    chunks = keypoints // LANES
    parts = n // chunks
    blocks = keypoints // ROWS
    early = sum(w for _, w in subs[:MERGED_SUBS]) // LANES
    team = n // 4
    me = lax.axis_index("img")
    my_chunk = lax.rem(me, chunks)
    my_part = me // chunks

    seat = lax.rem(me, team)
    my_row = me // team
    upper = my_row // 2
    lower = 1 - upper
    half = n // 2
    leads = half - team, half
    lead = lower * leads[0] + upper * leads[1]

    def each_in(rows, first, gap, act):
        @pl.loop(0, rows * team)
        def _(step):
            i = step // team
            row = lower * (rows - 1 - i) + upper * i
            k = (first + gap * row) * team + lax.rem(seat + step, team)

            @pl.when(k != me)
            def _():
                act(k)

    def each_peer(act):
        each_in(4, 0, 1, act)

    def each_of(first, last, act):
        @pl.loop(first, last)
        def _(k):
            @pl.when(k != me)
            def _():
                act(k)

    def each_inner(act):
        each_in(2, 1, 1, act)

    def each_outer(act):
        each_in(2, 0, 3, act)

    def remote(src, dst, send, recv, to):
        return pltpu.make_async_remote_copy(
            src_ref=src, dst_ref=dst, send_sem=send, recv_sem=recv, device_id={"img": to}, device_id_type=MESH
        )

    def drain(like, sem):
        pltpu.make_async_copy(like, like, sem).wait()

    def others(buffer):
        return buffer.at[pl.ds(0, n - 1)]

    def piece_of(r, k):
        first, w = spans[r]
        return desc.at[0, pl.ds(pl.multiple_of(k * width, width), width), pl.ds(first, w)]

    def copy_want(k):
        return remote(want_out, want_all.at[me], want_ss, want_rs, k)

    def copy_attr_one(k):
        return remote(attr.at[0], attr_all.at[me], attr_ss1, attr_rs1, k)

    def copy_attr_two(j, k):
        return remote(attr_stage.at[j], attr_other, attr_ss2.at[j], attr_rs2, k)

    def copy_one(r, k):
        return remote(piece_of(r, k), pieces[r].at[me], ss1.at[r], rs1.at[r], k)

    def copy_two(u, k):
        return remote(stage[u].at[k], partner[u].at[me], ss2.at[u], rs2.at[u], k)

    def copy_stats(c, k):
        return remote(stats_out.at[c], stats_in.at[me], ss3.at[k], rs3, k)

    def copy_merged(q, k, source_chunk):
        return remote(merged_out.at[q], merged_in.at[source_chunk], ss4.at[q], rs4.at[source_chunk], k)

    def copy_direct(i, k):
        return remote(direct_out[i], direct_in[i].at[me], ss5.at[i], rs5.at[i], k)

    barrier = pltpu.get_barrier_semaphore()

    inner = jnp.logical_or(my_row == 1, my_row == 2)

    def tell(k):
        pl.semaphore_signal(barrier, inc=1, device_id={"img": k}, device_id_type=MESH)

    @pl.when(inner)
    def _():
        each_inner(tell)

    local_copies = [
        pltpu.make_async_copy(pairs, pairs_s, local_sem.at[0]),
        pltpu.make_async_copy(owner, owner_s, local_sem.at[1]),
        pltpu.make_async_copy(counts, counts_s, local_sem.at[2]),
        pltpu.make_async_copy(attr, own_attr, local_sem.at[3]),
        pltpu.make_async_copy(desc.at[0], own, local_sem.at[4]),
        pltpu.make_async_copy(attr.at[0], attr_all.at[me], local_sem.at[6]),
        *[pltpu.make_async_copy(piece_of(r, me), pieces[r].at[me], local_sem.at[7 + r]) for r in range(len(spans))],
    ]
    for copy in local_copies:
        copy.start()

    for copy in local_copies[:3]:
        copy.wait()
    want = owner_s[pairs_s[0, 1]]
    count_a = counts_s[pairs_s[0, 0]]
    count_b = counts_s[pairs_s[0, 1]]
    want_row = jnp.full((1, LANES), want, jnp.int32)
    want_out[...] = want_row
    want_all[me] = want_row

    def send_attr():
        for k in leads:
            @pl.when(me != k)
            def _():
                copy_attr_one(k).start()

    @pl.when(inner)
    def _():
        pl.semaphore_wait(barrier, 2 * team - 1)
        each_outer(tell)
        each_inner(lambda k: copy_want(k).start())
        each_inner(lambda k: copy_one(0, k).start())
        pl.semaphore_wait(barrier, 2 * team)
        each_outer(tell)
        each_outer(lambda k: copy_want(k).start())
        each_outer(lambda k: copy_one(0, k).start())

    @pl.when(jnp.logical_not(inner))
    def _():
        pl.semaphore_wait(barrier, 2 * team)
        each_inner(tell)
        each_inner(lambda k: copy_want(k).start())
        each_inner(lambda k: copy_one(0, k).start())
        pl.semaphore_wait(barrier, 2 * team)
        each_outer(lambda k: copy_want(k).start())
        each_outer(lambda k: copy_one(0, k).start())


    send_attr()
    each_peer(lambda k: copy_one(1, k).start())

    for copy in local_copies[3:]:
        copy.wait()
    rows8 = with_ones(own_attr[0].astype(jnp.float32))
    own_rows[...] = rows8.astype(jnp.bfloat16)
    row_scale[...] = jnp.broadcast_to(jnp.transpose(rows8)[:, 0:1] * (1.0 / math.sqrt(depth)), (keypoints, LANES))
    for block in range(blocks):
        rows = slice(block * ROWS, (block + 1) * ROWS)
        own_t[rows, :] = jnp.transpose(own[:, rows])

    drain(others(want_all), want_rs)
    to_scalars = pltpu.make_async_copy(want_all, want_s, local_sem.at[5])
    to_scalars.start()
    to_scalars.wait()

    def pick(u, index, put):
        start, w = subs[u]
        for r, (first, span) in enumerate(spans):
            low, high = max(start, first), min(start + w, first + span)
            if low < high:
                put(slice(low - start, high - start), pieces[r][index, :, low - first : high - first])

    def forward(u):
        def send(k):
            def put(cols, value):
                stage[u][k, :, cols] = value

            pick(u, want_s[k, 0, 0], put)
            copy_two(u, k).start()

        each_peer(send)

        def keep(cols, value):
            partner[u][me, :, cols] = value

        pick(u, want, keep)

    drain(others(pieces[0]), rs1.at[0])
    forward(0)

    @pl.when(me == lead)
    def _():
        drain(others(attr_all), attr_rs1)

        @pl.loop(0, half)
        def _(j):
            k = upper * half + j

            @pl.when(k != me)
            def _():
                attr_stage[j] = attr_all[want_s[k, 0, 0]]
                copy_attr_two(j, k).start()

        attr_other[...] = attr_all[want]


    drain(others(pieces[1]), rs1.at[1])

    forward(1)
    forward(2)

    @pl.when(me != lead)
    def _():
        drain(attr_other, attr_rs2)

    other8 = with_ones(attr_other[...].astype(jnp.float32))
    other_rows[...] = other8.astype(jnp.bfloat16)
    for chunk in range(chunks):
        other_scale[chunk] = other8[0:1, chunk * LANES : (chunk + 1) * LANES]

    lane_ix = lax.broadcasted_iota(jnp.int32, (1, LANES), 1)
    first_row = lax.broadcasted_iota(jnp.int32, (4, LANES), 0) == 0

    def score(u, first_chunk):
        w = subs[u][1]
        narrow = w == 2 * LANES
        tall = ROWS if w == LANES else ROWS // 2
        spot = range(keypoints // tall)
        row_ix = lax.broadcasted_iota(jnp.int32, (tall, LANES), 0)
        lanes = [slice(i * LANES, (i + 1) * LANES) for i in range(w // LANES)]
        block_b = partner[u][...].reshape(depth, w)
        block_tops, block_sums = [], []
        for block in spot:
            rows = slice(block * tall, (block + 1) * tall)
            raw = jnp.dot(own_t[rows, :], block_b, preferred_element_type=jnp.float32)
            valid = block * tall + row_ix < count_a
            tops, weight = [], []
            for i, cols in enumerate(lanes):
                scaled = raw[:, cols] * row_scale[rows, :] * other_scale[first_chunk + i]
                masked = jnp.where(valid, scaled, far_low)
                scores[first_chunk + i, rows, :] = masked
                if narrow:
                    tops.append(jnp.max(masked, axis=0, keepdims=True))
                    weight.append(jnp.exp(masked - tops[i]))
                else:
                    tops.append(jnp.max(masked.reshape(tall // 8, 8, LANES), axis=0))
            block_tops.append(tops)
            if narrow:
                block_sums.append(split_dot(own_rows[:, rows], jnp.concatenate(weight, axis=1), ((1,), (0,))))
        tops = [functools.reduce(jnp.maximum, [found[i] for found in block_tops]) for i in range(len(lanes))]
        if narrow:
            sums = [
                sum(block_sums[block][:, cols] * jnp.exp(block_tops[block][i] - tops[i]) for block in spot)
                for i, cols in enumerate(lanes)
            ]
            return [jnp.where(first_row, top, total[0:4]) for top, total in zip(tops, sums)]
        tops = [jnp.max(top, axis=0, keepdims=True) for top in tops]
        sums = [jnp.zeros((8, LANES), jnp.float32) for _ in lanes]
        for block in spot:
            rows = slice(block * tall, (block + 1) * tall)
            weight = [jnp.exp(scores[first_chunk + i, rows, :] - top) for i, top in enumerate(tops)]
            part = split_dot(own_rows[:, rows], jnp.concatenate(weight, axis=1), ((1,), (0,)))
            sums = [total + part[:, cols] for total, cols in zip(sums, lanes)]
        return [jnp.where(first_row, top, total[0:4]) for top, total in zip(tops, sums)]

    def merge(slot, partial):
        hit = want_all[...] == slot
        tops = partial[:, 0:1, :]
        peak = jnp.maximum(jnp.max(jnp.where(hit, tops, far_low), axis=0), 0.0)
        fade = jnp.where(hit, jnp.exp(tops - peak[None]), 0.0)
        total = jnp.sum(fade * partial, axis=0)
        partition = jnp.exp(-peak) + total[1:2]
        return jnp.where(first_row, peak + jnp.log(partition), total / partition)

    for u in range(len(subs)):
        base = subs[u][0] // LANES
        drain(others(partner[u]), rs2.at[u])
        for i, stats in enumerate(score(u, base)):
            c = base + i
            if u < late:
                stats_out[c] = stats
                for part in range(parts):
                    k = part * chunks + c

                    @pl.when(k != me)
                    def _():
                        copy_stats(c, k).start()

                    @pl.when(k == me)
                    def _():
                        stats_in[me] = stats
            else:
                cols = slice(i * LANES, (i + 1) * LANES)
                direct_out[u - late][:, cols] = stats
                direct_in[u - late][me, :, cols] = stats
        if u >= late:
            each_of(0, team, lambda k: copy_direct(u - late, k).start())

    def send_rest(k):
        for i in range(len(subs) - late):
            copy_direct(i, k).start()

    each_of(team, n, send_rest)


    def row_block(block):
        rows = slice(block * ROWS, (block + 1) * ROWS)
        top = jnp.full((ROWS, LANES), far_low, jnp.float32)
        for chunk in range(chunks):
            top = jnp.maximum(top, jnp.where(chunk * LANES + lane_ix < count_b, scores[chunk, rows, :], far_low))
        top = jnp.max(top, axis=1, keepdims=True)
        sums = jnp.zeros((8, ROWS), jnp.float32)
        for chunk in range(chunks):
            cols = slice(chunk * LANES, (chunk + 1) * LANES)
            weight = jnp.where(chunk * LANES + lane_ix < count_b, jnp.exp(scores[chunk, rows, :] - top), 0.0)
            sums = sums + split_dot(other_rows[:, cols], weight, ((1,), (1,)))
        row_valid = block * ROWS + lax.broadcasted_iota(jnp.int32, (2, ROWS), 1) < count_a
        match_o[0, :, rows] = jnp.where(row_valid, sums[2:4] / sums[1:2], 0.0)

    row_block(0)
    row_block(1)

    @pl.when(my_chunk < early)
    def _():
        drain(others(stats_in), rs3)

        @pl.loop(0, chunks)
        def _(q):
            slot = my_part * chunks + q
            merged = merge(slot, stats_in[...])
            merged_out[q] = merged

            @pl.when(slot != me)
            def _():
                copy_merged(q, slot, my_chunk).start()

            @pl.when(slot == me)
            def _():
                merged_in[my_chunk] = merged

    for block in range(2, blocks):
        row_block(block)

    def write(chunk, result):
        cols = slice(chunk * LANES, (chunk + 1) * LANES)
        lse_o[:, cols] = result[0:1]
        xy_o[0, :, cols] = result[2:4]

    drain(others(want_all), want_ss)
    for r in range(len(spans)):
        drain(others(pieces[r]), ss1.at[r])
    for u in range(len(subs)):
        drain(others(partner[u]), ss2.at[u])

    for k in leads:
        @pl.when(me != k)
        def _():
            drain(attr_other, attr_ss1)

    @pl.when(me == lead)
    def _():
        @pl.loop(0, half)
        def _(j):
            k = upper * half + j

            @pl.when(k != me)
            def _():
                copy_attr_two(j, k).wait_send()

    for part in range(parts):
        @pl.loop(0, early)
        def _(c):
            k = part * chunks + c

            @pl.when(k != me)
            def _():
                copy_stats(c, k).wait_send()

    for i in range(len(subs) - late):
        drain(others(direct_in[i]), ss5.at[i])

    @pl.when(my_chunk < early)
    def _():
        @pl.loop(0, chunks)
        def _(q):
            slot = my_part * chunks + q

            @pl.when(slot != me)
            def _():
                copy_merged(q, slot, my_chunk).wait_send()

    for chunk in range(early):
        k = my_part * chunks + chunk

        @pl.when(k != me)
        def _():
            copy_merged(0, k, chunk).wait_recv()

        write(chunk, merged_in[chunk])

    for u in range(late, len(subs)):
        i = u - late
        drain(others(direct_in[i]), rs5.at[i])
        for j in range(subs[u][1] // LANES):
            part = direct_in[i][:, :, j * LANES : (j + 1) * LANES]
            write(subs[u][0] // LANES + j, merge(me, part))


def one_tile(n, descriptors, attributes, counts, owner_slot, pair_list):
    _, depth, keypoints = descriptors.shape
    chunks = keypoints // LANES
    spans, subs = plan(keypoints)
    width = depth // n
    late = [w for _, w in subs[MERGED_SUBS:]]
    vmem = pl.BlockSpec(memory_space=pltpu.VMEM)
    hbm = pl.BlockSpec(memory_space=pltpu.HBM)
    f32, bf16, i32 = jnp.float32, jnp.bfloat16, jnp.int32
    sems = pltpu.SemaphoreType.DMA
    shapes = (1, 2, keypoints), (1, keypoints), (1, 2, keypoints)
    out_shape = tuple(jax.ShapeDtypeStruct(shape, f32) for shape in shapes)
    results = pl.pallas_call(
        functools.partial(tile_kernel, n),
        out_shape=tuple(pltpu.VMEM(shape, f32) for shape in shapes),
        in_specs=[hbm] * 5,
        out_specs=(vmem, vmem, vmem),
        scratch_shapes=[
            pltpu.VMEM((depth, keypoints), bf16),
            pltpu.VMEM((keypoints, depth), bf16),
            pltpu.VMEM((1, 3, keypoints), bf16),
            pltpu.VMEM((keypoints, LANES), f32),
            pltpu.VMEM((8, keypoints), bf16),
            pltpu.VMEM((8, keypoints), bf16),
            pltpu.VMEM((chunks, 1, LANES), f32),
            pltpu.VMEM((1, LANES), i32),
            pltpu.VMEM((n, 1, LANES), i32),
            pltpu.SMEM((n, 1, LANES), i32),
            pltpu.SMEM(counts.shape, i32),
            pltpu.SMEM(owner_slot.shape, i32),
            pltpu.SMEM(pair_list.shape, i32),
            pltpu.VMEM((n, 3, keypoints), bf16),
            pltpu.VMEM((n // 2, 3, keypoints), bf16),
            pltpu.VMEM((3, keypoints), bf16),
            pltpu.VMEM((chunks, keypoints, LANES), f32),
            pltpu.VMEM((chunks, 4, LANES), f32),
            pltpu.VMEM((n, 4, LANES), f32),
            pltpu.VMEM((chunks, 4, LANES), f32),
            pltpu.VMEM((chunks, 4, LANES), f32),
            sems((7 + len(spans),)),
            sems,
            sems,
            sems,
            sems,
            sems((n // 2,)),
            sems,
            *[sems((len(spans),))] * 2,
            *[sems((len(subs),))] * 2,
            sems((n,)),
            sems,
            *[sems((chunks,))] * 2,
            *[sems((len(late),))] * 2,
            *[pltpu.VMEM((n, width, w), bf16) for _, w in spans],
            *[pltpu.VMEM((n, width, w), bf16) for _, w in subs] * 2,
            *[pltpu.VMEM((4, w), f32) for w in late],
            *[pltpu.VMEM((n, 4, w), f32) for w in late],
        ],
        compiler_params=pltpu.CompilerParams(collective_id=0, has_side_effects=True),
    )(descriptors, attributes, counts, owner_slot, pair_list)
    return pl.pallas_call(
        put_out,
        out_shape=out_shape,
        in_specs=[vmem] * 3,
        out_specs=(hbm, hbm, hbm),
        scratch_shapes=[sems((3,))],
    )(*[pltpu.with_memory_space_constraint(result, pltpu.VMEM) for result in results])


def solution(mesh):
    n = mesh.shape["img"]

    def shards(descriptors, attributes, counts, owner_slot, pair_list):
        _, depth, keypoints = descriptors.shape
        if n * TILE == depth and n % 4 == 0:
            return one_tile(n, descriptors, attributes, counts, owner_slot, pair_list)
        chunks = keypoints // LANES
        parts = n // chunks
        rounds = min(ROUNDS, depth * chunks // (n * MIN_WIDTH))
        width = depth * chunks // (n * rounds)
        vmem = pl.BlockSpec(memory_space=pltpu.VMEM)
        hbm = pl.BlockSpec(memory_space=pltpu.HBM)
        f32, bf16, i32 = jnp.float32, jnp.bfloat16, jnp.int32
        sems = pltpu.SemaphoreType.DMA
        out_shape = (
            jax.ShapeDtypeStruct((1, 2, keypoints), f32),
            jax.ShapeDtypeStruct((1, keypoints), f32),
            jax.ShapeDtypeStruct((1, 2, keypoints), f32),
        )
        results = pl.pallas_call(
            functools.partial(kernel, n, rounds),
            out_shape=out_shape,
            in_specs=[hbm] * 5,
            out_specs=(vmem, vmem, vmem),
            scratch_shapes=[
                pltpu.VMEM((depth, keypoints), bf16),
                pltpu.VMEM((keypoints, depth), bf16),
                pltpu.VMEM((1, 3, keypoints), bf16),
                pltpu.VMEM((keypoints, LANES), f32),
                pltpu.VMEM((8, keypoints), bf16),
                pltpu.VMEM((8, keypoints), bf16),
                pltpu.VMEM((chunks, 1, LANES), f32),
                pltpu.VMEM((1, LANES), i32),
                pltpu.VMEM((n, 1, LANES), i32),
                pltpu.SMEM((n, 1, LANES), i32),
                pltpu.SMEM(counts.shape, i32),
                pltpu.SMEM(owner_slot.shape, i32),
                pltpu.SMEM(pair_list.shape, i32),
                pltpu.VMEM((n, 3, LANES), bf16),
                pltpu.VMEM((n, 3, LANES), bf16),
                pltpu.VMEM((chunks, 3, LANES), bf16),
                *[pltpu.VMEM((rounds, n, width, LANES), bf16)] * 2,
                pltpu.VMEM((chunks, keypoints, LANES), f32),
                pltpu.VMEM((keypoints, LANES), f32),
                pltpu.VMEM((chunks, 4, LANES), f32),
                pltpu.VMEM((n, 4, LANES), f32),
                pltpu.VMEM((chunks, 4, LANES), f32),
                pltpu.VMEM((chunks, 4, LANES), f32),
                pltpu.VMEM((chunks // rounds, n, 4, LANES), f32),
                sems((7 + rounds,)),
                *[sems((n,))] * 2,
                sems((chunks,)),
                *[sems((n,))] * 2,
                sems((chunks,)),
                *[sems((rounds, n))] * 4,
                *[sems((n,))] * 2,
                *[sems((chunks,))] * 2,
                *[sems((chunks // rounds, n))] * 2,
                *[pltpu.VMEM((n, width, LANES), bf16)] * rounds,
            ],
            compiler_params=pltpu.CompilerParams(
                collective_id=0, has_side_effects=True
            ),
        )(descriptors, attributes, counts, owner_slot, pair_list)
        return pl.pallas_call(
            put_out,
            out_shape=out_shape,
            in_specs=[vmem] * 3,
            out_specs=(hbm, hbm, hbm),
            scratch_shapes=[sems((3,))],
        )(*results)

    placed = (
        P(("groups", "img"), None, None),
        P(("groups", "img"), None, None),
        P("groups"),
        P("groups"),
        P(("groups", "img"), None),
    )
    return jax.shard_map(
        shards,
        mesh=mesh,
        in_specs=placed,
        out_specs=(
            P(("groups", "img"), None, None),
            P(("groups", "img"), None),
            P(("groups", "img"), None, None),
        ),
        check_vma=False,
    )
```
